32 devices in a mesh: tm: 8 (over z, y), row: 4 (over x, core).
Axes of the slice: x: 2, y: 2, z: 4, core: 2. Of those that a mesh axis runs over, the one named last changes fastest.
Arguments:
- inv_diag: float32 [32, 512, 512], P('tm', 'row'), may hold values from -0.04 to 1.1, as said below
- coupling: float32 [32, 512, 512], P('tm', 'row'), may hold values from -0.99 to 0.04, as said below
- noise: float32 [32, 512, 1024], P('tm', None, 'row'), may hold values from -2 to 2
- obs_day: int32 [131072], P(('tm', 'row')), may hold values from 0 to 31
- obs_node: int32 [131072], P(('tm', 'row')), may hold values from 0 to 511
- obs_value: float32 [131072], P(('tm', 'row')), may hold values from -0.6 to 0.6
Outputs:
- samples: float32 [32, 512, 1024], P('tm', None, 'row')
The draws below stay inside these ranges and needn't reach their ends.
Inputs may be any that keep to these rules, and one draw needn't show every extreme that they name: `inv_diag`: one 512 x 512 block a day. `coupling`: one 512 x 512 block a day.
All inputs are finite; a program needn't handle non-finite values.
Results may differ from the reference program's by a relative error of at most 0.0003.
Values sent between devices are 32-bit elements; how exact they have to be, the bound alone decides.
No kernel may reach another device: no remote copies, remote signals or barrier semaphores. Data moves between devices by JAX's collectives and lax.ppermute only.
A program may use at most 256 MiB of HBM per device.

```python
import math
import jax
import jax.numpy as jnp
from jax import lax

NODES = 512
SAMPLES = 1024
WINDOW_DAYS = 32
OBS = 131072


def draw_inv_diag(key, part):
    entry_key = jax.random.fold_in(key, 101)
    diag_key = jax.random.fold_in(key, 102)
    entry_scale = 0.2 / math.sqrt(NODES)
    entries = jnp.clip(jax.random.normal(entry_key, (WINDOW_DAYS, NODES, NODES), jnp.float32) * entry_scale, -0.04, 0.04)
    main_diagonal = jax.random.uniform(diag_key, (WINDOW_DAYS, NODES), jnp.float32, 0.9, 1.1)
    identity = jnp.eye(NODES, dtype=jnp.float32)
    return entries * (1.0 - identity) + identity * main_diagonal[:, None, :]


def draw_coupling(key, part):
    rate_key = jax.random.fold_in(key, 201)
    spike_random_key = jax.random.fold_in(key, 202)
    entry_key = jax.random.fold_in(key, 203)
    entry_scale = 0.2 / math.sqrt(NODES)
    rate_high = math.log(0.08)
    entries = jnp.clip(jax.random.normal(entry_key, (WINDOW_DAYS, NODES, NODES), jnp.float32) * entry_scale, -0.04, 0.04)
    lower_rate_limit = math.log(0.2 / WINDOW_DAYS)
    event_rates = jnp.exp(jax.random.uniform(rate_key, (NODES,), jnp.float32, lower_rate_limit, rate_high))
    spike_events = jnp.where(jax.random.uniform(spike_random_key, (WINDOW_DAYS,), jnp.float32) < 3.0 / WINDOW_DAYS, 0.6, 1.0)
    damping_factor = 0.99 * jnp.exp(-event_rates)[None, :] * spike_events[:, None]
    identity = jnp.eye(NODES, dtype=jnp.float32)
    return entries * (1.0 - identity) - identity * damping_factor[:, None, :]


def set_ends(values, rng, low, top_value):
    extent = values.shape
    spot = [jax.random.randint(jax.random.fold_in(rng, axis), (), 0, extent[axis]) for axis in range(len(extent))]
    values = values.at[tuple(spot)].set(low)
    longest = extent.index(max(extent))
    spot[longest] = (spot[longest] + 1) % extent[longest]
    return values.at[tuple(spot)].set(top_value)


def block_levels(key, shape, shards, smallest, high):
    factor_of = 1.0
    for position, blocks in shards:
        heights = jax.random.uniform(jax.random.fold_in(jax.random.fold_in(key, 6), position), (blocks,), jnp.float32, smallest / len(shards), high / len(shards))
        factor_of = factor_of * jnp.repeat(jnp.exp(heights), shape[position] // blocks).reshape((-1,) + (1,) * (len(shape) - 1 - position))
    return factor_of


def normal_values(stream_key, dims, spread, limit, shards=(), kind=jnp.bfloat16):
    factor_of = block_levels(stream_key, dims, shards, -0.22, 0.18) if shards else 1.0
    drawn = jax.random.normal(stream_key, dims, jnp.float32) * spread * factor_of
    return jnp.minimum(jnp.maximum(drawn, -limit), limit).astype(kind)


def setup_inputs(seed: int = 0) -> dict:
    key_of = jax.random.split(jax.random.key(seed), 7)
    inv_diag = draw_inv_diag(jax.random.fold_in(key_of[6], 71), 0)
    coupling = draw_coupling(jax.random.fold_in(key_of[6], 71), 0)
    noise = normal_values(key_of[2], (WINDOW_DAYS, NODES, SAMPLES), 0.3, 2.0, ((0, 8), (2, 4)), jnp.float32)
    obs_day = set_ends(jax.random.randint(key_of[3], (OBS,), 0, WINDOW_DAYS), jax.random.fold_in(key_of[3], 1), 0, WINDOW_DAYS - 1).astype(jnp.int32)
    obs_node = set_ends(jax.random.randint(key_of[4], (OBS,), 0, NODES), jax.random.fold_in(key_of[4], 1), 0, NODES - 1).astype(jnp.int32)
    obs_value = normal_values(key_of[5], (OBS,), 0.1, 0.6, ((0, 32),), jnp.float32)
    return dict(inv_diag=inv_diag, coupling=coupling, noise=noise, obs_day=obs_day, obs_node=obs_node, obs_value=obs_value)


highest = lax.Precision.HIGHEST


def forward_day(applied, inputs):
    inverse_block, link_block, source = inputs
    current = jnp.dot(inverse_block, source - applied, precision=highest, preferred_element_type=jnp.float32)
    return jnp.dot(link_block, current, precision=highest, preferred_element_type=jnp.float32), current


def backward_day(following, inputs):
    inverse_block, link_block, mean_part, noise_block = inputs
    inner = mean_part[:, None] + noise_block - jnp.dot(link_block.T, following, precision=highest, preferred_element_type=jnp.float32)
    current = jnp.dot(inverse_block.T, inner, precision=highest, preferred_element_type=jnp.float32)
    return current, current


def reference(inv_diag, coupling, noise, obs_day, obs_node, obs_value):
    right_side = jnp.zeros((WINDOW_DAYS, NODES), jnp.float32).at[obs_day, obs_node].add(obs_value)
    initial_applied = jnp.zeros((NODES,), jnp.float32)
    _, mean_path = lax.scan(forward_day, initial_applied, (inv_diag, coupling, right_side))
    initial_state = jnp.zeros((NODES, SAMPLES), jnp.float32)
    _, samples = lax.scan(backward_day, initial_state, (inv_diag, coupling, mean_path, noise), reverse=True)
    return samples
```

```python
import functools

import jax
import jax.numpy as jnp
from jax import lax
from jax.experimental import pallas as pl
from jax.experimental.pallas import tpu as pltpu
from jax.sharding import PartitionSpec as P

F32 = jnp.float32
BF16 = jnp.bfloat16
CORES = 2
PAIR = 2
LINES = 8


def split(value):
    high = value.astype(BF16)
    return high, (value - high.astype(F32)).astype(BF16)


def dot_parts(left, right, dims):
    product = functools.partial(
        lax.dot_general, dimension_numbers=(dims, ((), ())), preferred_element_type=F32
    )
    return product(left[0], right[0]) + (product(left[0], right[1]) + product(left[1], right[0]))


NN = ((1,), (0,))
TN = ((0,), (0,))
NT = ((1,), (1,))


def call(body, out_shape, name, scratch=(), scalars=1, inputs=0, specs=None):
    return pl.pallas_call(
        body,
        out_shape=out_shape,
        grid=(1,),
        in_specs=[pl.BlockSpec(memory_space=pltpu.SMEM)] * scalars
        + (specs or [pl.BlockSpec(memory_space=pltpu.VMEM)] * inputs),
        out_specs=jax.tree.map(lambda _: pl.BlockSpec(memory_space=pltpu.VMEM), out_shape),
        scratch_shapes=list(scratch),
        compiler_params=pltpu.CompilerParams(vmem_limit_bytes=56 * 1024 * 1024),
        name=name,
    )


def shape(*dims, dtype=F32):
    return jax.ShapeDtypeStruct(dims, dtype)


def bin_observations(obs_day, obs_node, obs_value, days, nodes):
    chunk = min(512, obs_day.shape[0])
    chunks = obs_day.shape[0] // chunk

    def body(day_ref, node_ref, value_ref, out_ref):
        total = jnp.zeros((3 * days, nodes), F32)
        for index in range(chunks):
            row = pl.ds(index, 1)
            value = value_ref[row, :]
            high = value.astype(BF16).astype(F32)
            middle = (value - high).astype(BF16).astype(F32)
            low = value - high - middle
            is_day = lax.broadcasted_iota(jnp.int32, (days, chunk), 0) == day_ref[row, :]
            marked = jnp.concatenate(
                [jnp.where(is_day, part, 0.0).astype(BF16) for part in (high, middle, low)], axis=0
            )
            is_node = lax.broadcasted_iota(jnp.int32, (nodes, chunk), 0) == node_ref[row, :]
            total += lax.dot_general(
                marked, is_node.astype(F32).astype(BF16), (NT, ((), ())), preferred_element_type=F32
            )
        out_ref[...] = total[:days] + (total[days : 2 * days] + total[2 * days :])

    return call(body, shape(days, nodes), "bin_observations", scalars=0, inputs=3)(
        *(value.reshape(chunks, chunk) for value in (obs_day, obs_node, obs_value))
    )


def day_step(day, position, row_count, own, pieces, noise, right_side, state):
    nodes, columns = noise.shape[1:]
    share = nodes // row_count
    square = shape(nodes, nodes)
    first = state is None

    def body(position_ref, *refs):
        refs = list(refs)
        inverse_rows = [refs.pop(0) for _ in range(row_count)]
        link_rows = [refs.pop(0) for _ in range(row_count)]
        noise_ref, source_ref = refs.pop(0), refs.pop(0)
        if not first:
            path_ref, gram_ref, sum_ref, applied_ref, back_ref = [refs.pop(0) for _ in range(5)]
        (path_out, gram_out, sum_out, applied_out, back_out) = [refs.pop(0) for _ in range(5)]
        (moved_out, own_out, map_out, local_out, current_out) = [refs.pop(0) for _ in range(5)]
        full_inverse, full_link = refs
        me = position_ref[0]
        for offset in range(row_count):
            at = pl.ds(pl.multiple_of((me ^ offset) * share, share), share)
            full_inverse[at, :] = inverse_rows[offset][0]
            full_link[at, :] = link_rows[offset][0]
        inverse, link = split(full_inverse[...]), split(full_link[...])
        noise_parts = split(noise_ref[0])
        if first:
            moved, moved_parts = full_inverse[...], inverse
            wanted = source_ref[0]
        else:
            moved = dot_parts(inverse, split(path_ref[...]), NN)
            moved_parts = split(moved)
            wanted = source_ref[0] - applied_ref[...]
        current = dot_parts(split(wanted), inverse, NT)
        current_parts = split(current)
        applied_out[...] = dot_parts(current_parts, link, NT)
        back = dot_parts(current_parts, moved_parts, NN)
        gram = dot_parts(moved_parts, moved_parts, TN)
        total = dot_parts(moved_parts, noise_parts, TN)
        if not first:
            back, gram, total = back + back_ref[...], gram + gram_ref[...], total + sum_ref[...]
        path_out[...] = -dot_parts(link, moved_parts, NN)
        gram_out[...] = gram
        sum_out[...] = total
        back_out[...] = back
        moved_out[...] = moved
        own_out[0], own_out[1] = inverse
        step = split(-dot_parts(link, inverse, NN))
        map_out[0], map_out[1] = step
        local_out[...] = dot_parts(inverse, noise_parts, TN)
        current_out[...] = current

    one_day = pl.BlockSpec((1, share, nodes), lambda _: (day, 0, 0))
    specs = []
    operands = []
    for which in range(2):
        for offset in range(row_count):
            if offset < CORES:
                operands.append(own[which][offset])
                specs.append(one_day)
            else:
                operands.append(pieces[which][offset])
                specs.append(pl.BlockSpec(memory_space=pltpu.VMEM))
    operands += [noise, right_side]
    specs += [
        pl.BlockSpec((1, nodes, columns), lambda _: (day, 0, 0)),
        pl.BlockSpec((1, LINES, nodes), lambda _: (day, 0, 0)),
    ]
    if not first:
        operands += list(state)
        specs += [pl.BlockSpec(memory_space=pltpu.VMEM)] * 5
    line = shape(LINES, nodes)
    halves = shape(2, nodes, nodes, dtype=BF16)
    outs = (
        square, square, shape(nodes, columns), line, line,
        square, halves, halves, shape(nodes, columns), line,
    )
    results = call(
        body,
        outs,
        f"day_{day}",
        scratch=[pltpu.VMEM((nodes, nodes), F32)] * 2,
        specs=specs,
    )(position, *operands)
    return results[:5], results[5:]


def local(inv_diag, coupling, noise, obs_day, obs_node, obs_value):
    part_count = lax.axis_size("tm")
    row_count = lax.axis_size("row")
    my_part = lax.axis_index("tm")
    my_row = lax.axis_index("row")
    day_count, share, nodes = inv_diag.shape
    columns = noise.shape[2]
    half = columns // PAIR
    half_nodes = nodes // CORES
    groups = part_count // PAIR
    chips = row_count // CORES

    def to_row(value, distance):
        return lax.ppermute(value, "row", [(i, i ^ distance) for i in range(row_count)])

    def to_pair(value):
        return lax.ppermute(value, "tm", [(i, i ^ 1) for i in range(part_count)])

    def to_group(value, source, target):
        return lax.ppermute(
            value, "tm", [(PAIR * source + i, PAIR * target + i) for i in range(PAIR)]
        )

    position = jnp.reshape(my_row, (1,)).astype(jnp.int32)
    side = jnp.reshape(my_part % PAIR, (1,)).astype(jnp.int32)
    core = jnp.reshape(my_row % CORES, (1,)).astype(jnp.int32)

    pieces = []
    for day in range(day_count):
        rows = [None] * CORES
        links = [None] * CORES
        for chip in range(1, chips):
            got_rows = to_row(inv_diag[day : day + 1], CORES * chip)
            got_links = to_row(coupling[day : day + 1], CORES * chip)
            rows += [got_rows, to_row(got_rows, 1)]
            links += [got_links, to_row(got_links, 1)]
        pieces.append((rows, links))
    own = [[inv_diag, to_row(inv_diag, 1)], [coupling, to_row(coupling, 1)]]

    dense = bin_observations(obs_day, obs_node, obs_value, part_count * day_count, nodes)
    sent = lax.all_to_all(
        dense.reshape(part_count, day_count, nodes), "tm", split_axis=0, concat_axis=0, tiled=True
    )
    right_side = jnp.sum(sent, axis=0)
    distance = 1
    while distance < row_count:
        right_side = right_side + to_row(right_side, distance)
        distance *= 2
    right_side = jnp.broadcast_to(right_side[:, None, :], (day_count, LINES, nodes))

    state = None
    kept = []
    for day in range(day_count):
        state, saved = day_step(
            day, position, row_count, own, pieces[day], noise, right_side, state
        )
        kept.append(saved)
    path, gram, summed, applied, back = state

    def halves_body(side_ref, core_ref, path_ref, sum_ref, path_half, keep, send):
        path_half[...] = path_ref[
            pl.ds(pl.multiple_of(core_ref[0] * half_nodes, half_nodes), half_nodes), :
        ]
        low, high = sum_ref[:, :half], sum_ref[:, half:]
        first = side_ref[0] == 0
        keep[...] = jnp.where(first, low, high)
        send[...] = jnp.where(first, high, low)

    columns_half = shape(nodes, half)
    path_half, keep, send = call(
        halves_body,
        (shape(half_nodes, nodes), columns_half, columns_half),
        "halves",
        scalars=2,
        inputs=2,
    )(side, core, path, summed)
    other_half = to_pair(path_half)
    other_sum = to_pair(send)
    other_applied = to_pair(applied)
    other_rest = to_row(other_half, 1)

    def pair_body(
        side_ref, core_ref, path_ref, half_ref, rest_ref, sum_ref, other_ref, applied_ref,
        other_applied_ref, low_out, high_out, both_out, sum_out, high_sum_out, flux_out,
        low_flux_out, scratch, lines,
    ):
        me, mate = side_ref[0], 1 - side_ref[0]
        mine = core_ref[0]
        scratch[me] = path_ref[...]
        scratch[mate, pl.ds(pl.multiple_of(mine * half_nodes, half_nodes), half_nodes), :] = (
            half_ref[...]
        )
        scratch[
            mate, pl.ds(pl.multiple_of((1 - mine) * half_nodes, half_nodes), half_nodes), :
        ] = rest_ref[...]
        lines[me] = applied_ref[...]
        lines[mate] = other_applied_ref[...]
        low, high = split(scratch[0]), split(scratch[1])
        low_out[0], low_out[1] = low
        high_out[0], high_out[1] = high
        both_out[0], both_out[1] = split(dot_parts(high, low, NN))
        first = me == 0
        low_sum = jnp.where(first, sum_ref[...], other_ref[...])
        high_sum = jnp.where(first, other_ref[...], sum_ref[...])
        sum_out[...] = dot_parts(low, split(high_sum), TN) + low_sum
        high_sum_out[...] = high_sum
        flux_out[...] = dot_parts(split(lines[0]), high, NT) + lines[1]
        low_flux_out[...] = lines[0]

    line = shape(LINES, nodes)
    map_shape = shape(2, nodes, nodes, dtype=BF16)
    low_map, high_map, both_map, pair_sum, high_sum, pair_flux, low_flux = call(
        pair_body,
        (map_shape, map_shape, map_shape, columns_half, columns_half, line, line),
        "pair_maps",
        scratch=[pltpu.VMEM((PAIR, nodes, nodes), F32), pltpu.VMEM((PAIR, LINES, nodes), F32)],
        scalars=2,
        inputs=7,
    )(side, core, path, other_half, other_rest, keep, other_sum, applied, other_applied)

    def link_body(map_ref, local_ref, got_ref, out_ref):
        out_ref[...] = (
            dot_parts((map_ref[0], map_ref[1]), split(got_ref[...]), TN) + local_ref[...]
        )

    def line_body(dims, map_ref, local_ref, got_ref, out_ref):
        out_ref[...] = (
            dot_parts(split(got_ref[...]), (map_ref[0], map_ref[1]), dims) + local_ref[...]
        )

    advance = call(link_body, columns_half, "noise_link", scalars=0, inputs=3)
    forward = call(
        functools.partial(line_body, NT), line, "forward_link", scalars=0, inputs=3
    )
    backward = call(
        functools.partial(line_body, NN), line, "backward_link", scalars=0, inputs=3
    )

    leaving = jnp.zeros((nodes, half), F32)
    current = pair_sum
    for group in range(groups - 1, 0, -1):
        leaving = leaving + to_group(current, group, group - 1)
        if group > 1:
            current = advance(both_map, pair_sum, leaving)

    entering = jnp.zeros((LINES, nodes), F32)
    flux = pair_flux
    for group in range(groups - 1):
        entering = entering + to_group(flux, group, group + 1)
        if group < groups - 2:
            flux = forward(both_map, pair_flux, entering)

    def mean_body(side_ref, low_ref, flux_ref, entering_ref, gram_ref, back_ref, own_out, back_out):
        given = entering_ref[...]
        after = dot_parts(split(given), (low_ref[0], low_ref[1]), NT) + flux_ref[...]
        given = jnp.where(side_ref[0] == 0, given, after)
        own_out[...] = given
        back_out[...] = back_ref[...] - dot_parts(split(given), split(gram_ref[...]), NN)

    own_entering, own_back = call(mean_body, (line, line), "mean_turn", inputs=5)(
        side, low_map, low_flux, entering, gram, back
    )
    other_back = to_pair(own_back)
    low_back = jnp.where(side[0] == 0, own_back, other_back)
    high_back = jnp.where(side[0] == 0, other_back, own_back)
    pair_back = backward(low_map, low_back, high_back)
    mean_leaving = jnp.zeros((LINES, nodes), F32)
    mean = pair_back
    for group in range(groups - 1, 0, -1):
        mean_leaving = mean_leaving + to_group(mean, group, group - 1)
        if group > 1:
            mean = backward(both_map, pair_back, mean_leaving)

    def divide_body(side_ref, high_ref, sum_ref, leaving_ref, mean_ref, back_ref, keep, send, line_out):
        high = (high_ref[0], high_ref[1])
        between = dot_parts(high, split(leaving_ref[...]), TN) + sum_ref[...]
        first = side_ref[0] == 0
        keep[...] = jnp.where(first, between, leaving_ref[...])
        send[...] = jnp.where(first, leaving_ref[...], between)
        mean_between = dot_parts(split(mean_ref[...]), high, NN) + back_ref[...]
        line_out[...] = jnp.where(first, mean_between, mean_ref[...])

    kept_half, sent_half, mean_line = call(
        divide_body, (columns_half, columns_half, line), "divide", inputs=5
    )(side, high_map, high_sum, leaving, mean_leaving, high_back)
    got_half = to_pair(sent_half)

    def mean_days_body(entering_ref, *refs):
        given = split(entering_ref[...])
        out_ref = refs[-1]
        for day in range(day_count):
            moved_ref, own_ref, current_ref = refs[3 * day : 3 * day + 3]
            current = current_ref[...] - dot_parts(given, split(moved_ref[...]), NT)
            out_ref[day] = dot_parts(split(current), (own_ref[0], own_ref[1]), NN)

    mean_days = call(
        mean_days_body, shape(day_count, LINES, nodes), "mean_days", scalars=0,
        inputs=1 + 3 * day_count,
    )(own_entering, *(saved[i] for saved in kept for i in (0, 1, 4)))

    def last_body(side_ref, keep_ref, got_ref, line_ref, days_ref, *refs):
        maps, locals_, out_ref = refs[:day_count], refs[day_count : 2 * day_count], refs[-1]
        first = side_ref[0] == 0
        spread = jnp.full((LINES, columns), 1.0 / LINES, BF16)

        def as_columns(lines):
            return sum(
                lax.dot_general(part, spread, (TN, ((), ())), preferred_element_type=F32)
                for part in split(lines)
            )

        low = jnp.where(first, keep_ref[...], got_ref[...])
        high = jnp.where(first, got_ref[...], keep_ref[...])
        following = jnp.concatenate([low, high], axis=1) + as_columns(line_ref[...])
        for day in reversed(range(day_count)):
            following = (
                dot_parts((maps[day][0], maps[day][1]), split(following), TN)
                + locals_[day][...]
                + as_columns(days_ref[day])
            )
            out_ref[day] = following

    return call(
        last_body, shape(day_count, nodes, columns), "last_days", inputs=4 + 2 * day_count
    )(
        side, kept_half, got_half, mean_line, mean_days,
        *(saved[2] for saved in kept), *(saved[3] for saved in kept),
    )


def solution(mesh):
    return jax.shard_map(
        local,
        mesh=mesh,
        in_specs=(
            P("tm", "row", None),
            P("tm", "row", None),
            P("tm", None, "row"),
            P(("tm", "row")),
            P(("tm", "row")),
            P(("tm", "row")),
        ),
        out_specs=P("tm", None, "row"),
        check_vma=False,
    )
```

```python
import functools

import jax
import jax.numpy as jnp
from jax import lax
from jax.experimental import pallas as pl
from jax.experimental.pallas import tpu as pltpu
from jax.sharding import PartitionSpec as P

F32 = jnp.float32
BF16 = jnp.bfloat16
CORES = 2
PAIR = 2
LINES = 8

NN = ((1,), (0,))
TN = ((0,), (0,))
NT = ((1,), (1,))


def split(value):
    high = value.astype(BF16)
    return high, (value - high.astype(F32)).astype(BF16)


def parts(ref):
    return ref[0], ref[1]


def dot_parts(left, right, dims):
    product = functools.partial(
        lax.dot_general, dimension_numbers=(dims, ((), ())), preferred_element_type=F32
    )
    return product(left[0], right[0]) + (product(left[0], right[1]) + product(left[1], right[0]))


def shape(*dims, dtype=F32):
    return jax.ShapeDtypeStruct(dims, dtype)


def in_vmem(value):
    return pltpu.with_memory_space_constraint(value, pltpu.VMEM)


def call(body, outs, name, scalars, arrays, work=1, scratch=(), out_specs=None):
    vmem = pl.BlockSpec(memory_space=pltpu.VMEM)
    out_shape = outs if out_specs else jax.tree.map(lambda o: pltpu.VMEM(o.shape, o.dtype), outs)
    return pl.pallas_call(
        body,
        out_shape=out_shape,
        in_specs=[pl.BlockSpec(memory_space=pltpu.SMEM)] * len(scalars) + [vmem] * len(arrays),
        out_specs=out_specs or jax.tree.map(lambda _: vmem, outs),
        scratch_shapes=list(scratch),
        compiler_params=pltpu.CompilerParams(vmem_limit_bytes=20 * 1024 * 1024),
        cost_estimate=pl.CostEstimate(
            flops=int(work * 1.0e9), transcendentals=0, bytes_accessed=1024
        ),
        name=name,
    )(*scalars, *map(in_vmem, arrays))


def bin_observations(obs_day, obs_node, obs_value, days, nodes):
    chunk = min(512, obs_day.shape[0])
    chunks = obs_day.shape[0] // chunk

    def body(day_ref, node_ref, value_ref, out_ref):
        total = jnp.zeros((3 * days, nodes), F32)
        for index in range(chunks):
            row = pl.ds(index, 1)
            value = value_ref[row, :]
            high = value.astype(BF16).astype(F32)
            middle = (value - high).astype(BF16).astype(F32)
            low = value - high - middle
            is_day = lax.broadcasted_iota(jnp.int32, (days, chunk), 0) == day_ref[row, :]
            marked = jnp.concatenate(
                [jnp.where(is_day, part, 0.0).astype(BF16) for part in (high, middle, low)], axis=0
            )
            is_node = lax.broadcasted_iota(jnp.int32, (nodes, chunk), 0) == node_ref[row, :]
            total += lax.dot_general(
                marked, is_node.astype(F32).astype(BF16), (NT, ((), ())), preferred_element_type=F32
            )
        out_ref[...] = total[:days] + (total[days : 2 * days] + total[2 * days :])

    return call(
        body,
        shape(days, nodes),
        "bin_observations",
        (),
        [value.reshape(chunks, chunk) for value in (obs_day, obs_node, obs_value)],
        work=2,
    )


def gather_rows(position_ref, refs, take, out_ref):
    share = refs[0].shape[-2]
    for offset, ref in enumerate(refs):
        at = pl.ds(pl.multiple_of((position_ref[0] ^ offset) * share, share), share)
        out_ref[0, at, :], out_ref[1, at, :] = split(ref[take(offset)])


def inverse_step(inverse, path, noise, wanted):
    moved = inverse if path is None else split(dot_parts(inverse, path, NN))
    current = dot_parts(split(wanted), inverse, NT)
    return moved, current, (
        dot_parts(moved, noise, TN),
        dot_parts(moved, moved, TN),
        dot_parts(split(current), moved, NN),
    )


def local(inv_diag, coupling, noise, obs_day, obs_node, obs_value):
    part_count = lax.axis_size("tm")
    row_count = lax.axis_size("row")
    my_part = lax.axis_index("tm")
    my_row = lax.axis_index("row")
    day_count, share, nodes = inv_diag.shape
    columns = noise.shape[2]
    half = columns // PAIR
    half_nodes = nodes // CORES
    groups = part_count // PAIR
    early = day_count // 2

    def to_row(value, distance):
        return lax.ppermute(value, "row", [(i, i ^ distance) for i in range(row_count)])

    def to_pair(value):
        return lax.ppermute(value, "tm", [(i, i ^ 1) for i in range(part_count)])

    def to_group(value, source, target):
        return lax.ppermute(
            value, "tm", [(PAIR * source + i, PAIR * target + i) for i in range(PAIR)]
        )

    position = jnp.reshape(my_row, (1,)).astype(jnp.int32)
    side = jnp.reshape(my_part % PAIR, (1,)).astype(jnp.int32)
    core = jnp.reshape(my_row % CORES, (1,)).astype(jnp.int32)

    line = shape(LINES, nodes)
    square = shape(nodes, nodes)
    map_parts = shape(2, nodes, nodes, dtype=BF16)
    columns_half = shape(nodes, half)
    columns_full = shape(nodes, columns)

    def after(value, *others):
        return lax.optimization_barrier((value, *others))[0]

    ranges = [(inv_diag, 0, early), (coupling, 0, early), (inv_diag, early, day_count)]
    ranges += [(coupling, day, day + 1) for day in range(early, day_count)]
    arrived = []
    for index, (values, start, stop) in enumerate(ranges):
        rows = values[start:stop]
        if index >= 2:
            rows = after(rows, *arrived[index - 2])
        arrived.append([to_row(rows, distance) for distance in range(CORES, row_count, CORES)])

    def shared(index, *ahead):
        pieces = []
        for got in arrived[index]:
            pieces += [got, to_row(after(got, *ahead) if ahead else got, 1)]
        return pieces

    own_inverse = [inv_diag, to_row(inv_diag, 1)]
    own_link = [coupling, to_row(coupling, 1)]

    def taking(start, day):
        return lambda offset: day if offset < CORES else day - start

    right_side = bin_observations(obs_day, obs_node, obs_value, part_count * day_count, nodes)
    distance = part_count // 2
    while distance:
        count = right_side.shape[0] // 2
        upper = (my_part // distance) % 2 == 1
        low, high = right_side[:count], right_side[count:]
        got = lax.ppermute(
            jnp.where(upper, low, high), "tm", [(i, i ^ distance) for i in range(part_count)]
        )
        right_side = jnp.where(upper, high, low) + got
        distance //= 2
    distance = 1
    while distance < row_count:
        right_side = right_side + to_row(right_side, distance)
        distance *= 2
    right_side = jnp.broadcast_to(right_side[:, None, :], (day_count, LINES, nodes))

    def early_body(position_ref, *refs):
        inverse_refs, link_refs = refs[:row_count], refs[row_count : 2 * row_count]
        noise_ref, source_ref = refs[2 * row_count : 2 * row_count + 2]
        path_out, gram_out, sum_out, applied_out, back_out = refs[2 * row_count + 2 :][:5]
        inverse_out, link_out, moved_out, current_out = refs[2 * row_count + 7 :]
        path = applied = None
        for day in range(early):
            gather_rows(position_ref, inverse_refs, taking(0, day), inverse_out.at[day])
            gather_rows(position_ref, link_refs, taking(0, day), link_out.at[day])
            wanted = source_ref[day] if day == 0 else source_ref[day] - applied
            moved, current, terms = inverse_step(
                parts(inverse_out.at[day]), path, split(noise_ref[day]), wanted
            )
            moved_out[day, 0], moved_out[day, 1] = moved
            current_out[day] = current
            link = parts(link_out.at[day])
            path_value = -dot_parts(link, moved, NN)
            path = split(path_value)
            applied = dot_parts(split(current), link, NT)
            for out, term in zip((sum_out, gram_out, back_out), terms, strict=True):
                out[...] = term if day == 0 else out[...] + term
        path_out[0], path_out[1] = path
        applied_out[...] = applied

    def several(count, value):
        return shape(count, *value.shape, dtype=value.dtype)

    (path, gram, summed, applied, back, inverses_0, links_0, moved_0, currents_0) = call(
        early_body,
        (
            map_parts, square, columns_full, line, line,
            several(early, map_parts), several(early, map_parts), several(early, map_parts),
            several(early, line),
        ),
        "early_days",
        (position,),
        [*own_inverse, *shared(0), *own_link, *shared(1), noise, right_side],
        work=6,
    )

    def late_body(position_ref, *refs):
        inverse_refs = refs[:row_count]
        noise_ref, source_ref, path_ref, gram_ref, sum_ref, applied_ref, back_ref = refs[
            row_count : row_count + 7
        ]
        gram_out, sum_out, back_out, inverse_out, moved_out, current_out = refs[row_count + 7 :]
        for day in range(early, day_count):
            gather_rows(
                position_ref, inverse_refs, taking(early, day), inverse_out.at[day - early]
            )
        moved, current, terms = inverse_step(
            parts(inverse_out.at[0]),
            parts(path_ref),
            split(noise_ref[early]),
            source_ref[early] - applied_ref[...],
        )
        moved_out[0], moved_out[1] = moved
        current_out[...] = current
        sum_out[...] = sum_ref[...] + terms[0]
        gram_out[...] = gram_ref[...] + terms[1]
        back_out[...] = back_ref[...] + terms[2]

    late = day_count - early
    gram, summed, back, inverses_1, moved, current = call(
        late_body,
        (square, columns_full, line, several(late, map_parts), map_parts, line),
        "late_inverses",
        (position,),
        [
            *own_inverse, *shared(2, path), noise, right_side, path, gram, summed, applied, back,
        ],
        work=3,
    )
    moved_late, current_late, links_late = [moved], [current], []

    def next_body(day, position_ref, *refs):
        link_refs = refs[:row_count]
        (noise_ref, source_ref, inverse_ref, gram_ref, sum_ref, back_ref, moved_ref, current_ref) = (
            refs[row_count : row_count + 8]
        )
        gram_out, sum_out, back_out, link_out, moved_out, current_out = refs[row_count + 8 :]
        gather_rows(position_ref, link_refs, taking(day, day), link_out)
        link = parts(link_out)
        path = split(-dot_parts(link, parts(moved_ref), NN))
        applied = dot_parts(split(current_ref[...]), link, NT)
        moved, current, terms = inverse_step(
            parts(inverse_ref.at[day + 1 - early]),
            path,
            split(noise_ref[day + 1]),
            source_ref[day + 1] - applied,
        )
        moved_out[0], moved_out[1] = moved
        current_out[...] = current
        sum_out[...] = sum_ref[...] + terms[0]
        gram_out[...] = gram_ref[...] + terms[1]
        back_out[...] = back_ref[...] + terms[2]

    for day in range(early, day_count - 1):
        gram, summed, back, link, moved, current = call(
            functools.partial(next_body, day),
            (square, columns_full, line, map_parts, map_parts, line),
            f"late_day_{day}",
            (position,),
            [
                *own_link, *shared(3 + day - early, moved), noise, right_side, inverses_1, gram, summed,
                back, moved, current,
            ],
            work=4,
        )
        moved_late.append(moved)
        current_late.append(current)
        links_late.append(link)

    def halves_body(side_ref, sum_ref, keep, send):
        low, high = sum_ref[:, :half], sum_ref[:, half:]
        first = side_ref[0] == 0
        keep[...] = jnp.where(first, low, high)
        send[...] = jnp.where(first, high, low)

    keep, send = call(
        halves_body, (columns_half, columns_half), "halves", (side,), [summed], work=0.1
    )
    other_sum = to_pair(send)

    def last_link_body(position_ref, core_ref, *refs):
        link_refs = refs[:row_count]
        moved_ref, current_ref, path_out, half_out, flux_out, link_out, whole = refs[row_count:]
        gather_rows(position_ref, link_refs, taking(day_count - 1, day_count - 1), link_out)
        link = parts(link_out)
        whole[...] = -dot_parts(link, parts(moved_ref), NN)
        half_out[...] = whole[
            pl.ds(pl.multiple_of(core_ref[0] * half_nodes, half_nodes), half_nodes), :
        ]
        path_out[0], path_out[1] = split(whole[...])
        flux_out[...] = dot_parts(split(current_ref[...]), link, NT)

    path, path_half, flux, link = call(
        last_link_body,
        (map_parts, shape(half_nodes, nodes), line, map_parts),
        "last_link",
        (position, core),
        [*own_link, *shared(2 + late, moved), moved, current],
        work=1.5,
        scratch=[pltpu.VMEM((nodes, nodes), F32)],
    )
    links_late.append(link)
    other_half = to_pair(after(path_half, other_sum))
    other_flux = to_pair(flux)
    other_rest = to_row(other_half, 1)

    def own_maps_body(noise_ref, inverse_0, inverse_1, link_0, *refs):
        link_refs, (map_out, local_out) = refs[:late], refs[late:]
        for day in range(day_count):
            inverse = parts(inverse_0.at[day] if day < early else inverse_1.at[day - early])
            link = parts(link_0.at[day] if day < early else link_refs[day - early])
            map_out[day, 0], map_out[day, 1] = split(-dot_parts(link, inverse, NN))
            local_out[day] = dot_parts(inverse, split(noise_ref[day]), TN)

    step_maps, local_terms = call(
        own_maps_body,
        (several(day_count, map_parts), several(day_count, columns_full)),
        "own_maps",
        (),
        [noise, inverses_0, inverses_1, links_0, *links_late],
        work=2 * day_count,
    )

    def pair_body(
        side_ref, core_ref, path_ref, half_ref, rest_ref, sum_ref, other_ref, flux_ref,
        other_flux_ref, maps_out, sum_out, high_sum_out, flux_out, low_flux_out,
    ):
        me, mate = side_ref[0], 1 - side_ref[0]
        mine = core_ref[0]
        maps_out[me] = path_ref[...]
        for which, ref in ((mine, half_ref), (1 - mine, rest_ref)):
            at = pl.ds(pl.multiple_of(which * half_nodes, half_nodes), half_nodes)
            maps_out[mate, 0, at, :], maps_out[mate, 1, at, :] = split(ref[...])
        first = me == 0
        low_sum = jnp.where(first, sum_ref[...], other_ref[...])
        high_sum = jnp.where(first, other_ref[...], sum_ref[...])
        low_flux = jnp.where(first, flux_ref[...], other_flux_ref[...])
        high_flux = jnp.where(first, other_flux_ref[...], flux_ref[...])
        sum_out[...] = dot_parts(parts(maps_out.at[0]), split(high_sum), TN) + low_sum
        high_sum_out[...] = high_sum
        flux_out[...] = dot_parts(split(low_flux), parts(maps_out.at[1]), NT) + high_flux
        low_flux_out[...] = low_flux

    pair_maps, pair_sum, high_sum, pair_flux, low_flux = call(
        pair_body,
        (several(PAIR, map_parts), columns_half, columns_half, line, line),
        "pair_maps",
        (side, core),
        [after(path, local_terms), other_half, other_rest, keep, other_sum, flux, other_flux],
        work=1.5,
    )

    def group_map_body(maps_ref, out_ref):
        out_ref[0], out_ref[1] = split(
            dot_parts(parts(maps_ref.at[1]), parts(maps_ref.at[0]), NN)
        )

    group_map = call(group_map_body, map_parts, "group_map", (), [pair_maps])

    def advance_body(map_ref, local_ref, got_ref, out_ref):
        out_ref[...] = dot_parts(parts(map_ref), split(got_ref[...]), TN) + local_ref[...]

    def line_body(dims, map_ref, local_ref, got_ref, out_ref):
        out_ref[...] = dot_parts(split(got_ref[...]), parts(map_ref), dims) + local_ref[...]

    leaving = None
    value = pair_sum
    for group in range(groups - 1, 0, -1):
        got = to_group(value, group, group - 1)
        leaving = got if leaving is None else leaving + got
        if group > 1:
            value = call(
                advance_body, columns_half, "noise_link", (), [group_map, pair_sum, leaving]
            )

    entering = None
    value = pair_flux
    for group in range(groups - 1):
        got = to_group(value, group, group + 1)
        entering = got if entering is None else entering + got
        if group < groups - 2:
            value = call(
                functools.partial(line_body, NT), line, "forward_link", (),
                [group_map, pair_flux, entering], work=0.5,
            )

    def turn_body(side_ref, maps_ref, flux_ref, entering_ref, gram_ref, back_ref, own_out, back_out):
        given = entering_ref[...]
        after = dot_parts(split(given), parts(maps_ref.at[0]), NT) + flux_ref[...]
        given = jnp.where(side_ref[0] == 0, given, after)
        own_out[...] = given
        back_out[...] = back_ref[...] - dot_parts(split(given), split(gram_ref[...]), NN)

    own_entering, own_back = call(
        turn_body, (line, line), "mean_turn", (side,),
        [pair_maps, low_flux, entering, gram, back],
    )
    other_back = to_pair(own_back)

    def pair_back_body(side_ref, maps_ref, own_ref, other_ref, pair_out, high_out):
        first = side_ref[0] == 0
        low = jnp.where(first, own_ref[...], other_ref[...])
        high = jnp.where(first, other_ref[...], own_ref[...])
        pair_out[...] = dot_parts(split(high), parts(maps_ref.at[0]), NN) + low
        high_out[...] = high

    pair_back, high_back = call(
        pair_back_body, (line, line), "pair_back", (side,), [pair_maps, own_back, other_back],
        work=0.5,
    )
    mean_leaving = None
    value = pair_back
    for group in range(groups - 1, 0, -1):
        got = to_group(value, group, group - 1)
        mean_leaving = got if mean_leaving is None else mean_leaving + got
        if group > 1:
            value = call(
                functools.partial(line_body, NN), line, "backward_link", (),
                [group_map, pair_back, mean_leaving], work=0.5,
            )

    def divide_body(side_ref, maps_ref, sum_ref, leaving_ref, keep_out, send_out):
        between = dot_parts(parts(maps_ref.at[1]), split(leaving_ref[...]), TN) + sum_ref[...]
        first = side_ref[0] == 0
        keep_out[...] = jnp.where(first, between, leaving_ref[...])
        send_out[...] = jnp.where(first, leaving_ref[...], between)

    kept_half, sent_half = call(
        divide_body, (columns_half, columns_half), "divide", (side,),
        [pair_maps, high_sum, leaving],
    )
    got_half = to_pair(sent_half)

    def as_columns(lines):
        spread = jnp.full((LINES, columns), 1.0 / LINES, BF16)
        return sum(
            lax.dot_general(part, spread, (TN, ((), ())), preferred_element_type=F32)
            for part in split(lines)
        )

    def terms_body(entering_ref, local_ref, inverse_0, inverse_1, moved_0_ref, current_0, *refs):
        out_ref = refs[-1]
        given = split(entering_ref[...])
        for day in range(day_count):
            if day < early:
                inverse, moved = inverse_0.at[day], moved_0_ref.at[day]
                current = current_0[day]
            else:
                inverse, moved = inverse_1.at[day - early], refs[day - early]
                current = refs[late + day - early][...]
            current = current - dot_parts(given, parts(moved), NT)
            term = dot_parts(split(current), parts(inverse), NN)
            out_ref[day] = local_ref[day] + as_columns(term)

    terms = call(
        terms_body, several(day_count, columns_full), "mean_terms", (),
        [
            own_entering, local_terms, inverses_0, inverses_1, moved_0, currents_0,
            *moved_late, *current_late,
        ],
        work=4,
    )

    def last_body(
        side_ref, keep_ref, got_ref, mean_ref, back_ref, pair_ref, map_ref, term_ref, out_ref,
        held, sems,
    ):
        first = side_ref[0] == 0
        between = dot_parts(split(mean_ref[...]), parts(pair_ref.at[1]), NN) + back_ref[...]
        mean = jnp.where(first, between, mean_ref[...])
        low = jnp.where(first, keep_ref[...], got_ref[...])
        high = jnp.where(first, got_ref[...], keep_ref[...])
        following = jnp.concatenate([low, high], axis=1) + as_columns(mean)
        copies = []
        for day in reversed(range(day_count)):
            following = dot_parts(parts(map_ref.at[day]), split(following), TN) + term_ref[day]
            held[day] = following
            copies.append(
                pltpu.make_async_copy(held.at[day], out_ref.at[day], sems.at[day])
            )
            copies[-1].start()
        for copy in copies:
            copy.wait()

    return call(
        last_body, shape(day_count, nodes, columns), "last_days", (side,),
        [kept_half, got_half, mean_leaving, high_back, pair_maps, step_maps, terms],
        work=4,
        scratch=[
            pltpu.VMEM((day_count, nodes, columns), F32), pltpu.SemaphoreType.DMA((day_count,)),
        ],
        out_specs=pl.BlockSpec(memory_space=pl.ANY),
    )


def solution(mesh):
    return jax.shard_map(
        local,
        mesh=mesh,
        in_specs=(
            P("tm", "row", None),
            P("tm", "row", None),
            P("tm", None, "row"),
            P(("tm", "row")),
            P(("tm", "row")),
            P(("tm", "row")),
        ),
        out_specs=P("tm", None, "row"),
        check_vma=False,
    )
```

```python
import functools

import jax
import jax.numpy as jnp
from jax import lax
from jax.experimental import pallas as pl
from jax.experimental.pallas import tpu as pltpu
from jax.sharding import PartitionSpec as P

F32 = jnp.float32
BF16 = jnp.bfloat16
CORES = 2
PAIR = 2
LINES = 8

NN = ((1,), (0,))
TN = ((0,), (0,))
NT = ((1,), (1,))


def split(value):
    high = value.astype(BF16)
    return high, (value - high.astype(F32)).astype(BF16)


def parts(ref):
    return ref[0], ref[1]


def dot_parts(left, right, dims):
    product = functools.partial(
        lax.dot_general, dimension_numbers=(dims, ((), ())), preferred_element_type=F32
    )
    return product(left[0], right[0]) + (product(left[0], right[1]) + product(left[1], right[0]))


def shape(*dims, dtype=F32):
    return jax.ShapeDtypeStruct(dims, dtype)


def in_vmem(value):
    return pltpu.with_memory_space_constraint(value, pltpu.VMEM)


def call(body, outs, name, scalars, arrays, work=1, scratch=(), out_specs=None):
    vmem = pl.BlockSpec(memory_space=pltpu.VMEM)
    out_shape = outs if out_specs else jax.tree.map(lambda o: pltpu.VMEM(o.shape, o.dtype), outs)
    return pl.pallas_call(
        body,
        out_shape=out_shape,
        in_specs=[pl.BlockSpec(memory_space=pltpu.SMEM)] * len(scalars) + [vmem] * len(arrays),
        out_specs=out_specs or jax.tree.map(lambda _: vmem, outs),
        scratch_shapes=list(scratch),
        compiler_params=pltpu.CompilerParams(vmem_limit_bytes=12 * 1024 * 1024),
        cost_estimate=pl.CostEstimate(
            flops=int(work * 2.0e8), transcendentals=0, bytes_accessed=1024
        ),
        name=name,
    )(*scalars, *map(in_vmem, arrays))


def deal(where_ref, distance, total, keep_out, sent_out):
    count = total.shape[0] // 2
    upper = (where_ref[1] & distance) != 0
    keep_out[...] = jnp.where(upper, total[count:], total[:count])
    sent_out[...] = jnp.where(upper, total[:count], total[count:])


def halved(where, distance, keep, got):
    def body(where_ref, keep_ref, got_ref, *outs):
        total = keep_ref[...] + got_ref[...]
        if distance:
            deal(where_ref, distance, total, *outs)
        else:
            outs[0][...] = total

    days, nodes = keep.shape
    outs = [shape(days // 2, nodes)] * 2 if distance else [keep]
    outs = [shape(*out.shape) for out in outs]
    return (*call(body, outs, "halved", (where,), [keep, got], work=0.05), None)[:2]


def bin_observations(where, obs_day, obs_node, obs_value, days, nodes, distance):
    chunk = min(512, obs_day.shape[0])
    chunks = obs_day.shape[0] // chunk

    def body(where_ref, day_ref, node_ref, value_ref, keep_out, sent_out):
        total = jnp.zeros((3 * days, nodes), F32)
        for index in range(chunks):
            row = pl.ds(index, 1)
            value = value_ref[row, :]
            high = value.astype(BF16).astype(F32)
            middle = (value - high).astype(BF16).astype(F32)
            low = value - high - middle
            is_day = lax.broadcasted_iota(jnp.int32, (days, chunk), 0) == day_ref[row, :]
            marked = jnp.concatenate(
                [jnp.where(is_day, part, 0.0).astype(BF16) for part in (high, middle, low)], axis=0
            )
            is_node = lax.broadcasted_iota(jnp.int32, (nodes, chunk), 0) == node_ref[row, :]
            total += lax.dot_general(
                marked, is_node.astype(F32).astype(BF16), (NT, ((), ())), preferred_element_type=F32
            )
        total = total[:days] + (total[days : 2 * days] + total[2 * days :])
        deal(where_ref, distance, total, keep_out, sent_out)

    return call(
        body,
        [shape(days // 2, nodes)] * 2,
        "bin_observations",
        (where,),
        [value.reshape(chunks, chunk) for value in (obs_day, obs_node, obs_value)],
        work=2,
    )


def gather_rows(where_ref, refs, take, out_ref):
    share = refs[0].shape[-2]
    for offset, ref in enumerate(refs):
        at = pl.ds(pl.multiple_of((where_ref[0] ^ offset) * share, share), share)
        if len(ref.shape) == 3:
            ref = ref.at[take(offset) if callable(take) else take]
        out_ref[0, at, :], out_ref[1, at, :] = split(ref[...])


def local(inv_diag, coupling, noise, obs_day, obs_node, obs_value):
    part_count = lax.axis_size("tm")
    row_count = lax.axis_size("row")
    my_part = lax.axis_index("tm")
    my_row = lax.axis_index("row")
    day_count, share, nodes = inv_diag.shape
    columns = noise.shape[2]
    half = columns // PAIR
    half_nodes = nodes // CORES
    groups = part_count // PAIR
    early = day_count // 2
    late = day_count - early

    def to_row(value, distance):
        return lax.ppermute(value, "row", [(i, i ^ distance) for i in range(row_count)])

    def to_pair(value):
        return lax.ppermute(value, "tm", [(i, i ^ 1) for i in range(part_count)])

    def to_group(value, source, target):
        return lax.ppermute(
            value, "tm", [(PAIR * source + i, PAIR * target + i) for i in range(PAIR)]
        )

    def after(value, *others):
        return lax.optimization_barrier((value, *others))[0]

    where = jnp.stack([my_row, my_part]).astype(jnp.int32)

    line = shape(LINES, nodes)
    square = shape(nodes, nodes)
    map_parts = shape(2, nodes, nodes, dtype=BF16)
    samples_half = shape(half, nodes)
    samples_full = shape(columns, nodes)

    keep, sent = bin_observations(
        where, obs_day, obs_node, obs_value, part_count * day_count, nodes, part_count // 2
    )

    arrived = []

    def send_rows(rows):
        arrived.append([to_row(rows, distance) for distance in range(CORES, row_count, CORES)])

    for day in range(early):
        blocks = (inv_diag[day], coupling[day])
        if day:
            blocks = tuple(after(block, stacked) for block in blocks)
        stacked = jnp.stack(blocks)
        send_rows(stacked)
    late_rows = [inv_diag[early:], *(coupling[day : day + 1] for day in range(early, day_count))]
    where = after(where, keep, stacked, *late_rows)
    for index, rows in enumerate(late_rows):
        send_rows(after(rows, *arrived[index]))

    def shared(index, *ahead):
        pieces = []
        for got in arrived[index]:
            pieces += [got, to_row(after(got, *ahead) if ahead else got, 1)]
        return pieces

    own_inverse = [inv_diag, to_row(inv_diag, 1)]
    own_link = [coupling, to_row(coupling, 1)]

    def taking(start, day):
        return lambda offset: day if offset < CORES else day - start

    reduced = []
    distance = part_count // 2
    while distance:
        got = lax.ppermute(sent, "tm", [(i, i ^ distance) for i in range(part_count)])
        distance //= 2
        keep, sent = halved(where, distance, keep, got)
        reduced.append(keep)
    right_side = keep
    distance = 1
    while distance < row_count:
        right_side = right_side + to_row(right_side, distance)
        distance *= 2
    right_side = jnp.broadcast_to(right_side[:, None, :], (day_count, LINES, nodes))

    def store(out_ref, pair):
        out_ref[0], out_ref[1] = pair

    def early_body(day, where_ref, *refs):
        inverse_refs, link_refs = list(refs[:CORES]), list(refs[CORES : 2 * CORES])
        got_refs, refs = refs[2 * CORES : CORES + row_count], refs[CORES + row_count :]
        state_refs, refs = refs[: 3 if day else 0], refs[3 if day else 0 :]
        noise_ref, path_out, gram_out, sum_out, inverse_out, link_out, moved_out = refs[:7]
        map_out, term_out = refs[7:]
        gather_rows(
            where_ref, inverse_refs + [ref.at[0] for ref in got_refs], day, inverse_out
        )
        gather_rows(where_ref, link_refs + [ref.at[1] for ref in got_refs], day, link_out)
        inverse, link = parts(inverse_out), parts(link_out)
        given = split(noise_ref[day])
        term = dot_parts(given, inverse, TN)
        step = split(-dot_parts(link, inverse, NN))
        if day == 0:
            moved, path, total, gram = inverse, step, term, 0.0
        else:
            moved = split(dot_parts(inverse, parts(state_refs[0]), NN))
            path = split(-dot_parts(link, moved, NN))
            total = state_refs[1][...] + dot_parts(given, moved, TN)
            gram = state_refs[2][...]
        store(path_out, path)
        store(moved_out, moved)
        store(map_out, step)
        sum_out[...] = total
        gram_out[...] = gram + dot_parts(moved, moved, TN)
        term_out[...] = term

    state = []
    inverses, links, moveds, step_maps, local_terms = [], [], [], [], []
    for day in range(early):
        ahead = (right_side, *state[:1]) if day else (where, reduced[len(reduced) // 2])
        path, gram, summed, inverse, link, moved, step, term = call(
            functools.partial(early_body, day),
            (
                map_parts, square, samples_full, map_parts, map_parts, map_parts, map_parts,
                samples_full,
            ),
            f"day_{day}",
            (where,),
            [
                *own_inverse, *own_link,
                *(piece for piece in shared(day, *ahead)), *state, noise,
            ],
            work=5,
        )
        state = [path, summed, gram]
        for kept, value in zip(
            (inverses, links, moveds, step_maps, local_terms),
            (inverse, link, moved, step, term),
            strict=True,
        ):
            kept.append(value)

    def early_lines_body(source_ref, *refs):
        applied_out, back_out, current_out = refs[-3:]
        applied = back = None
        for day in range(early):
            inverse_ref, link_ref, moved_ref = refs[3 * day : 3 * day + 3]
            wanted = source_ref[day] if day == 0 else source_ref[day] - applied
            current = dot_parts(split(wanted), parts(inverse_ref), NT)
            current_out[day] = current
            applied = dot_parts(split(current), parts(link_ref), NT)
            term = dot_parts(split(current), parts(moved_ref), NN)
            back = term if day == 0 else back + term
        applied_out[...] = applied
        back_out[...] = back

    applied, back, early_currents = call(
        early_lines_body,
        (line, line, shape(early, LINES, nodes)),
        "early_lines",
        (),
        [
            right_side,
            *(ref for day in range(early) for ref in (inverses[day], links[day], moveds[day])),
        ],
        work=2,
    )

    def late_body(where_ref, *refs):
        inverse_refs, refs = refs[:row_count], refs[row_count:]
        noise_ref, source_ref, path_ref, sum_ref, gram_ref, applied_ref, back_ref = refs[:7]
        gram_out, sum_out, back_out, moved_out, current_out = refs[7:12]
        inverse_outs, term_outs = refs[12 : 12 + late], refs[12 + late :]
        for index in range(late):
            gather_rows(
                where_ref, inverse_refs, taking(early, early + index), inverse_outs[index]
            )
        inverse = parts(inverse_outs[0])
        moved = split(dot_parts(inverse, parts(path_ref), NN))
        store(moved_out, moved)
        current = dot_parts(split(source_ref[early] - applied_ref[...]), inverse, NT)
        current_out[...] = current
        for index in range(late):
            given = split(noise_ref[early + index])
            term_outs[index][...] = dot_parts(given, parts(inverse_outs[index]), TN)
            if index == 0:
                sum_out[...] = sum_ref[...] + dot_parts(given, moved, TN)
        gram_out[...] = gram_ref[...] + dot_parts(moved, moved, TN)
        back_out[...] = back_ref[...] + dot_parts(split(current), moved, NN)

    results = call(
        late_body,
        (square, samples_full, line, map_parts, line, *[map_parts] * late, *[samples_full] * late),
        "late_inverses",
        (where,),
        [*own_inverse, *shared(early, path), noise, right_side, *state, applied, back],
        work=4,
    )
    gram, summed, back, moved, current = results[:5]
    inverses += results[5 : 5 + late]
    local_terms += results[5 + late :]
    moveds.append(moved)
    late_currents = [current]

    def next_body(day, where_ref, *refs):
        link_refs, refs = refs[:row_count], refs[row_count:]
        noise_ref, source_ref, inverse_ref, gram_ref, sum_ref, back_ref, moved_ref, current_ref = (
            refs[:8]
        )
        gram_out, back_out, link_out, moved_out, current_out, *sum_outs = refs[8:]
        gather_rows(where_ref, link_refs, taking(day, day), link_out)
        link, inverse = parts(link_out), parts(inverse_ref)
        path = split(-dot_parts(link, parts(moved_ref), NN))
        moved = split(dot_parts(inverse, path, NN))
        store(moved_out, moved)
        total = sum_ref[...] + dot_parts(split(noise_ref[day + 1]), moved, TN)
        if len(sum_outs) == 1:
            sum_outs[0][...] = total
        else:
            first = (where_ref[1] & (PAIR - 1)) == 0
            sum_outs[0][...] = jnp.where(first, total[:half], total[half:])
            sum_outs[1][...] = jnp.where(first, total[half:], total[:half])
        applied = dot_parts(split(current_ref[...]), link, NT)
        current = dot_parts(split(source_ref[day + 1] - applied), inverse, NT)
        current_out[...] = current
        gram_out[...] = gram_ref[...] + dot_parts(moved, moved, TN)
        back_out[...] = back_ref[...] + dot_parts(split(current), moved, NN)

    for day in range(early, day_count - 1):
        sums = [samples_half] * 2 if day == day_count - 2 else [samples_full]
        gram, back, link, moved, current, *sums = call(
            functools.partial(next_body, day),
            (square, line, map_parts, map_parts, line, *sums),
            f"day_{day}",
            (where,),
            [
                *own_link, *shared(day + 1, moved), noise, right_side, inverses[day + 1], gram,
                summed, back, moved, current,
            ],
            work=4,
        )
        summed = sums[0]
        moveds.append(moved)
        late_currents.append(current)
        links.append(link)
    keep, send = sums
    other_sum = to_pair(send)

    def last_link_body(where_ref, *refs):
        link_refs, refs = refs[:row_count], refs[row_count:]
        moved_ref, current_ref, path_out, half_out, flux_out, link_out, whole = refs
        gather_rows(where_ref, link_refs, taking(day_count - 1, day_count - 1), link_out)
        link = parts(link_out)
        whole[...] = -dot_parts(link, parts(moved_ref), NN)
        half_out[...] = whole[
            pl.ds(pl.multiple_of((where_ref[0] & (CORES - 1)) * half_nodes, half_nodes), half_nodes), :
        ]
        store(path_out, split(whole[...]))
        flux_out[...] = dot_parts(split(current_ref[...]), link, NT)

    path, path_half, flux, link = call(
        last_link_body,
        (map_parts, shape(half_nodes, nodes), line, map_parts),
        "last_link",
        (where,),
        [*own_link, *shared(day_count, moved, send), moved, current],
        work=1.5,
        scratch=[pltpu.VMEM((nodes, nodes), F32)],
    )
    links.append(link)

    def late_maps_body(*refs):
        for index in range(late):
            store(
                refs[2 * late + index],
                split(-dot_parts(parts(refs[late + index]), parts(refs[index]), NN)),
            )

    step_maps += call(
        late_maps_body, [map_parts] * late, "late_maps", (), [*inverses[early:], *links[early:]],
        work=late,
    )
    other_half = to_pair(after(path_half, other_sum, *step_maps[early:]))
    other_flux = to_pair(flux)
    other_rest = to_row(other_half, 1)

    def pair_body(
        where_ref, path_ref, half_ref, rest_ref, sum_ref, other_ref, flux_ref,
        other_flux_ref, low_out, high_out, sum_out, high_sum_out, flux_out, low_flux_out, maps,
    ):
        me = where_ref[1] & (PAIR - 1)
        mate = 1 - me
        mine = (where_ref[0] & (CORES - 1))
        maps[me] = path_ref[...]
        for which, ref in ((mine, half_ref), (1 - mine, rest_ref)):
            at = pl.ds(pl.multiple_of(which * half_nodes, half_nodes), half_nodes)
            maps[mate, 0, at, :], maps[mate, 1, at, :] = split(ref[...])
        first = me == 0
        low_sum = jnp.where(first, sum_ref[...], other_ref[...])
        high_sum = jnp.where(first, other_ref[...], sum_ref[...])
        low_flux = jnp.where(first, flux_ref[...], other_flux_ref[...])
        high_flux = jnp.where(first, other_flux_ref[...], flux_ref[...])
        low_out[...] = maps[0]
        high_out[...] = maps[1]
        sum_out[...] = dot_parts(split(high_sum), parts(low_out), NN) + low_sum
        high_sum_out[...] = high_sum
        flux_out[...] = dot_parts(split(low_flux), parts(high_out), NT) + high_flux
        low_flux_out[...] = low_flux

    low_map, high_map, pair_sum, high_sum, pair_flux, low_flux = call(
        pair_body,
        (map_parts, map_parts, samples_half, samples_half, line, line),
        "pair_maps",
        (where,),
        [path, other_half, other_rest, keep, other_sum, flux, other_flux],
        work=1.5,
        scratch=[pltpu.VMEM((PAIR, 2, nodes, nodes), BF16)],
    )

    def group_map_body(low_ref, high_ref, out_ref):
        store(out_ref, split(dot_parts(parts(high_ref), parts(low_ref), NN)))

    group_map = call(
        group_map_body, map_parts, "group_map", (), [low_map, after(high_map, pair_sum)]
    )

    def link_body(dims, map_ref, local_ref, *refs):
        got = refs[0][...]
        for ref in refs[1:-1]:
            got = got + ref[...]
        refs[-1][...] = dot_parts(split(got), parts(map_ref), dims) + local_ref[...]

    def linked(dims, value_map, value, got, name):
        return call(
            functools.partial(link_body, dims), shape(*value.shape), name, (),
            [value_map, value, *got], work=0.6,
        )

    def turn_body(where_ref, low_ref, flux_ref, gram_ref, back_ref, *refs):
        own_out, back_out = refs[-2:]
        given = refs[0][...]
        for ref in refs[1:-2]:
            given = given + ref[...]
        behind = dot_parts(split(given), parts(low_ref), NT) + flux_ref[...]
        given = jnp.where((where_ref[1] & (PAIR - 1)) == 0, given, behind)
        own_out[...] = given
        back_out[...] = back_ref[...] - dot_parts(split(given), split(gram_ref[...]), NN)

    def pair_back_body(where_ref, map_ref, own_ref, other_ref, pair_out, high_out):
        first = (where_ref[1] & (PAIR - 1)) == 0
        low = jnp.where(first, own_ref[...], other_ref[...])
        high = jnp.where(first, other_ref[...], own_ref[...])
        pair_out[...] = dot_parts(split(high), parts(map_ref), NN) + low
        high_out[...] = high

    mean = {}

    def mean_hops():
        value, got = pair_flux, []
        ahead = yield
        for group in range(groups - 1):
            got.append(to_group(after(value, *ahead), group, group + 1))
            if group < groups - 2:
                value = linked(NT, group_map, pair_flux, got, "forward_link")
            ahead = yield (value if group < groups - 2 else got[-1])
        mean["entering"], own_back = call(
            turn_body, (line, line), "mean_turn", (where,),
            [low_map, low_flux, gram, back, *got],
        )
        other_back = to_pair(after(own_back, *ahead))
        value, mean["high_back"] = call(
            pair_back_body, (line, line), "pair_back", (where,), [low_map, own_back, other_back],
            work=0.6,
        )
        pair_back, got = value, []
        ahead = yield value
        for group in range(groups - 1, 0, -1):
            got.append(to_group(after(value, *ahead), group, group - 1))
            if group > 1:
                value = linked(NN, group_map, pair_back, got, "backward_link")
            mean["leaving"] = got
            ahead = yield (value if group > 1 else got[-1])

    hops = mean_hops()
    next(hops)

    leaving = []
    value = pair_sum
    for group in range(groups - 1, 0, -1):
        got = to_group(value, group, group - 1)
        hops.send((value,))
        brought = hops.send(())
        leaving.append(after(got, brought))
        if group > 1:
            value = linked(NN, group_map, pair_sum, leaving, "noise_link")

    def divide_body(where_ref, map_ref, sum_ref, *refs):
        keep_out, send_out = refs[-2:]
        given = refs[0][...]
        for ref in refs[1:-2]:
            given = given + ref[...]
        between = dot_parts(split(given), parts(map_ref), NN) + sum_ref[...]
        first = (where_ref[1] & (PAIR - 1)) == 0
        keep_out[...] = jnp.where(first, between, given)
        send_out[...] = jnp.where(first, given, between)

    kept_half, sent_half = call(
        divide_body, (samples_half, samples_half), "divide", (where,),
        [high_map, high_sum, *leaving],
    )
    got_half = to_pair(sent_half)
    hops.send((sent_half,))

    def terms_body(entering_ref, early_ref, *refs):
        outs = refs[-day_count:]
        given = split(entering_ref[...])
        for day in range(day_count):
            local_ref, inverse_ref, moved_ref = refs[3 * day : 3 * day + 3]
            current = early_ref[day] if day < early else refs[3 * day_count + day - early][...]
            current = current - dot_parts(given, parts(moved_ref), NT)
            term = dot_parts(split(current), parts(inverse_ref), NN)
            outs[day][...] = local_ref[...] + term[:1]

    terms = call(
        terms_body, [samples_full] * day_count, "mean_terms", (),
        [
            after(mean["entering"], sent_half), early_currents,
            *(
                value for day in range(day_count)
                for value in (local_terms[day], inverses[day], moveds[day])
            ),
            *late_currents,
        ],
        work=4,
    )

    def last_body(where_ref, keep_ref, got_ref, back_ref, high_ref, *refs):
        got_means, refs = refs[: groups - 1], refs[groups - 1 :]
        map_refs, term_refs = refs[:day_count], refs[day_count : 2 * day_count]
        out_ref, held, sems = refs[2 * day_count :]
        first = (where_ref[1] & (PAIR - 1)) == 0
        given = got_means[0][...]
        for ref in got_means[1:]:
            given = given + ref[...]
        between = dot_parts(split(given), parts(high_ref), NN) + back_ref[...]
        given = jnp.where(first, between, given)
        low = jnp.where(first, keep_ref[...], got_ref[...])
        high = jnp.where(first, got_ref[...], keep_ref[...])
        following = jnp.concatenate([low, high], axis=0) + given[:1]
        copies = []
        for day in reversed(range(day_count)):
            following = dot_parts(split(following), parts(map_refs[day]), NN) + term_refs[day][...]
            held[day] = following.T
            copies.append(pltpu.make_async_copy(held.at[day], out_ref.at[day], sems.at[day]))
            copies[-1].start()
        for copy in copies:
            copy.wait()

    return call(
        last_body, shape(day_count, nodes, columns), "last_days", (where,),
        [
            kept_half, got_half, mean["high_back"], high_map, *mean["leaving"], *step_maps,
            *terms,
        ],
        work=4,
        scratch=[
            pltpu.VMEM((day_count, nodes, columns), F32), pltpu.SemaphoreType.DMA((day_count,)),
        ],
        out_specs=pl.BlockSpec(memory_space=pl.ANY),
    )


def solution(mesh):
    return jax.shard_map(
        local,
        mesh=mesh,
        in_specs=(
            P("tm", "row", None),
            P("tm", "row", None),
            P("tm", None, "row"),
            P(("tm", "row")),
            P(("tm", "row")),
            P(("tm", "row")),
        ),
        out_specs=P("tm", None, "row"),
        check_vma=False,
    )
```

```python
import functools

import jax
import jax.numpy as jnp
from jax import lax
from jax.experimental import pallas as pl
from jax.experimental.pallas import tpu as pltpu
from jax.sharding import PartitionSpec as P

F32 = jnp.float32
BF16 = jnp.bfloat16
CORES = 2
PAIR = 2
LINES = 8

NN = ((1,), (0,))
TN = ((0,), (0,))
NT = ((1,), (1,))


def split(value):
    high = value.astype(BF16)
    return high, (value - high.astype(F32)).astype(BF16)


def parts(ref):
    return ref[0], ref[1]


def dot_parts(left, right, dims):
    product = functools.partial(
        lax.dot_general, dimension_numbers=(dims, ((), ())), preferred_element_type=F32
    )
    return product(left[0], right[0]) + (product(left[0], right[1]) + product(left[1], right[0]))


def shape(*dims, dtype=F32):
    return jax.ShapeDtypeStruct(dims, dtype)


def in_vmem(value):
    return pltpu.with_memory_space_constraint(value, pltpu.VMEM)


def call(body, outs, name, scalars, arrays, work=1, scratch=(), out_specs=None):
    vmem = pl.BlockSpec(memory_space=pltpu.VMEM)
    out_shape = outs if out_specs else jax.tree.map(lambda o: pltpu.VMEM(o.shape, o.dtype), outs)
    return pl.pallas_call(
        body,
        out_shape=out_shape,
        in_specs=[vmem] * (len(scalars) + len(arrays)),
        out_specs=out_specs or jax.tree.map(lambda _: vmem, outs),
        scratch_shapes=list(scratch),
        compiler_params=pltpu.CompilerParams(vmem_limit_bytes=12 * 1024 * 1024),
        cost_estimate=pl.CostEstimate(
            flops=int(work * 2.0e8), transcendentals=0, bytes_accessed=1024
        ),
        name=name,
    )(*map(in_vmem, (*scalars, *arrays)))


def deal(where_ref, distance, total, keep_out, sent_out):
    count = total.shape[0] // 2
    upper = (where_ref[1, 0] & distance) != 0
    keep_out[...] = jnp.where(upper, total[count:], total[:count])
    sent_out[...] = jnp.where(upper, total[:count], total[count:])


def halved(where, distance, keep, got):
    def body(where_ref, keep_ref, got_ref, *outs):
        total = keep_ref[...] + got_ref[...]
        if distance:
            deal(where_ref, distance, total, *outs)
        else:
            outs[0][...] = total

    days, nodes = keep.shape
    outs = [shape(days // 2, nodes)] * 2 if distance else [keep]
    outs = [shape(*out.shape) for out in outs]
    return (*call(body, outs, "halved", (where,), [keep, got], work=0.05), None)[:2]


def bin_observations(where, obs_day, obs_node, obs_value, days, nodes, distance):
    chunk = min(512, obs_day.shape[0])
    chunks = obs_day.shape[0] // chunk

    def body(where_ref, day_ref, node_ref, value_ref, keep_out, sent_out):
        total = jnp.zeros((3 * days, nodes), F32)
        for index in range(chunks):
            row = pl.ds(index, 1)
            value = value_ref[row, :]
            high = value.astype(BF16).astype(F32)
            middle = (value - high).astype(BF16).astype(F32)
            low = value - high - middle
            is_day = lax.broadcasted_iota(jnp.int32, (days, chunk), 0) == day_ref[row, :]
            marked = jnp.concatenate(
                [jnp.where(is_day, part, 0.0).astype(BF16) for part in (high, middle, low)], axis=0
            )
            is_node = lax.broadcasted_iota(jnp.int32, (nodes, chunk), 0) == node_ref[row, :]
            total += lax.dot_general(
                marked, is_node.astype(F32).astype(BF16), (NT, ((), ())), preferred_element_type=F32
            )
        total = total[:days] + (total[days : 2 * days] + total[2 * days :])
        deal(where_ref, distance, total, keep_out, sent_out)

    return call(
        body,
        [shape(days // 2, nodes)] * 2,
        "bin_observations",
        (where,),
        [value.reshape(chunks, chunk) for value in (obs_day, obs_node, obs_value)],
        work=2,
    )


def gather_rows(where_ref, refs, take, out_ref):
    share = refs[0].shape[-2]
    for offset, ref in enumerate(refs):
        at = pl.ds(pl.multiple_of((where_ref[0, 0] ^ offset) * share, share), share)
        if len(ref.shape) == 3:
            ref = ref.at[take(offset) if callable(take) else take]
        out_ref[0, at, :], out_ref[1, at, :] = split(ref[...])


def local(inv_diag, coupling, noise, obs_day, obs_node, obs_value):
    part_count = lax.axis_size("tm")
    row_count = lax.axis_size("row")
    my_part = lax.axis_index("tm")
    my_row = lax.axis_index("row")
    day_count, share, nodes = inv_diag.shape
    columns = noise.shape[2]
    half = columns // PAIR
    half_nodes = nodes // CORES
    groups = part_count // PAIR
    chips = row_count // CORES
    early = day_count // 2
    late = day_count - early

    def to_row(value, distance):
        return lax.ppermute(value, "row", [(i, i ^ distance) for i in range(row_count)])

    def to_pair(value):
        return lax.ppermute(value, "tm", [(i, i ^ 1) for i in range(part_count)])

    def to_group(value, source, target):
        return lax.ppermute(
            value, "tm", [(PAIR * source + i, PAIR * target + i) for i in range(PAIR)]
        )

    def after(value, *others):
        return lax.optimization_barrier((value, *others))[0]

    where = jnp.broadcast_to(jnp.stack([my_row, my_part]).astype(jnp.int32)[:, None], (2, 128))

    line = shape(LINES, nodes)
    square = shape(nodes, nodes)
    map_parts = shape(2, nodes, nodes, dtype=BF16)
    samples_half = shape(half, nodes)
    samples_full = shape(columns, nodes)

    keep, sent = bin_observations(
        where, obs_day, obs_node, obs_value, part_count * day_count, nodes, part_count // 2
    )

    def over_chips(rows):
        return [to_row(rows, distance) for distance in range(CORES, row_count, CORES)]

    def shared(arrived, *ahead):
        return [piece for got in arrived for piece in (got, to_row(after(got, *ahead), 1))]

    early_rows = coupling[:early]
    late_rows = [coupling[day : day + 1] for day in range(early, day_count)]
    got_inverses = over_chips(inv_diag)
    got_links = [over_chips(early_rows)]
    for index, rows in enumerate(late_rows[:-1]):
        got_links.append(over_chips(after(rows, *(got_inverses, *got_links)[index])))
    own_inverse = [inv_diag, to_row(inv_diag, 1)]
    own_link = [coupling, to_row(coupling, 1)]
    where = after(where, keep, early_rows, *late_rows)

    distance = part_count // 2
    while distance:
        got = lax.ppermute(sent, "tm", [(i, i ^ distance) for i in range(part_count)])
        distance //= 2
        keep, sent = halved(where, distance, keep, got)
    right_side = keep + to_row(keep, 1)

    def pack_body(rows_ref, source_ref, out_ref):
        out_ref[:share, :] = rows_ref[0]
        out_ref[share:, :] = jnp.zeros((LINES, nodes), F32)
        out_ref[share : share + day_count, :] = source_ref[...]

    packed = call(
        pack_body, shape(share + LINES, nodes), "pack", (), [late_rows[-1], right_side], work=0.1
    )
    got_links.append(over_chips(after(packed, *(got_inverses, *got_links)[late - 1])))

    def store(out_ref, pair):
        out_ref[0], out_ref[1] = pair

    def inverses_body(where_ref, *refs):
        row_refs, noise_ref, gram_out, outs = (
            refs[:row_count], refs[row_count], refs[row_count + 1], refs[row_count + 2 :],
        )
        for day in range(day_count):
            gather_rows(where_ref, row_refs, lambda offset: day, outs[day])
            outs[day_count + day][...] = dot_parts(
                split(noise_ref[day]), parts(outs[day]), TN
            )
        gram_out[...] = dot_parts(parts(outs[0]), parts(outs[0]), TN)

    gram, *results = call(
        inverses_body,
        [square, *[map_parts] * day_count, *[samples_full] * day_count],
        "inverses",
        (where,),
        [*own_inverse, *shared(got_inverses, where, packed), noise],
        work=4,
    )
    inverses, local_terms = results[:day_count], results[day_count:]

    def early_body(where_ref, *refs):
        own_refs, got_refs, refs = refs[:CORES], refs[CORES:row_count], refs[row_count:]
        noise_ref, term_ref, refs = refs[0], refs[1], refs[2:]
        inverse_refs, refs = refs[: early + 1], refs[early + 1 :]
        sum_out, *outs = refs
        link_outs, moved_outs, map_outs = outs[:early], outs[early : 2 * early], outs[2 * early :]
        for day in range(early):
            gather_rows(where_ref, (*own_refs, *got_refs), lambda offset: day, link_outs[day])
        total = term_ref[...]
        moved = parts(inverse_refs[0])
        for day in range(early):
            link = parts(link_outs[day])
            path = split(-dot_parts(link, moved, NN))
            if day == 0:
                store(map_outs[0], path)
            else:
                store(map_outs[day], split(-dot_parts(link, parts(inverse_refs[day]), NN)))
            moved = split(dot_parts(parts(inverse_refs[day + 1]), path, NN))
            store(moved_outs[day], moved)
            total = total + dot_parts(split(noise_ref[day + 1]), moved, TN)
        sum_out[...] = total

    summed, *results = call(
        early_body,
        [samples_full, *[map_parts] * (3 * early)],
        "early_days",
        (where,),
        [*own_link, *shared(got_links[0], gram), noise, local_terms[0], *inverses[: early + 1]],
        work=6,
    )
    links, step_maps = list(results[:early]), list(results[2 * early :])
    moveds = [inverses[0], *results[early : 2 * early]]

    def next_body(day, where_ref, *refs):
        own_refs, got_refs, refs = refs[:CORES], refs[CORES:row_count], refs[row_count:]
        noise_ref, inverse_ref, sum_ref, moved_ref, link_out, moved_out, *sum_outs = refs
        gather_rows(
            where_ref, (*own_refs, *got_refs), lambda offset: day if offset < CORES else 0, link_out
        )
        path = split(-dot_parts(parts(link_out), parts(moved_ref), NN))
        moved = split(dot_parts(parts(inverse_ref), path, NN))
        store(moved_out, moved)
        total = sum_ref[...] + dot_parts(split(noise_ref[day + 1]), moved, TN)
        if len(sum_outs) == 1:
            sum_outs[0][...] = total
        else:
            first = (where_ref[1, 0] & (PAIR - 1)) == 0
            sum_outs[0][...] = jnp.where(first, total[:half], total[half:])
            sum_outs[1][...] = jnp.where(first, total[half:], total[:half])

    for day in range(early, day_count - 1):
        sums = [samples_half] * 2 if day == day_count - 2 else [samples_full]
        link, moved, *sums = call(
            functools.partial(next_body, day),
            [map_parts, map_parts, *sums],
            f"day_{day}",
            (where,),
            [
                *own_link, *shared(got_links[1 + day - early], summed), noise, inverses[day + 1],
                summed, moveds[day],
            ],
            work=3,
        )
        summed = sums[0]
        moveds.append(moved)
        links.append(link)
    keep, send = sums
    other_sum = to_pair(send)

    def last_link_body(where_ref, *refs):
        own_refs, got_refs, refs = refs[:CORES], refs[CORES:row_count], refs[row_count:]
        moved_ref, whole_out, half_out, link_out = refs
        gather_rows(
            where_ref,
            (*own_refs, *(ref.at[pl.ds(0, share)] for ref in got_refs)),
            lambda offset: day_count - 1,
            link_out,
        )
        whole_out[...] = -dot_parts(parts(link_out), parts(moved_ref), NN)
        half_out[...] = whole_out[
            pl.ds(pl.multiple_of((where_ref[0, 0] & (CORES - 1)) * half_nodes, half_nodes), half_nodes), :
        ]

    path, path_half, link = call(
        last_link_body,
        (square, shape(half_nodes, nodes), map_parts),
        "last_link",
        (where,),
        [*own_link, *shared(got_links[-1], send), moveds[-1]],
        work=1.5,
    )
    links.append(link)
    other_half = to_pair(after(path_half, other_sum))

    def lines_body(source_ref, *refs):
        got_refs, refs = refs[: chips - 1], refs[chips - 1 :]
        flux_out, back_out, current_out = refs[-3:]
        source = source_ref[...]
        for ref in got_refs:
            source = source + ref[share : share + day_count, :]
        applied = jnp.zeros((LINES, nodes), F32)
        back = applied
        for day in range(day_count):
            inverse_ref, link_ref, moved_ref = refs[3 * day : 3 * day + 3]
            wanted = source[day : day + 1] - applied
            current = dot_parts(split(wanted), parts(inverse_ref), NT)
            current_out[day] = current
            current = split(current)
            applied = dot_parts(current, parts(link_ref), NT)
            back = back + dot_parts(current, parts(moved_ref), NN)
        flux_out[...] = applied
        back_out[...] = back

    flux, back, currents = call(
        lines_body,
        (line, line, shape(day_count, LINES, nodes)),
        "lines",
        (),
        [
            right_side,
            *got_links[-1],
            *(
                ref for day in range(day_count)
                for ref in (inverses[day], links[day], moveds[day])
            ),
        ],
        work=5,
    )
    other_flux = to_pair(flux)

    def grams_body(gram_ref, *refs):
        total = gram_ref[...]
        for ref in refs[:-1]:
            total = total + dot_parts(parts(ref), parts(ref), TN)
        store(refs[-1], split(total))

    gram = call(grams_body, map_parts, "grams", (), [after(gram, flux), *moveds[1:]], work=3)

    def late_maps_body(*refs):
        for index in range(late):
            store(
                refs[2 * late + index],
                split(-dot_parts(parts(refs[late + index]), parts(refs[index]), NN)),
            )

    step_maps += call(
        late_maps_body,
        [map_parts] * late,
        "late_maps",
        (),
        [after(inverses[early], gram), *inverses[early + 1 :], *links[early:]],
        work=late,
    )

    other_rest = to_row(after(other_half, other_flux, *step_maps), 1)

    def pair_body(
        where_ref, path_ref, half_ref, rest_ref, sum_ref, other_ref, flux_ref, other_flux_ref,
        low_out, high_out, sum_out, high_sum_out, flux_out, low_flux_out,
    ):
        first = (where_ref[1, 0] & (PAIR - 1)) == 0
        lead = (where_ref[0, 0] & (CORES - 1)) == 0
        half_rows, rest_rows = half_ref[...], rest_ref[...]
        for at, rows in (
            (slice(0, half_nodes), jnp.where(lead, half_rows, rest_rows)),
            (slice(half_nodes, nodes), jnp.where(lead, rest_rows, half_rows)),
        ):
            own = path_ref[at, :]
            low_out[0, at, :], low_out[1, at, :] = split(jnp.where(first, own, rows))
            high_out[0, at, :], high_out[1, at, :] = split(jnp.where(first, rows, own))
        low_sum = jnp.where(first, sum_ref[...], other_ref[...])
        high_sum = jnp.where(first, other_ref[...], sum_ref[...])
        low_flux = jnp.where(first, flux_ref[...], other_flux_ref[...])
        high_flux = jnp.where(first, other_flux_ref[...], flux_ref[...])
        flux_out[...] = dot_parts(split(low_flux), parts(high_out), NT) + high_flux
        low_flux_out[...] = low_flux
        sum_out[...] = dot_parts(split(high_sum), parts(low_out), NN) + low_sum
        high_sum_out[...] = high_sum

    low_map, high_map, pair_sum, high_sum, pair_flux, low_flux = call(
        pair_body,
        (map_parts, map_parts, samples_half, samples_half, line, line),
        "pair_maps",
        (where,),
        [path, other_half, other_rest, keep, other_sum, flux, other_flux],
        work=1.5,
    )

    def group_map_body(low_ref, high_ref, out_ref):
        store(out_ref, split(dot_parts(parts(high_ref), parts(low_ref), NN)))

    group_map = call(
        group_map_body, map_parts, "group_map", (), [low_map, after(high_map, pair_sum)]
    )

    def link_body(dims, map_ref, local_ref, *refs):
        got = refs[0][...]
        for ref in refs[1:-1]:
            got = got + ref[...]
        refs[-1][...] = dot_parts(split(got), parts(map_ref), dims) + local_ref[...]

    def linked(dims, value_map, value, got, name):
        return call(
            functools.partial(link_body, dims), shape(*value.shape), name, (),
            [value_map, value, *got], work=0.6,
        )

    def added(refs):
        total = refs[0][...]
        for ref in refs[1:]:
            total = total + ref[...]
        return total

    def turn_body(where_ref, low_ref, flux_ref, gram_ref, back_ref, *refs):
        own_out, back_out, part_out = refs[-3:]
        given = added(refs[:-3])
        behind = dot_parts(split(given), parts(low_ref), NT) + flux_ref[...]
        first = (where_ref[1, 0] & (PAIR - 1)) == 0
        given = jnp.where(first, given, behind)
        own_out[...] = given
        own_back = back_ref[...] - dot_parts(split(given), parts(gram_ref), NN)
        back_out[...] = own_back
        part_out[...] = jnp.where(first, own_back, dot_parts(split(own_back), parts(low_ref), NN))

    def first_back_body(where_ref, map_ref, own_ref, other_ref, part_ref, mate_ref, *refs):
        value_out, pair_out, high_out = refs[-3:]
        first = (where_ref[1, 0] & (PAIR - 1)) == 0
        pair_back = part_ref[...] + mate_ref[...]
        pair_out[...] = pair_back
        high_out[...] = jnp.where(first, other_ref[...], own_ref[...])
        value_out[...] = dot_parts(split(added(refs[:-3])), parts(map_ref), NN) + pair_back

    mean = {}

    def mean_hops():
        value, got = pair_flux, []
        yield value
        for group in range(groups - 1):
            got.append(to_group(value, group, group + 1))
            if group < groups - 2:
                value = linked(NT, group_map, pair_flux, got, "forward_link")
                yield value
        mean["entering"], own_back, part = call(
            turn_body, (line, line, line), "mean_turn", (where,),
            [low_map, low_flux, gram, back, *got],
        )
        yield part
        last = PAIR * (groups - 1)
        got = [
            lax.ppermute(part, "tm", [(last + i, last - PAIR + (i ^ cross)) for i in range(PAIR)])
            for cross in range(PAIR)
        ]
        both = to_pair(jnp.concatenate([own_back, part], axis=0))
        value, pair_back, mean["high_back"] = call(
            first_back_body, (line, line, line), "first_back", (where,),
            [group_map, own_back, both[:LINES], part, both[LINES:], *got], work=0.6,
        )
        mean["leaving"] = got
        for group in range(groups - 2, 0, -1):
            yield value
            got.append(to_group(value, group, group - 1))
            if group > 1:
                value = linked(NN, group_map, pair_back, got, "backward_link")
        yield got[-1]

    hops = mean_hops()
    ahead = next(hops)

    leaving = []
    value = pair_sum
    for group in range(groups - 1, 0, -1):
        got = to_group(after(value, ahead), group, group - 1)
        next(hops)
        ahead = next(hops, ahead)
        leaving.append(after(got, ahead))
        if group > 1:
            value = linked(NN, group_map, pair_sum, leaving, "noise_link")
    for ahead in hops:
        pass

    def divide_body(where_ref, map_ref, sum_ref, *refs):
        keep_out, send_out = refs[-2:]
        given = refs[0][...]
        for ref in refs[1:-2]:
            given = given + ref[...]
        between = dot_parts(split(given), parts(map_ref), NN) + sum_ref[...]
        first = (where_ref[1, 0] & (PAIR - 1)) == 0
        keep_out[...] = jnp.where(first, between, given)
        send_out[...] = jnp.where(first, given, between)

    kept_half, sent_half = call(
        divide_body, (samples_half, samples_half), "divide", (where,),
        [high_map, high_sum, *leaving],
    )
    got_half = to_pair(sent_half)

    def terms_body(entering_ref, current_ref, *refs):
        outs = refs[-day_count:]
        given = split(entering_ref[...])
        for day in range(day_count):
            local_ref, inverse_ref, moved_ref = refs[3 * day : 3 * day + 3]
            current = current_ref[day] - dot_parts(given, parts(moved_ref), NT)
            term = dot_parts(split(current), parts(inverse_ref), NN)
            outs[day][...] = local_ref[...] + term[:1]

    terms = call(
        terms_body, [samples_full] * day_count, "mean_terms", (),
        [
            after(mean["entering"], sent_half), currents,
            *(
                value for day in range(day_count)
                for value in (local_terms[day], inverses[day], moveds[day])
            ),
        ],
        work=4,
    )

    def last_body(where_ref, keep_ref, got_ref, back_ref, high_ref, *refs):
        count = len(mean["leaving"])
        got_means, refs = refs[:count], refs[count:]
        map_refs, term_refs = refs[:day_count], refs[day_count : 2 * day_count]
        out_ref, held, sems = refs[2 * day_count :]
        first = (where_ref[1, 0] & (PAIR - 1)) == 0
        given = got_means[0][...]
        for ref in got_means[1:]:
            given = given + ref[...]
        between = dot_parts(split(given), parts(high_ref), NN) + back_ref[...]
        given = jnp.where(first, between, given)
        low = jnp.where(first, keep_ref[...], got_ref[...])
        high = jnp.where(first, got_ref[...], keep_ref[...])
        following = jnp.concatenate([low, high], axis=0) + given[:1]
        copies = []
        for day in reversed(range(day_count)):
            following = dot_parts(split(following), parts(map_refs[day]), NN) + term_refs[day][...]
            held[day] = following.T
            copies.append(pltpu.make_async_copy(held.at[day], out_ref.at[day], sems.at[day]))
            copies[-1].start()
        for copy in copies:
            copy.wait()

    return call(
        last_body, shape(day_count, nodes, columns), "last_days", (where,),
        [
            kept_half, got_half, mean["high_back"], high_map, *mean["leaving"], *step_maps,
            *terms,
        ],
        work=4,
        scratch=[
            pltpu.VMEM((day_count, nodes, columns), F32), pltpu.SemaphoreType.DMA((day_count,)),
        ],
        out_specs=pl.BlockSpec(memory_space=pl.ANY),
    )


def solution(mesh):
    return jax.shard_map(
        local,
        mesh=mesh,
        in_specs=(
            P("tm", "row", None),
            P("tm", "row", None),
            P("tm", None, "row"),
            P(("tm", "row")),
            P(("tm", "row")),
            P(("tm", "row")),
        ),
        out_specs=P("tm", None, "row"),
        check_vma=False,
    )
```

```python
import functools

import jax
import jax.numpy as jnp
from jax import lax
from jax.experimental import pallas as pl
from jax.experimental.pallas import tpu as pltpu
from jax.sharding import PartitionSpec as P

F32 = jnp.float32
BF16 = jnp.bfloat16
CORES = 2
PAIR = 2
LINES = 8

NN = ((1,), (0,))
TN = ((0,), (0,))
NT = ((1,), (1,))


def split(value):
    high = value.astype(BF16)
    return high, (value - high.astype(F32)).astype(BF16)


def parts(ref):
    return ref[0], ref[1]


def dot_parts(left, right, dims):
    product = functools.partial(
        lax.dot_general, dimension_numbers=(dims, ((), ())), preferred_element_type=F32
    )
    return product(left[0], right[0]) + (product(left[0], right[1]) + product(left[1], right[0]))


def shape(*dims, dtype=F32):
    return jax.ShapeDtypeStruct(dims, dtype)


def in_vmem(value):
    return pltpu.with_memory_space_constraint(value, pltpu.VMEM)


def call(body, outs, name, scalars, arrays, work=1, scratch=(), out_specs=None):
    vmem = pl.BlockSpec(memory_space=pltpu.VMEM)
    out_shape = outs if out_specs else jax.tree.map(lambda o: pltpu.VMEM(o.shape, o.dtype), outs)
    return pl.pallas_call(
        body,
        out_shape=out_shape,
        in_specs=[vmem] * (len(scalars) + len(arrays)),
        out_specs=out_specs or jax.tree.map(lambda _: vmem, outs),
        scratch_shapes=list(scratch),
        compiler_params=pltpu.CompilerParams(vmem_limit_bytes=12 * 1024 * 1024),
        cost_estimate=pl.CostEstimate(
            flops=int(work * 2.0e8), transcendentals=0, bytes_accessed=1024
        ),
        name=name,
    )(*map(in_vmem, (*scalars, *arrays)))


def deal(where_ref, distance, total, keep_out, sent_out):
    count = total.shape[0] // 2
    upper = (where_ref[1, 0] & distance) != 0
    keep_out[...] = jnp.where(upper, total[count:], total[:count])
    sent_out[...] = jnp.where(upper, total[:count], total[count:])


def halved(where, distance, keep, got):
    def body(where_ref, keep_ref, got_ref, *outs):
        total = keep_ref[...] + got_ref[...]
        if distance:
            deal(where_ref, distance, total, *outs)
        else:
            outs[0][...] = total

    days, nodes = keep.shape
    outs = [shape(days // 2, nodes)] * 2 if distance else [keep]
    outs = [shape(*out.shape) for out in outs]
    return (*call(body, outs, "halved", (where,), [keep, got], work=0.05), None)[:2]


def bin_observations(where, obs_day, obs_node, obs_value, days, nodes, distance):
    chunk = min(512, obs_day.shape[0])
    chunks = obs_day.shape[0] // chunk

    def body(where_ref, day_ref, node_ref, value_ref, keep_out, sent_out):
        total = jnp.zeros((3 * days, nodes), F32)
        for index in range(chunks):
            row = pl.ds(index, 1)
            value = value_ref[row, :]
            high = value.astype(BF16).astype(F32)
            middle = (value - high).astype(BF16).astype(F32)
            low = value - high - middle
            is_day = lax.broadcasted_iota(jnp.int32, (days, chunk), 0) == day_ref[row, :]
            marked = jnp.concatenate(
                [jnp.where(is_day, part, 0.0).astype(BF16) for part in (high, middle, low)], axis=0
            )
            is_node = lax.broadcasted_iota(jnp.int32, (nodes, chunk), 0) == node_ref[row, :]
            total += lax.dot_general(
                marked, is_node.astype(F32).astype(BF16), (NT, ((), ())), preferred_element_type=F32
            )
        total = total[:days] + (total[days : 2 * days] + total[2 * days :])
        deal(where_ref, distance, total, keep_out, sent_out)

    return call(
        body,
        [shape(days // 2, nodes)] * 2,
        "bin_observations",
        (where,),
        [value.reshape(chunks, chunk) for value in (obs_day, obs_node, obs_value)],
        work=2,
    )


def gather_rows(where_ref, refs, take, out_ref):
    share = refs[0].shape[-2]
    for offset, ref in enumerate(refs):
        at = pl.ds(pl.multiple_of((where_ref[0, 0] ^ offset) * share, share), share)
        if len(ref.shape) == 3:
            ref = ref.at[take(offset) if callable(take) else take]
        out_ref[0, at, :], out_ref[1, at, :] = split(ref[...])


def local(inv_diag, coupling, noise, obs_day, obs_node, obs_value):
    part_count = lax.axis_size("tm")
    row_count = lax.axis_size("row")
    my_part = lax.axis_index("tm")
    my_row = lax.axis_index("row")
    day_count, share, nodes = inv_diag.shape
    columns = noise.shape[2]
    half = columns // PAIR
    half_nodes = nodes // CORES
    groups = part_count // PAIR
    chips = row_count // CORES
    early = day_count // 2
    late = day_count - early

    def to_row(value, distance):
        return lax.ppermute(value, "row", [(i, i ^ distance) for i in range(row_count)])

    def to_pair(value):
        return lax.ppermute(value, "tm", [(i, i ^ 1) for i in range(part_count)])

    def to_group(value, source, target):
        return lax.ppermute(
            value, "tm", [(PAIR * source + i, PAIR * target + i) for i in range(PAIR)]
        )

    def after(value, *others):
        return lax.optimization_barrier((value, *others))[0]

    where = jnp.broadcast_to(jnp.stack([my_row, my_part]).astype(jnp.int32)[:, None], (2, 128))

    line = shape(LINES, nodes)
    square = shape(nodes, nodes)
    map_parts = shape(2, nodes, nodes, dtype=BF16)
    samples_half = shape(half, nodes)
    samples_full = shape(columns, nodes)

    keep, sent = bin_observations(
        where, obs_day, obs_node, obs_value, part_count * day_count, nodes, part_count // 2
    )

    def over_chips(rows):
        return [to_row(rows, distance) for distance in range(CORES, row_count, CORES)]

    def shared(arrived, *ahead):
        return [piece for got in arrived for piece in (got, to_row(after(got, *ahead), 1))]

    early_rows = coupling[:early]
    late_rows = [coupling[day : day + 1] for day in range(early, day_count)]
    got_inverses = over_chips(inv_diag)
    got_links = [over_chips(early_rows)]
    for index, rows in enumerate(late_rows[:-1]):
        got_links.append(over_chips(after(rows, *(got_inverses, *got_links)[index])))
    own_inverse = [inv_diag, to_row(inv_diag, 1)]
    own_link = [coupling, to_row(coupling, 1)]
    where = after(where, keep, early_rows, *late_rows)

    distance = part_count // 2
    while distance:
        got = lax.ppermute(sent, "tm", [(i, i ^ distance) for i in range(part_count)])
        distance //= 2
        keep, sent = halved(where, distance, keep, got)
    right_side = keep + to_row(keep, 1)

    def pack_body(rows_ref, source_ref, out_ref):
        out_ref[:share, :] = rows_ref[0]
        out_ref[share:, :] = jnp.zeros((LINES, nodes), F32)
        out_ref[share : share + day_count, :] = source_ref[...]

    packed = call(
        pack_body, shape(share + LINES, nodes), "pack", (), [late_rows[-1], right_side], work=0.1
    )
    got_links.append(over_chips(after(packed, *(got_inverses, *got_links)[late - 1])))

    def store(out_ref, pair):
        out_ref[0], out_ref[1] = pair

    def inverses_body(where_ref, *refs):
        row_refs, noise_ref, gram_out, outs = (
            refs[:row_count], refs[row_count], refs[row_count + 1], refs[row_count + 2 :],
        )
        for day in range(day_count):
            gather_rows(where_ref, row_refs, lambda offset: day, outs[day])
            outs[day_count + day][...] = dot_parts(
                split(noise_ref[day]), parts(outs[day]), TN
            )
        gram_out[...] = dot_parts(parts(outs[0]), parts(outs[0]), TN)

    gram, *results = call(
        inverses_body,
        [square, *[map_parts] * day_count, *[samples_full] * day_count],
        "inverses",
        (where,),
        [*own_inverse, *shared(got_inverses, where, packed), noise],
        work=4,
    )
    inverses, local_terms = results[:day_count], results[day_count:]

    def early_body(where_ref, *refs):
        own_refs, got_refs, refs = refs[:CORES], refs[CORES:row_count], refs[row_count:]
        noise_ref, term_ref, refs = refs[0], refs[1], refs[2:]
        inverse_refs, refs = refs[: early + 1], refs[early + 1 :]
        sum_out, *outs = refs
        link_outs, moved_outs, map_outs = outs[:early], outs[early : 2 * early], outs[2 * early :]
        for day in range(early):
            gather_rows(where_ref, (*own_refs, *got_refs), lambda offset: day, link_outs[day])
        total = term_ref[...]
        moved = parts(inverse_refs[0])
        for day in range(early):
            link = parts(link_outs[day])
            path = split(-dot_parts(link, moved, NN))
            if day == 0:
                store(map_outs[0], path)
            else:
                store(map_outs[day], split(-dot_parts(link, parts(inverse_refs[day]), NN)))
            moved = split(dot_parts(parts(inverse_refs[day + 1]), path, NN))
            store(moved_outs[day], moved)
            total = total + dot_parts(split(noise_ref[day + 1]), moved, TN)
        sum_out[...] = total

    summed, *results = call(
        early_body,
        [samples_full, *[map_parts] * (3 * early)],
        "early_days",
        (where,),
        [*own_link, *shared(got_links[0], gram), noise, local_terms[0], *inverses[: early + 1]],
        work=6,
    )
    links, step_maps = list(results[:early]), list(results[2 * early :])
    moveds = [inverses[0], *results[early : 2 * early]]

    def next_body(day, where_ref, *refs):
        own_refs, got_refs, refs = refs[:CORES], refs[CORES:row_count], refs[row_count:]
        noise_ref, inverse_ref, sum_ref, moved_ref, link_out, moved_out, *sum_outs = refs
        gather_rows(
            where_ref, (*own_refs, *got_refs), lambda offset: day if offset < CORES else 0, link_out
        )
        path = split(-dot_parts(parts(link_out), parts(moved_ref), NN))
        moved = split(dot_parts(parts(inverse_ref), path, NN))
        store(moved_out, moved)
        total = sum_ref[...] + dot_parts(split(noise_ref[day + 1]), moved, TN)
        if len(sum_outs) == 1:
            sum_outs[0][...] = total
        else:
            first = (where_ref[1, 0] & (PAIR - 1)) == 0
            sum_outs[0][...] = jnp.where(first, total[:half], total[half:])
            sum_outs[1][...] = jnp.where(first, total[half:], total[:half])

    for day in range(early, day_count - 1):
        sums = [samples_half] * 2 if day == day_count - 2 else [samples_full]
        link, moved, *sums = call(
            functools.partial(next_body, day),
            [map_parts, map_parts, *sums],
            f"day_{day}",
            (where,),
            [
                *own_link, *shared(got_links[1 + day - early], summed), noise, inverses[day + 1],
                summed, moveds[day],
            ],
            work=3,
        )
        summed = sums[0]
        moveds.append(moved)
        links.append(link)
    keep, send = sums
    other_sum = to_pair(send)

    def last_link_body(where_ref, *refs):
        own_refs, got_refs, refs = refs[:CORES], refs[CORES:row_count], refs[row_count:]
        moved_ref, whole_out, half_out, link_out = refs
        gather_rows(
            where_ref,
            (*own_refs, *(ref.at[pl.ds(0, share)] for ref in got_refs)),
            lambda offset: day_count - 1,
            link_out,
        )
        whole_out[...] = -dot_parts(parts(link_out), parts(moved_ref), NN)
        half_out[...] = whole_out[
            pl.ds(pl.multiple_of((where_ref[0, 0] & (CORES - 1)) * half_nodes, half_nodes), half_nodes), :
        ]

    path, path_half, link = call(
        last_link_body,
        (square, shape(half_nodes, nodes), map_parts),
        "last_link",
        (where,),
        [*own_link, *shared(got_links[-1], send), moveds[-1]],
        work=1.5,
    )
    links.append(link)
    other_half = to_pair(after(path_half, other_sum))

    def lines_body(source_ref, *refs):
        got_refs, refs = refs[: chips - 1], refs[chips - 1 :]
        flux_out, back_out, current_out = refs[-3:]
        source = source_ref[...]
        for ref in got_refs:
            source = source + ref[share : share + day_count, :]
        applied = jnp.zeros((LINES, nodes), F32)
        back = applied
        for day in range(day_count):
            inverse_ref, link_ref, moved_ref = refs[3 * day : 3 * day + 3]
            wanted = source[day : day + 1] - applied
            current = dot_parts(split(wanted), parts(inverse_ref), NT)
            current_out[day] = current
            current = split(current)
            applied = dot_parts(current, parts(link_ref), NT)
            back = back + dot_parts(current, parts(moved_ref), NN)
        flux_out[...] = applied
        back_out[...] = back

    flux, back, currents = call(
        lines_body,
        (line, line, shape(day_count, LINES, nodes)),
        "lines",
        (),
        [
            right_side,
            *got_links[-1],
            *(
                ref for day in range(day_count)
                for ref in (inverses[day], links[day], moveds[day])
            ),
        ],
        work=5,
    )
    other_flux = to_pair(flux)

    def grams_body(gram_ref, *refs):
        total = gram_ref[...]
        for ref in refs[:-1]:
            total = total + dot_parts(parts(ref), parts(ref), TN)
        store(refs[-1], split(total))

    gram = call(grams_body, map_parts, "grams", (), [after(gram, flux), *moveds[1:]], work=3)

    def late_maps_body(*refs):
        for index in range(late):
            store(
                refs[2 * late + index],
                split(-dot_parts(parts(refs[late + index]), parts(refs[index]), NN)),
            )

    step_maps += call(
        late_maps_body,
        [map_parts] * late,
        "late_maps",
        (),
        [after(inverses[early], gram), *inverses[early + 1 :], *links[early:]],
        work=late,
    )

    other_rest = to_row(after(other_half, other_flux, *step_maps), 1)

    def pair_body(
        where_ref, path_ref, half_ref, rest_ref, sum_ref, other_ref, flux_ref, other_flux_ref,
        low_out, high_out, sum_out, high_sum_out, flux_out, low_flux_out,
    ):
        first = (where_ref[1, 0] & (PAIR - 1)) == 0
        lead = (where_ref[0, 0] & (CORES - 1)) == 0
        half_rows, rest_rows = half_ref[...], rest_ref[...]
        for at, rows in (
            (slice(0, half_nodes), jnp.where(lead, half_rows, rest_rows)),
            (slice(half_nodes, nodes), jnp.where(lead, rest_rows, half_rows)),
        ):
            own = path_ref[at, :]
            low_out[0, at, :], low_out[1, at, :] = split(jnp.where(first, own, rows))
            high_out[0, at, :], high_out[1, at, :] = split(jnp.where(first, rows, own))
        low_sum = jnp.where(first, sum_ref[...], other_ref[...])
        high_sum = jnp.where(first, other_ref[...], sum_ref[...])
        low_flux = jnp.where(first, flux_ref[...], other_flux_ref[...])
        high_flux = jnp.where(first, other_flux_ref[...], flux_ref[...])
        flux_out[...] = dot_parts(split(low_flux), parts(high_out), NT) + high_flux
        low_flux_out[...] = low_flux
        sum_out[...] = dot_parts(split(high_sum), parts(low_out), NN) + low_sum
        high_sum_out[...] = high_sum

    low_map, high_map, pair_sum, high_sum, pair_flux, low_flux = call(
        pair_body,
        (map_parts, map_parts, samples_half, samples_half, line, line),
        "pair_maps",
        (where,),
        [path, other_half, other_rest, keep, other_sum, flux, other_flux],
        work=1.5,
    )

    def group_map_body(low_ref, high_ref, out_ref):
        store(out_ref, split(dot_parts(parts(high_ref), parts(low_ref), NN)))

    group_map = call(
        group_map_body, map_parts, "group_map", (), [low_map, after(high_map, pair_sum)]
    )

    def link_body(dims, map_ref, local_ref, *refs):
        got = refs[0][...]
        for ref in refs[1:-1]:
            got = got + ref[...]
        refs[-1][...] = dot_parts(split(got), parts(map_ref), dims) + local_ref[...]

    def linked(dims, value_map, value, got, name):
        return call(
            functools.partial(link_body, dims), shape(*value.shape), name, (),
            [value_map, value, *got], work=0.6,
        )

    def added(refs):
        total = refs[0][...]
        for ref in refs[1:]:
            total = total + ref[...]
        return total

    def turn_body(where_ref, low_ref, flux_ref, gram_ref, back_ref, *refs):
        own_out, back_out, part_out = refs[-3:]
        given = added(refs[:-3])
        behind = dot_parts(split(given), parts(low_ref), NT) + flux_ref[...]
        first = (where_ref[1, 0] & (PAIR - 1)) == 0
        given = jnp.where(first, given, behind)
        own_out[...] = given
        own_back = back_ref[...] - dot_parts(split(given), parts(gram_ref), NN)
        back_out[...] = own_back
        part_out[...] = jnp.where(first, own_back, dot_parts(split(own_back), parts(low_ref), NN))

    def first_back_body(where_ref, map_ref, own_ref, other_ref, part_ref, mate_ref, *refs):
        value_out, pair_out, high_out = refs[-3:]
        first = (where_ref[1, 0] & (PAIR - 1)) == 0
        pair_back = part_ref[...] + mate_ref[...]
        pair_out[...] = pair_back
        high_out[...] = jnp.where(first, other_ref[...], own_ref[...])
        value_out[...] = dot_parts(split(added(refs[:-3])), parts(map_ref), NN) + pair_back

    mean = {}
    noise_step = []

    def mean_hops():
        value, got = pair_flux, []
        yield value
        for group in range(groups - 1):
            got.append(to_group(value, group, group + 1))
            if group < groups - 2:
                value = linked(NT, group_map, pair_flux, got, "forward_link")
                yield value
        mean["entering"], own_back, part = call(
            turn_body, (line, line, line), "mean_turn", (where,),
            [low_map, low_flux, gram, back, after(got[0], *noise_step), *got[1:]],
        )
        yield part
        last = PAIR * (groups - 1)
        got = [
            lax.ppermute(part, "tm", [(last + i, last - PAIR + (i ^ cross)) for i in range(PAIR)])
            for cross in range(PAIR)
        ]
        both = to_pair(jnp.concatenate([own_back, part], axis=0))
        value, pair_back, mean["high_back"] = call(
            first_back_body, (line, line, line), "first_back", (where,),
            [group_map, own_back, both[:LINES], part, both[LINES:], *got], work=0.6,
        )
        mean["leaving"] = got
        for group in range(groups - 2, 0, -1):
            yield value
            got.append(to_group(value, group, group - 1))
            if group > 1:
                gated = [after(got[0], *noise_step), *got[1:]]
                value = linked(NN, group_map, pair_back, gated, "backward_link")
        yield value

    hops = mean_hops()
    ahead = next(hops)

    leaving = []
    value = pair_sum
    for group in range(groups - 1, 0, -1):
        got = to_group(after(value, ahead), group, group - 1)
        ahead = next(hops)
        if group > 1:
            ahead = next(hops)
        leaving.append(after(got, ahead))
        if group > 1:
            value = linked(NN, group_map, pair_sum, leaving, "noise_link")
            noise_step[:] = [value]
    for _ in hops:
        pass

    def divide_body(where_ref, map_ref, sum_ref, *refs):
        keep_out, send_out = refs[-2:]
        given = refs[0][...]
        for ref in refs[1:-2]:
            given = given + ref[...]
        between = dot_parts(split(given), parts(map_ref), NN) + sum_ref[...]
        first = (where_ref[1, 0] & (PAIR - 1)) == 0
        keep_out[...] = jnp.where(first, between, given)
        send_out[...] = jnp.where(first, given, between)

    kept_half, sent_half = call(
        divide_body, (samples_half, samples_half), "divide", (where,),
        [high_map, high_sum, *leaving],
    )
    got_half = to_pair(sent_half)

    def terms_body(entering_ref, current_ref, *refs):
        outs = refs[-day_count:]
        given = split(entering_ref[...])
        for day in range(day_count):
            local_ref, inverse_ref, moved_ref = refs[3 * day : 3 * day + 3]
            current = current_ref[day] - dot_parts(given, parts(moved_ref), NT)
            term = dot_parts(split(current), parts(inverse_ref), NN)
            outs[day][...] = local_ref[...] + term[:1]

    terms = call(
        terms_body, [samples_full] * day_count, "mean_terms", (),
        [
            after(mean["entering"], sent_half), currents,
            *(
                value for day in range(day_count)
                for value in (local_terms[day], inverses[day], moveds[day])
            ),
        ],
        work=4,
    )

    def last_body(where_ref, keep_ref, got_ref, back_ref, high_ref, *refs):
        count = len(mean["leaving"])
        got_means, refs = refs[:count], refs[count:]
        map_refs, term_refs = refs[:day_count], refs[day_count : 2 * day_count]
        out_ref, held, sems = refs[2 * day_count :]
        first = (where_ref[1, 0] & (PAIR - 1)) == 0
        given = got_means[0][...]
        for ref in got_means[1:]:
            given = given + ref[...]
        between = dot_parts(split(given), parts(high_ref), NN) + back_ref[...]
        given = jnp.where(first, between, given)
        low = jnp.where(first, keep_ref[...], got_ref[...])
        high = jnp.where(first, got_ref[...], keep_ref[...])
        following = jnp.concatenate([low, high], axis=0) + given[:1]
        copies = []
        for day in reversed(range(day_count)):
            following = dot_parts(split(following), parts(map_refs[day]), NN) + term_refs[day][...]
            held[day] = following.T
            copies.append(pltpu.make_async_copy(held.at[day], out_ref.at[day], sems.at[day]))
            copies[-1].start()
        for copy in copies:
            copy.wait()

    return call(
        last_body, shape(day_count, nodes, columns), "last_days", (where,),
        [
            kept_half, got_half, mean["high_back"], high_map, *mean["leaving"], *step_maps,
            *terms,
        ],
        work=4,
        scratch=[
            pltpu.VMEM((day_count, nodes, columns), F32), pltpu.SemaphoreType.DMA((day_count,)),
        ],
        out_specs=pl.BlockSpec(memory_space=pl.ANY),
    )


def solution(mesh):
    return jax.shard_map(
        local,
        mesh=mesh,
        in_specs=(
            P("tm", "row", None),
            P("tm", "row", None),
            P("tm", None, "row"),
            P(("tm", "row")),
            P(("tm", "row")),
            P(("tm", "row")),
        ),
        out_specs=P("tm", None, "row"),
        check_vma=False,
    )
```

```python
import functools

import jax
import jax.numpy as jnp
from jax import lax
from jax.experimental import pallas as pl
from jax.experimental.pallas import tpu as pltpu
from jax.sharding import PartitionSpec as P

F32 = jnp.float32
BF16 = jnp.bfloat16
CORES = 2
PAIR = 2
LINES = 8

NN = ((1,), (0,))
TN = ((0,), (0,))
NT = ((1,), (1,))


def split(value):
    high = value.astype(BF16)
    return high, (value - high.astype(F32)).astype(BF16)


def parts(ref):
    return ref[0], ref[1]


def dot_parts(left, right, dims):
    product = functools.partial(
        lax.dot_general, dimension_numbers=(dims, ((), ())), preferred_element_type=F32
    )
    return product(left[0], right[0]) + (product(left[0], right[1]) + product(left[1], right[0]))


def shape(*dims, dtype=F32):
    return jax.ShapeDtypeStruct(dims, dtype)


def in_vmem(value):
    return pltpu.with_memory_space_constraint(value, pltpu.VMEM)


def call(body, outs, name, scalars, arrays, work=1, scratch=(), out_specs=None):
    vmem = pl.BlockSpec(memory_space=pltpu.VMEM)
    out_shape = outs if out_specs else jax.tree.map(lambda o: pltpu.VMEM(o.shape, o.dtype), outs)
    return pl.pallas_call(
        body,
        out_shape=out_shape,
        in_specs=[vmem] * (len(scalars) + len(arrays)),
        out_specs=out_specs or jax.tree.map(lambda _: vmem, outs),
        scratch_shapes=list(scratch),
        compiler_params=pltpu.CompilerParams(vmem_limit_bytes=12 * 1024 * 1024),
        cost_estimate=pl.CostEstimate(
            flops=int(work * 2.0e8), transcendentals=0, bytes_accessed=1024
        ),
        name=name,
    )(*map(in_vmem, (*scalars, *arrays)))


def deal(where_ref, distance, total, keep_out, sent_out):
    count = total.shape[0] // 2
    upper = (where_ref[1, 0] & distance) != 0
    keep_out[...] = jnp.where(upper, total[count:], total[:count])
    sent_out[...] = jnp.where(upper, total[:count], total[count:])


def halved(where, distance, keep, got):
    def body(where_ref, keep_ref, got_ref, *outs):
        total = keep_ref[...] + got_ref[...]
        if distance:
            deal(where_ref, distance, total, *outs)
        else:
            outs[0][...] = total

    days, nodes = keep.shape
    outs = [shape(days // 2, nodes)] * 2 if distance else [keep]
    outs = [shape(*out.shape) for out in outs]
    return (*call(body, outs, "halved", (where,), [keep, got], work=0.05), None)[:2]


def bin_observations(where, obs_day, obs_node, obs_value, days, nodes, distance):
    chunk = min(512, obs_day.shape[0])
    chunks = obs_day.shape[0] // chunk

    def body(where_ref, day_ref, node_ref, value_ref, keep_out, sent_out):
        total = jnp.zeros((3 * days, nodes), F32)
        for index in range(chunks):
            row = pl.ds(index, 1)
            value = value_ref[row, :]
            high = value.astype(BF16).astype(F32)
            middle = (value - high).astype(BF16).astype(F32)
            low = value - high - middle
            is_day = lax.broadcasted_iota(jnp.int32, (days, chunk), 0) == day_ref[row, :]
            marked = jnp.concatenate(
                [jnp.where(is_day, part, 0.0).astype(BF16) for part in (high, middle, low)], axis=0
            )
            is_node = lax.broadcasted_iota(jnp.int32, (nodes, chunk), 0) == node_ref[row, :]
            total += lax.dot_general(
                marked, is_node.astype(F32).astype(BF16), (NT, ((), ())), preferred_element_type=F32
            )
        total = total[:days] + (total[days : 2 * days] + total[2 * days :])
        deal(where_ref, distance, total, keep_out, sent_out)

    return call(
        body,
        [shape(days // 2, nodes)] * 2,
        "bin_observations",
        (where,),
        [value.reshape(chunks, chunk) for value in (obs_day, obs_node, obs_value)],
        work=2,
    )


def gather_rows(where_ref, refs, take, out_ref):
    share = refs[0].shape[-2]
    for offset, ref in enumerate(refs):
        at = pl.ds(pl.multiple_of((where_ref[0, 0] ^ offset) * share, share), share)
        if len(ref.shape) == 3:
            ref = ref.at[take(offset) if callable(take) else take]
        out_ref[0, at, :], out_ref[1, at, :] = split(ref[...])


def local(inv_diag, coupling, noise, obs_day, obs_node, obs_value):
    part_count = lax.axis_size("tm")
    row_count = lax.axis_size("row")
    my_part = lax.axis_index("tm")
    my_row = lax.axis_index("row")
    day_count, share, nodes = inv_diag.shape
    columns = noise.shape[2]
    half = columns // PAIR
    half_nodes = nodes // CORES
    groups = part_count // PAIR
    chips = row_count // CORES
    early = day_count // 2
    late = day_count - early

    def to_row(value, distance):
        return lax.ppermute(value, "row", [(i, i ^ distance) for i in range(row_count)])

    def to_pair(value):
        return lax.ppermute(value, "tm", [(i, i ^ 1) for i in range(part_count)])

    def to_group(value, source, target):
        return lax.ppermute(
            value, "tm", [(PAIR * source + i, PAIR * target + i) for i in range(PAIR)]
        )

    def after(value, *others):
        return lax.optimization_barrier((value, *others))[0]

    where = jnp.broadcast_to(jnp.stack([my_row, my_part]).astype(jnp.int32)[:, None], (2, 128))

    line = shape(LINES, nodes)
    square = shape(nodes, nodes)
    map_parts = shape(2, nodes, nodes, dtype=BF16)
    samples_half = shape(half, nodes)
    samples_full = shape(columns, nodes)

    keep, sent = bin_observations(
        where, obs_day, obs_node, obs_value, part_count * day_count, nodes, part_count // 2
    )

    def over_chips(rows):
        return [to_row(rows, distance) for distance in range(CORES, row_count, CORES)]

    def shared(arrived, *ahead):
        return [piece for got in arrived for piece in (got, to_row(after(got, *ahead), 1))]

    arrived = []

    def send_rows(*rows):
        for piece in rows:
            if len(arrived) >= 2:
                piece = after(piece, *arrived[len(arrived) - 2][-1])
            pieces.append(over_chips(piece))
        arrived.append(pieces[-len(rows) :])

    pieces = []
    link_rows = [coupling[day : day + 1] for day in range(day_count)]
    for rows in (inv_diag, *link_rows[:-1]):
        send_rows(rows)
    own_inverse = [inv_diag, to_row(inv_diag, 1)]
    own_link = [coupling, to_row(coupling, 1)]
    where = after(where, keep, *link_rows)

    distance = part_count // 2
    while distance:
        got = lax.ppermute(sent, "tm", [(i, i ^ distance) for i in range(part_count)])
        distance //= 2
        keep, sent = halved(where, distance, keep, got)
    right_side = keep + to_row(keep, 1)

    first_rows = share // 2

    def pack_body(rows_ref, source_ref, first_out, rest_out):
        first_out[...] = rows_ref[0, :first_rows, :]
        rest_out[: share - first_rows, :] = rows_ref[0, first_rows:, :]
        rest_out[share - first_rows :, :] = jnp.zeros((LINES, nodes), F32)
        rest_out[share - first_rows : share - first_rows + day_count, :] = source_ref[...]

    packed = call(
        pack_body,
        (shape(first_rows, nodes), shape(share - first_rows + LINES, nodes)),
        "pack",
        (),
        [link_rows[-1], right_side],
        work=0.1,
    )
    send_rows(*packed)
    got_inverses, got_links = pieces[0], pieces[1:]

    def store(out_ref, pair):
        out_ref[0], out_ref[1] = pair

    def inverses_body(where_ref, *refs):
        row_refs, refs = refs[:row_count], refs[row_count:]
        noise_ref, gram_out, outs = refs[0], refs[1], refs[2:]
        for day in range(day_count):
            gather_rows(where_ref, row_refs, lambda offset: day, outs[day])
            outs[day_count + day][...] = dot_parts(
                split(noise_ref[day]), parts(outs[day]), TN
            )
        gram_out[...] = dot_parts(parts(outs[0]), parts(outs[0]), TN)

    gram, *results = call(
        inverses_body,
        [square, *[map_parts] * day_count, *[samples_full] * day_count],
        "inverses",
        (where,),
        [*own_inverse, *shared(got_inverses, where, *packed), noise],
        work=4,
    )
    inverses, local_terms = results[:day_count], results[day_count:]

    def early_body(where_ref, *refs):
        own_refs, refs = refs[:CORES], refs[CORES:]
        count = row_count - CORES
        got_refs, refs = refs[: count * early], refs[count * early :]
        noise_ref, term_ref, refs = refs[0], refs[1], refs[2:]
        inverse_refs, refs = refs[: early + 1], refs[early + 1 :]
        sum_out, *outs = refs
        link_outs, moved_outs, map_outs = outs[:early], outs[early : 2 * early], outs[2 * early :]
        for day in range(early):
            row_refs = (*own_refs, *got_refs[count * day : count * (day + 1)])
            gather_rows(
                where_ref, row_refs, lambda offset: day if offset < CORES else 0, link_outs[day]
            )
        total = term_ref[...]
        moved = parts(inverse_refs[0])
        for day in range(early):
            link = parts(link_outs[day])
            path = split(-dot_parts(link, moved, NN))
            if day == 0:
                store(map_outs[0], path)
            else:
                store(map_outs[day], split(-dot_parts(link, parts(inverse_refs[day]), NN)))
            moved = split(dot_parts(parts(inverse_refs[day + 1]), path, NN))
            store(moved_outs[day], moved)
            total = total + dot_parts(split(noise_ref[day + 1]), moved, TN)
        sum_out[...] = total

    summed, *results = call(
        early_body,
        [samples_full, *[map_parts] * (3 * early)],
        "early_days",
        (where,),
        [
            *own_link,
            *(piece for got in got_links[:early] for piece in shared(got, gram)),
            noise, local_terms[0], *inverses[: early + 1],
        ],
        work=6,
    )
    links, step_maps = list(results[:early]), list(results[2 * early :])
    moveds = [inverses[0], *results[early : 2 * early]]

    def next_body(day, where_ref, *refs):
        own_refs, got_refs, refs = refs[:CORES], refs[CORES:row_count], refs[row_count:]
        noise_ref, inverse_ref, sum_ref, moved_ref, link_out, moved_out, *sum_outs = refs
        gather_rows(
            where_ref, (*own_refs, *got_refs), lambda offset: day if offset < CORES else 0, link_out
        )
        path = split(-dot_parts(parts(link_out), parts(moved_ref), NN))
        moved = split(dot_parts(parts(inverse_ref), path, NN))
        store(moved_out, moved)
        total = sum_ref[...] + dot_parts(split(noise_ref[day + 1]), moved, TN)
        if len(sum_outs) == 1:
            sum_outs[0][...] = total
        else:
            first = (where_ref[1, 0] & (PAIR - 1)) == 0
            sum_outs[0][...] = jnp.where(first, total[:half], total[half:])
            sum_outs[1][...] = jnp.where(first, total[half:], total[:half])

    for day in range(early, day_count - 1):
        sums = [samples_half] * 2 if day == day_count - 2 else [samples_full]
        link, moved, *sums = call(
            functools.partial(next_body, day),
            [map_parts, map_parts, *sums],
            f"day_{day}",
            (where,),
            [
                *own_link, *shared(got_links[day], summed), noise, inverses[day + 1],
                summed, moveds[day],
            ],
            work=3,
        )
        summed = sums[0]
        moveds.append(moved)
        links.append(link)
    keep, send = sums
    other_sum = to_pair(send)

    def last_link_body(where_ref, *refs):
        own_refs, refs = refs[:CORES], refs[CORES:]
        count = row_count - CORES
        first_refs, rest_refs, refs = refs[:count], refs[count : 2 * count], refs[2 * count :]
        moved_ref, whole_out, half_out, link_out = refs
        rest_refs = [ref.at[pl.ds(0, share - first_rows)] for ref in rest_refs]
        pairs = [
            (ref.at[day_count - 1, pl.ds(0, first_rows)], ref.at[day_count - 1, pl.ds(first_rows, share - first_rows)])
            for ref in own_refs
        ] + list(zip(first_refs, rest_refs, strict=True))
        for offset, pair in enumerate(pairs):
            for ref, start, size in zip(
                pair, (0, first_rows), (first_rows, share - first_rows), strict=True
            ):
                start = (where_ref[0, 0] ^ offset) * share + start
                at = pl.ds(pl.multiple_of(start, first_rows), size)
                link_out[0, at, :], link_out[1, at, :] = split(ref[...])
        whole_out[...] = -dot_parts(parts(link_out), parts(moved_ref), NN)
        half_out[...] = whole_out[
            pl.ds(pl.multiple_of((where_ref[0, 0] & (CORES - 1)) * half_nodes, half_nodes), half_nodes), :
        ]

    path, path_half, link = call(
        last_link_body,
        (square, shape(half_nodes, nodes), map_parts),
        "last_link",
        (where,),
        [*own_link, *shared(got_links[-2], send), *shared(got_links[-1], send), moveds[-1]],
        work=1.5,
    )
    links.append(link)
    other_half = to_pair(after(path_half, other_sum))

    def lines_body(source_ref, *refs):
        got_refs, refs = refs[: chips - 1], refs[chips - 1 :]
        flux_out, back_out, current_out = refs[-3:]
        source = source_ref[...]
        for ref in got_refs:
            source = source + ref[share - first_rows : share - first_rows + day_count, :]
        applied = jnp.zeros((LINES, nodes), F32)
        back = applied
        for day in range(day_count):
            inverse_ref, link_ref, moved_ref = refs[3 * day : 3 * day + 3]
            wanted = source[day : day + 1] - applied
            current = dot_parts(split(wanted), parts(inverse_ref), NT)
            current_out[day] = current
            current = split(current)
            applied = dot_parts(current, parts(link_ref), NT)
            back = back + dot_parts(current, parts(moved_ref), NN)
        flux_out[...] = applied
        back_out[...] = back

    flux, back, currents = call(
        lines_body,
        (line, line, shape(day_count, LINES, nodes)),
        "lines",
        (),
        [
            right_side,
            *got_links[-1],
            *(
                ref for day in range(day_count)
                for ref in (inverses[day], links[day], moveds[day])
            ),
        ],
        work=5,
    )
    other_flux = to_pair(flux)

    def grams_body(gram_ref, *refs):
        total = gram_ref[...]
        for ref in refs[:-1]:
            total = total + dot_parts(parts(ref), parts(ref), TN)
        store(refs[-1], split(total))

    gram = call(grams_body, map_parts, "grams", (), [after(gram, flux), *moveds[1:]], work=3)

    def late_maps_body(*refs):
        for index in range(late):
            store(
                refs[2 * late + index],
                split(-dot_parts(parts(refs[late + index]), parts(refs[index]), NN)),
            )

    step_maps += call(
        late_maps_body,
        [map_parts] * late,
        "late_maps",
        (),
        [after(inverses[early], gram), *inverses[early + 1 :], *links[early:]],
        work=late,
    )

    other_rest = to_row(after(other_half, other_flux, *step_maps), 1)

    def pair_body(
        where_ref, path_ref, half_ref, rest_ref, sum_ref, other_ref, flux_ref, other_flux_ref,
        low_out, high_out, sum_out, high_sum_out, flux_out, low_flux_out,
    ):
        first = (where_ref[1, 0] & (PAIR - 1)) == 0
        lead = (where_ref[0, 0] & (CORES - 1)) == 0
        half_rows, rest_rows = half_ref[...], rest_ref[...]
        for at, rows in (
            (slice(0, half_nodes), jnp.where(lead, half_rows, rest_rows)),
            (slice(half_nodes, nodes), jnp.where(lead, rest_rows, half_rows)),
        ):
            own = path_ref[at, :]
            low_out[0, at, :], low_out[1, at, :] = split(jnp.where(first, own, rows))
            high_out[0, at, :], high_out[1, at, :] = split(jnp.where(first, rows, own))
        low_sum = jnp.where(first, sum_ref[...], other_ref[...])
        high_sum = jnp.where(first, other_ref[...], sum_ref[...])
        low_flux = jnp.where(first, flux_ref[...], other_flux_ref[...])
        high_flux = jnp.where(first, other_flux_ref[...], flux_ref[...])
        flux_out[...] = dot_parts(split(low_flux), parts(high_out), NT) + high_flux
        low_flux_out[...] = low_flux
        sum_out[...] = dot_parts(split(high_sum), parts(low_out), NN) + low_sum
        high_sum_out[...] = high_sum

    low_map, high_map, pair_sum, high_sum, pair_flux, low_flux = call(
        pair_body,
        (map_parts, map_parts, samples_half, samples_half, line, line),
        "pair_maps",
        (where,),
        [path, other_half, other_rest, keep, other_sum, flux, other_flux],
        work=1.5,
    )

    def group_map_body(low_ref, high_ref, out_ref):
        store(out_ref, split(dot_parts(parts(high_ref), parts(low_ref), NN)))

    group_map = call(
        group_map_body, map_parts, "group_map", (), [low_map, after(high_map, pair_sum)]
    )

    def link_body(dims, map_ref, local_ref, *refs):
        got = refs[0][...]
        for ref in refs[1:-1]:
            got = got + ref[...]
        refs[-1][...] = dot_parts(split(got), parts(map_ref), dims) + local_ref[...]

    def linked(dims, value_map, value, got, name):
        return call(
            functools.partial(link_body, dims), shape(*value.shape), name, (),
            [value_map, value, *got], work=0.6,
        )

    def added(refs):
        total = refs[0][...]
        for ref in refs[1:]:
            total = total + ref[...]
        return total

    def turn_body(where_ref, low_ref, flux_ref, gram_ref, back_ref, *refs):
        own_out, back_out, part_out = refs[-3:]
        given = added(refs[:-3])
        behind = dot_parts(split(given), parts(low_ref), NT) + flux_ref[...]
        first = (where_ref[1, 0] & (PAIR - 1)) == 0
        given = jnp.where(first, given, behind)
        own_out[...] = given
        own_back = back_ref[...] - dot_parts(split(given), parts(gram_ref), NN)
        back_out[...] = own_back
        part_out[...] = jnp.where(first, own_back, dot_parts(split(own_back), parts(low_ref), NN))

    def first_back_body(where_ref, map_ref, own_ref, other_ref, part_ref, mate_ref, *refs):
        value_out, pair_out, high_out = refs[-3:]
        first = (where_ref[1, 0] & (PAIR - 1)) == 0
        pair_back = part_ref[...] + mate_ref[...]
        pair_out[...] = pair_back
        high_out[...] = jnp.where(first, other_ref[...], own_ref[...])
        value_out[...] = dot_parts(split(added(refs[:-3])), parts(map_ref), NN) + pair_back

    mean = {}
    noise_step = []

    def mean_hops():
        value, got = pair_flux, []
        yield value
        for group in range(groups - 1):
            got.append(to_group(value, group, group + 1))
            if group < groups - 2:
                value = linked(NT, group_map, pair_flux, got, "forward_link")
                yield value
        mean["entering"], own_back, part = call(
            turn_body, (line, line, line), "mean_turn", (where,),
            [low_map, low_flux, gram, back, after(got[0], *noise_step), *got[1:]],
        )
        yield part
        last = PAIR * (groups - 1)
        got = [
            lax.ppermute(part, "tm", [(last + i, last - PAIR + (i ^ cross)) for i in range(PAIR)])
            for cross in range(PAIR)
        ]
        both = to_pair(jnp.concatenate([own_back, part], axis=0))
        value, pair_back, mean["high_back"] = call(
            first_back_body, (line, line, line), "first_back", (where,),
            [group_map, own_back, both[:LINES], part, both[LINES:], *got], work=0.6,
        )
        mean["leaving"] = got
        for group in range(groups - 2, 0, -1):
            yield value
            got.append(to_group(value, group, group - 1))
            if group > 1:
                gated = [after(got[0], *noise_step), *got[1:]]
                value = linked(NN, group_map, pair_back, gated, "backward_link")
        yield value

    hops = mean_hops()
    ahead = next(hops)

    leaving = []
    value = pair_sum
    for group in range(groups - 1, 0, -1):
        got = to_group(after(value, ahead), group, group - 1)
        ahead = next(hops)
        if group > 1:
            ahead = next(hops)
        leaving.append(after(got, ahead))
        if group > 1:
            value = linked(NN, group_map, pair_sum, leaving, "noise_link")
            noise_step[:] = [value]
    for _ in hops:
        pass

    def divide_body(where_ref, map_ref, sum_ref, *refs):
        keep_out, send_out = refs[-2:]
        given = refs[0][...]
        for ref in refs[1:-2]:
            given = given + ref[...]
        between = dot_parts(split(given), parts(map_ref), NN) + sum_ref[...]
        first = (where_ref[1, 0] & (PAIR - 1)) == 0
        keep_out[...] = jnp.where(first, between, given)
        send_out[...] = jnp.where(first, given, between)

    kept_half, sent_half = call(
        divide_body, (samples_half, samples_half), "divide", (where,),
        [high_map, high_sum, *leaving],
    )
    got_half = to_pair(sent_half)

    def terms_body(entering_ref, current_ref, *refs):
        outs = refs[-day_count:]
        given = split(entering_ref[...])
        for day in range(day_count):
            local_ref, inverse_ref, moved_ref = refs[3 * day : 3 * day + 3]
            current = current_ref[day] - dot_parts(given, parts(moved_ref), NT)
            term = dot_parts(split(current), parts(inverse_ref), NN)
            outs[day][...] = local_ref[...] + term[:1]

    terms = call(
        terms_body, [samples_full] * day_count, "mean_terms", (),
        [
            after(mean["entering"], sent_half), currents,
            *(
                value for day in range(day_count)
                for value in (local_terms[day], inverses[day], moveds[day])
            ),
        ],
        work=4,
    )

    def last_body(where_ref, keep_ref, got_ref, back_ref, high_ref, *refs):
        count = len(mean["leaving"])
        got_means, refs = refs[:count], refs[count:]
        map_refs, term_refs = refs[:day_count], refs[day_count : 2 * day_count]
        out_ref, held, sems = refs[2 * day_count :]
        first = (where_ref[1, 0] & (PAIR - 1)) == 0
        given = got_means[0][...]
        for ref in got_means[1:]:
            given = given + ref[...]
        between = dot_parts(split(given), parts(high_ref), NN) + back_ref[...]
        given = jnp.where(first, between, given)
        low = jnp.where(first, keep_ref[...], got_ref[...])
        high = jnp.where(first, got_ref[...], keep_ref[...])
        following = jnp.concatenate([low, high], axis=0) + given[:1]
        copies = []
        for day in reversed(range(day_count)):
            following = dot_parts(split(following), parts(map_refs[day]), NN) + term_refs[day][...]
            held[day] = following.T
            copies.append(pltpu.make_async_copy(held.at[day], out_ref.at[day], sems.at[day]))
            copies[-1].start()
        for copy in copies:
            copy.wait()

    return call(
        last_body, shape(day_count, nodes, columns), "last_days", (where,),
        [
            kept_half, got_half, mean["high_back"], high_map, *mean["leaving"], *step_maps,
            *terms,
        ],
        work=4,
        scratch=[
            pltpu.VMEM((day_count, nodes, columns), F32), pltpu.SemaphoreType.DMA((day_count,)),
        ],
        out_specs=pl.BlockSpec(memory_space=pl.ANY),
    )


def solution(mesh):
    return jax.shard_map(
        local,
        mesh=mesh,
        in_specs=(
            P("tm", "row", None),
            P("tm", "row", None),
            P("tm", None, "row"),
            P(("tm", "row")),
            P(("tm", "row")),
            P(("tm", "row")),
        ),
        out_specs=P("tm", None, "row"),
        check_vma=False,
    )
```

```python
import functools

import jax
import jax.numpy as jnp
from jax import lax
from jax.experimental import pallas as pl
from jax.experimental.pallas import tpu as pltpu
from jax.sharding import PartitionSpec as P

F32 = jnp.float32
BF16 = jnp.bfloat16
CORES = 2
PAIR = 2
LINES = 8

NN = ((1,), (0,))
TN = ((0,), (0,))
NT = ((1,), (1,))


def split(value):
    high = value.astype(BF16)
    return high, (value - high.astype(F32)).astype(BF16)


def parts(ref):
    return ref[0], ref[1]


def dot_parts(left, right, dims):
    product = functools.partial(
        lax.dot_general, dimension_numbers=(dims, ((), ())), preferred_element_type=F32
    )
    return product(left[0], right[0]) + (product(left[0], right[1]) + product(left[1], right[0]))


def shape(*dims, dtype=F32):
    return jax.ShapeDtypeStruct(dims, dtype)


def in_vmem(value):
    return pltpu.with_memory_space_constraint(value, pltpu.VMEM)


def call(body, outs, name, scalars, arrays, work=1, scratch=(), out_specs=None):
    vmem = pl.BlockSpec(memory_space=pltpu.VMEM)
    out_shape = outs if out_specs else jax.tree.map(lambda o: pltpu.VMEM(o.shape, o.dtype), outs)
    return pl.pallas_call(
        body,
        out_shape=out_shape,
        in_specs=[vmem] * (len(scalars) + len(arrays)),
        out_specs=out_specs or jax.tree.map(lambda _: vmem, outs),
        scratch_shapes=list(scratch),
        compiler_params=pltpu.CompilerParams(vmem_limit_bytes=12 * 1024 * 1024),
        cost_estimate=pl.CostEstimate(
            flops=int(work * 2.0e8), transcendentals=0, bytes_accessed=1024
        ),
        name=name,
    )(*map(in_vmem, (*scalars, *arrays)))


def deal(where_ref, distance, total, keep_out, sent_out):
    count = total.shape[0] // 2
    upper = (where_ref[1, 0] & distance) != 0
    keep_out[...] = jnp.where(upper, total[count:], total[:count])
    sent_out[...] = jnp.where(upper, total[:count], total[count:])


def halved(where, distance, keep, got):
    def body(where_ref, keep_ref, got_ref, *outs):
        total = keep_ref[...] + got_ref[...]
        if distance:
            deal(where_ref, distance, total, *outs)
        else:
            outs[0][...] = total

    days, nodes = keep.shape
    outs = [shape(days // 2, nodes)] * 2 if distance else [keep]
    outs = [shape(*out.shape) for out in outs]
    return (*call(body, outs, "halved", (where,), [keep, got], work=0.05), None)[:2]


def bin_observations(where, obs_day, obs_node, obs_value, days, nodes, distance):
    chunk = min(512, obs_day.shape[0])
    chunks = obs_day.shape[0] // chunk

    def body(where_ref, day_ref, node_ref, value_ref, keep_out, sent_out):
        total = jnp.zeros((3 * days, nodes), F32)
        for index in range(chunks):
            row = pl.ds(index, 1)
            value = value_ref[row, :]
            high = value.astype(BF16).astype(F32)
            middle = (value - high).astype(BF16).astype(F32)
            low = value - high - middle
            is_day = lax.broadcasted_iota(jnp.int32, (days, chunk), 0) == day_ref[row, :]
            marked = jnp.concatenate(
                [jnp.where(is_day, part, 0.0).astype(BF16) for part in (high, middle, low)], axis=0
            )
            is_node = lax.broadcasted_iota(jnp.int32, (nodes, chunk), 0) == node_ref[row, :]
            total += lax.dot_general(
                marked, is_node.astype(F32).astype(BF16), (NT, ((), ())), preferred_element_type=F32
            )
        total = total[:days] + (total[days : 2 * days] + total[2 * days :])
        deal(where_ref, distance, total, keep_out, sent_out)

    return call(
        body,
        [shape(days // 2, nodes)] * 2,
        "bin_observations",
        (where,),
        [value.reshape(chunks, chunk) for value in (obs_day, obs_node, obs_value)],
        work=2,
    )


def gather_rows(where_ref, refs, take, out_ref):
    share = refs[0].shape[-2]
    for offset, ref in enumerate(refs):
        at = pl.ds(pl.multiple_of((where_ref[0, 0] ^ offset) * share, share), share)
        if len(ref.shape) == 3:
            ref = ref.at[take(offset) if callable(take) else take]
        out_ref[0, at, :], out_ref[1, at, :] = split(ref[...])


def local(inv_diag, coupling, noise, obs_day, obs_node, obs_value):
    part_count = lax.axis_size("tm")
    row_count = lax.axis_size("row")
    my_part = lax.axis_index("tm")
    my_row = lax.axis_index("row")
    day_count, share, nodes = inv_diag.shape
    columns = noise.shape[2]
    half = columns // PAIR
    half_nodes = nodes // CORES
    groups = part_count // PAIR
    chips = row_count // CORES
    early = day_count // 2
    late = day_count - early

    def to_row(value, distance):
        return lax.ppermute(value, "row", [(i, i ^ distance) for i in range(row_count)])

    def to_pair(value):
        return lax.ppermute(value, "tm", [(i, i ^ 1) for i in range(part_count)])

    def to_group(value, source, target):
        return lax.ppermute(
            value, "tm", [(PAIR * source + i, PAIR * target + i) for i in range(PAIR)]
        )

    def after(value, *others):
        return lax.optimization_barrier((value, *others))[0]

    where = jnp.broadcast_to(jnp.stack([my_row, my_part]).astype(jnp.int32)[:, None], (2, 128))

    line = shape(LINES, nodes)
    square = shape(nodes, nodes)
    map_parts = shape(2, nodes, nodes, dtype=BF16)
    samples_half = shape(half, nodes)
    samples_full = shape(columns, nodes)

    keep, sent = bin_observations(
        where, obs_day, obs_node, obs_value, part_count * day_count, nodes, part_count // 2
    )

    def over_chips(rows):
        return [to_row(rows, distance) for distance in range(CORES, row_count, CORES)]

    def shared(arrived, *ahead):
        return [piece for got in arrived for piece in (got, to_row(after(got, *ahead), 1))]

    arrived = []

    def send_rows(*rows):
        for piece in rows:
            if len(arrived) >= 2:
                piece = after(piece, *arrived[len(arrived) - 2][-1])
            pieces.append(over_chips(piece))
        arrived.append(pieces[-len(rows) :])

    pieces = []
    link_rows = [coupling[day : day + 1] for day in range(day_count)]
    for rows in (inv_diag, *link_rows[:-1]):
        send_rows(rows)
    own_inverse = [inv_diag, to_row(inv_diag, 1)]
    own_link = [coupling, to_row(coupling, 1)]
    where = after(where, keep, *link_rows)

    distance = part_count // 2
    while distance:
        got = lax.ppermute(sent, "tm", [(i, i ^ distance) for i in range(part_count)])
        distance //= 2
        keep, sent = halved(where, distance, keep, got)
    right_side = keep + to_row(keep, 1)

    first_rows = share // 2

    def pack_body(rows_ref, source_ref, first_out, rest_out):
        first_out[...] = rows_ref[0, :first_rows, :]
        rest_out[: share - first_rows, :] = rows_ref[0, first_rows:, :]
        rest_out[share - first_rows :, :] = jnp.zeros((LINES, nodes), F32)
        rest_out[share - first_rows : share - first_rows + day_count, :] = source_ref[...]

    packed = call(
        pack_body,
        (shape(first_rows, nodes), shape(share - first_rows + LINES, nodes)),
        "pack",
        (),
        [link_rows[-1], right_side],
        work=0.1,
    )
    send_rows(*packed)
    got_inverses, got_links = pieces[0], pieces[1:]

    def store(out_ref, pair):
        out_ref[0], out_ref[1] = pair

    def inverses_body(where_ref, *refs):
        row_refs, refs = refs[:row_count], refs[row_count:]
        noise_ref, gram_out, outs = refs[0], refs[1], refs[2:]
        for day in range(day_count):
            gather_rows(where_ref, row_refs, lambda offset: day, outs[day])
            outs[day_count + day][...] = dot_parts(
                split(noise_ref[day]), parts(outs[day]), TN
            )
        gram_out[...] = dot_parts(parts(outs[0]), parts(outs[0]), TN)

    gram, *results = call(
        inverses_body,
        [square, *[map_parts] * day_count, *[samples_full] * day_count],
        "inverses",
        (where,),
        [*own_inverse, *shared(got_inverses, where, *packed, *got_links[0]), noise],
        work=4,
    )
    inverses, local_terms = results[:day_count], results[day_count:]

    def early_body(where_ref, *refs):
        own_refs, refs = refs[:CORES], refs[CORES:]
        count = row_count - CORES
        got_refs, refs = refs[: count * early], refs[count * early :]
        noise_ref, term_ref, refs = refs[0], refs[1], refs[2:]
        inverse_refs, refs = refs[: early + 1], refs[early + 1 :]
        sum_out, *outs = refs
        link_outs, moved_outs, map_outs = outs[:early], outs[early : 2 * early], outs[2 * early :]
        for day in range(early):
            row_refs = (*own_refs, *got_refs[count * day : count * (day + 1)])
            gather_rows(
                where_ref, row_refs, lambda offset: day if offset < CORES else 0, link_outs[day]
            )
        total = term_ref[...]
        moved = parts(inverse_refs[0])
        for day in range(early):
            link = parts(link_outs[day])
            path = split(-dot_parts(link, moved, NN))
            if day == 0:
                store(map_outs[0], path)
            else:
                store(map_outs[day], split(-dot_parts(link, parts(inverse_refs[day]), NN)))
            moved = split(dot_parts(parts(inverse_refs[day + 1]), path, NN))
            store(moved_outs[day], moved)
            total = total + dot_parts(split(noise_ref[day + 1]), moved, TN)
        sum_out[...] = total

    summed, *results = call(
        early_body,
        [samples_full, *[map_parts] * (3 * early)],
        "early_days",
        (where,),
        [
            *own_link,
            *(piece for got in got_links[:early] for piece in shared(got, gram)),
            noise, local_terms[0], *inverses[: early + 1],
        ],
        work=6,
    )
    links, step_maps = list(results[:early]), list(results[2 * early :])
    moveds = [inverses[0], *results[early : 2 * early]]

    def next_body(day, where_ref, *refs):
        own_refs, got_refs, refs = refs[:CORES], refs[CORES:row_count], refs[row_count:]
        noise_ref, inverse_ref, sum_ref, moved_ref, link_out, moved_out, *sum_outs = refs
        gather_rows(
            where_ref, (*own_refs, *got_refs), lambda offset: day if offset < CORES else 0, link_out
        )
        path = split(-dot_parts(parts(link_out), parts(moved_ref), NN))
        moved = split(dot_parts(parts(inverse_ref), path, NN))
        store(moved_out, moved)
        total = sum_ref[...] + dot_parts(split(noise_ref[day + 1]), moved, TN)
        if len(sum_outs) == 1:
            sum_outs[0][...] = total
        else:
            first = (where_ref[1, 0] & (PAIR - 1)) == 0
            sum_outs[0][...] = jnp.where(first, total[:half], total[half:])
            sum_outs[1][...] = jnp.where(first, total[half:], total[:half])

    for day in range(early, day_count - 1):
        sums = [samples_half] * 2 if day == day_count - 2 else [samples_full]
        link, moved, *sums = call(
            functools.partial(next_body, day),
            [map_parts, map_parts, *sums],
            f"day_{day}",
            (where,),
            [
                *own_link, *shared(got_links[day], summed, *got_links[day + 1]), noise, inverses[day + 1],
                summed, moveds[day],
            ],
            work=3,
        )
        summed = sums[0]
        moveds.append(moved)
        links.append(link)
    keep, send = sums
    other_sum = to_pair(send)

    def last_link_body(where_ref, *refs):
        own_refs, refs = refs[:CORES], refs[CORES:]
        count = row_count - CORES
        first_refs, rest_refs, refs = refs[:count], refs[count : 2 * count], refs[2 * count :]
        moved_ref, whole_out, half_out, link_out = refs
        rest_refs = [ref.at[pl.ds(0, share - first_rows)] for ref in rest_refs]
        pairs = [
            (ref.at[day_count - 1, pl.ds(0, first_rows)], ref.at[day_count - 1, pl.ds(first_rows, share - first_rows)])
            for ref in own_refs
        ] + list(zip(first_refs, rest_refs, strict=True))
        for offset, pair in enumerate(pairs):
            for ref, start, size in zip(
                pair, (0, first_rows), (first_rows, share - first_rows), strict=True
            ):
                start = (where_ref[0, 0] ^ offset) * share + start
                at = pl.ds(pl.multiple_of(start, first_rows), size)
                link_out[0, at, :], link_out[1, at, :] = split(ref[...])
        whole_out[...] = -dot_parts(parts(link_out), parts(moved_ref), NN)
        half_out[...] = whole_out[
            pl.ds(pl.multiple_of((where_ref[0, 0] & (CORES - 1)) * half_nodes, half_nodes), half_nodes), :
        ]

    path, path_half, link = call(
        last_link_body,
        (square, shape(half_nodes, nodes), map_parts),
        "last_link",
        (where,),
        [*own_link, *shared(got_links[-2], send), *shared(got_links[-1], send), moveds[-1]],
        work=1.5,
    )
    links.append(link)
    other_half = to_pair(after(path_half, other_sum))

    def lines_body(source_ref, *refs):
        got_refs, refs = refs[: chips - 1], refs[chips - 1 :]
        flux_out, back_out, current_out = refs[-3:]
        source = source_ref[...]
        for ref in got_refs:
            source = source + ref[share - first_rows : share - first_rows + day_count, :]
        applied = jnp.zeros((LINES, nodes), F32)
        back = applied
        for day in range(day_count):
            inverse_ref, link_ref, moved_ref = refs[3 * day : 3 * day + 3]
            wanted = source[day : day + 1] - applied
            current = dot_parts(split(wanted), parts(inverse_ref), NT)
            current_out[day] = current
            current = split(current)
            applied = dot_parts(current, parts(link_ref), NT)
            back = back + dot_parts(current, parts(moved_ref), NN)
        flux_out[...] = applied
        back_out[...] = back

    flux, back, currents = call(
        lines_body,
        (line, line, shape(day_count, LINES, nodes)),
        "lines",
        (),
        [
            right_side,
            *got_links[-1],
            *(
                ref for day in range(day_count)
                for ref in (inverses[day], links[day], moveds[day])
            ),
        ],
        work=5,
    )
    other_flux = to_pair(flux)

    def grams_body(gram_ref, *refs):
        total = gram_ref[...]
        for ref in refs[:-1]:
            total = total + dot_parts(parts(ref), parts(ref), TN)
        store(refs[-1], split(total))

    gram = call(grams_body, map_parts, "grams", (), [after(gram, flux), *moveds[1:]], work=3)

    def late_maps_body(*refs):
        for index in range(late):
            store(
                refs[2 * late + index],
                split(-dot_parts(parts(refs[late + index]), parts(refs[index]), NN)),
            )

    step_maps += call(
        late_maps_body,
        [map_parts] * late,
        "late_maps",
        (),
        [after(inverses[early], gram), *inverses[early + 1 :], *links[early:]],
        work=late,
    )

    other_rest = to_row(after(other_half, other_flux, *step_maps), 1)

    def pair_body(
        where_ref, path_ref, half_ref, rest_ref, sum_ref, other_ref, flux_ref, other_flux_ref,
        low_out, high_out, sum_out, high_sum_out, flux_out, low_flux_out,
    ):
        first = (where_ref[1, 0] & (PAIR - 1)) == 0
        lead = (where_ref[0, 0] & (CORES - 1)) == 0
        half_rows, rest_rows = half_ref[...], rest_ref[...]
        for at, rows in (
            (slice(0, half_nodes), jnp.where(lead, half_rows, rest_rows)),
            (slice(half_nodes, nodes), jnp.where(lead, rest_rows, half_rows)),
        ):
            own = path_ref[at, :]
            low_out[0, at, :], low_out[1, at, :] = split(jnp.where(first, own, rows))
            high_out[0, at, :], high_out[1, at, :] = split(jnp.where(first, rows, own))
        low_sum = jnp.where(first, sum_ref[...], other_ref[...])
        high_sum = jnp.where(first, other_ref[...], sum_ref[...])
        low_flux = jnp.where(first, flux_ref[...], other_flux_ref[...])
        high_flux = jnp.where(first, other_flux_ref[...], flux_ref[...])
        flux_out[...] = dot_parts(split(low_flux), parts(high_out), NT) + high_flux
        low_flux_out[...] = low_flux
        sum_out[...] = dot_parts(split(high_sum), parts(low_out), NN) + low_sum
        high_sum_out[...] = high_sum

    low_map, high_map, pair_sum, high_sum, pair_flux, low_flux = call(
        pair_body,
        (map_parts, map_parts, samples_half, samples_half, line, line),
        "pair_maps",
        (where,),
        [path, other_half, other_rest, keep, other_sum, flux, other_flux],
        work=1.5,
    )

    def group_map_body(low_ref, high_ref, out_ref):
        store(out_ref, split(dot_parts(parts(high_ref), parts(low_ref), NN)))

    group_map = call(
        group_map_body, map_parts, "group_map", (), [low_map, after(high_map, pair_sum)]
    )

    def link_body(dims, map_ref, local_ref, *refs):
        got = refs[0][...]
        for ref in refs[1:-1]:
            got = got + ref[...]
        refs[-1][...] = dot_parts(split(got), parts(map_ref), dims) + local_ref[...]

    def linked(dims, value_map, value, got, name):
        return call(
            functools.partial(link_body, dims), shape(*value.shape), name, (),
            [value_map, value, *got], work=0.6,
        )

    def added(refs):
        total = refs[0][...]
        for ref in refs[1:]:
            total = total + ref[...]
        return total

    def turn_body(where_ref, low_ref, flux_ref, gram_ref, back_ref, *refs):
        own_out, back_out, part_out = refs[-3:]
        given = added(refs[:-3])
        behind = dot_parts(split(given), parts(low_ref), NT) + flux_ref[...]
        first = (where_ref[1, 0] & (PAIR - 1)) == 0
        given = jnp.where(first, given, behind)
        own_out[...] = given
        own_back = back_ref[...] - dot_parts(split(given), parts(gram_ref), NN)
        back_out[...] = own_back
        part_out[...] = jnp.where(first, own_back, dot_parts(split(own_back), parts(low_ref), NN))

    def first_back_body(where_ref, map_ref, own_ref, other_ref, part_ref, mate_ref, *refs):
        value_out, pair_out, high_out = refs[-3:]
        first = (where_ref[1, 0] & (PAIR - 1)) == 0
        pair_back = part_ref[...] + mate_ref[...]
        pair_out[...] = pair_back
        high_out[...] = jnp.where(first, other_ref[...], own_ref[...])
        value_out[...] = dot_parts(split(added(refs[:-3])), parts(map_ref), NN) + pair_back

    mean = {}
    noise_step = []

    def mean_hops():
        value, got = pair_flux, []
        yield value
        for group in range(groups - 1):
            got.append(to_group(value, group, group + 1))
            if group < groups - 2:
                value = linked(NT, group_map, pair_flux, got, "forward_link")
                yield value
        mean["entering"], own_back, part = call(
            turn_body, (line, line, line), "mean_turn", (where,),
            [low_map, low_flux, gram, back, after(got[0], *noise_step), *got[1:]],
        )
        yield part
        last = PAIR * (groups - 1)
        got = [
            lax.ppermute(part, "tm", [(last + i, last - PAIR + (i ^ cross)) for i in range(PAIR)])
            for cross in range(PAIR)
        ]
        both = to_pair(jnp.concatenate([own_back, part], axis=0))
        value, pair_back, mean["high_back"] = call(
            first_back_body, (line, line, line), "first_back", (where,),
            [group_map, own_back, both[:LINES], part, both[LINES:], *got], work=0.6,
        )
        mean["leaving"] = got
        for group in range(groups - 2, 0, -1):
            yield value
            got.append(to_group(value, group, group - 1))
            if group > 1:
                gated = [after(got[0], *noise_step), *got[1:]]
                value = linked(NN, group_map, pair_back, gated, "backward_link")
        yield value

    hops = mean_hops()
    ahead = next(hops)

    leaving = []
    value = pair_sum
    for group in range(groups - 1, 0, -1):
        got = to_group(after(value, ahead), group, group - 1)
        ahead = next(hops)
        if group > 1:
            ahead = next(hops)
        leaving.append(after(got, ahead))
        if group > 1:
            value = linked(NN, group_map, pair_sum, leaving, "noise_link")
            noise_step[:] = [value]
    for _ in hops:
        pass

    def divide_body(where_ref, map_ref, sum_ref, *refs):
        keep_out, send_out = refs[-2:]
        given = refs[0][...]
        for ref in refs[1:-2]:
            given = given + ref[...]
        between = dot_parts(split(given), parts(map_ref), NN) + sum_ref[...]
        first = (where_ref[1, 0] & (PAIR - 1)) == 0
        keep_out[...] = jnp.where(first, between, given)
        send_out[...] = jnp.where(first, given, between)

    kept_half, sent_half = call(
        divide_body, (samples_half, samples_half), "divide", (where,),
        [high_map, high_sum, *leaving],
    )
    got_half = to_pair(sent_half)

    def terms_body(entering_ref, current_ref, *refs):
        outs = refs[-day_count:]
        given = split(entering_ref[...])
        for day in range(day_count):
            local_ref, inverse_ref, moved_ref = refs[3 * day : 3 * day + 3]
            current = current_ref[day] - dot_parts(given, parts(moved_ref), NT)
            term = dot_parts(split(current), parts(inverse_ref), NN)
            outs[day][...] = local_ref[...] + term[:1]

    terms = call(
        terms_body, [samples_full] * day_count, "mean_terms", (),
        [
            after(mean["entering"], sent_half), currents,
            *(
                value for day in range(day_count)
                for value in (local_terms[day], inverses[day], moveds[day])
            ),
        ],
        work=4,
    )

    def last_body(where_ref, keep_ref, got_ref, back_ref, high_ref, *refs):
        count = len(mean["leaving"])
        got_means, refs = refs[:count], refs[count:]
        map_refs, term_refs = refs[:day_count], refs[day_count : 2 * day_count]
        out_ref, held, sems = refs[2 * day_count :]
        first = (where_ref[1, 0] & (PAIR - 1)) == 0
        given = got_means[0][...]
        for ref in got_means[1:]:
            given = given + ref[...]
        between = dot_parts(split(given), parts(high_ref), NN) + back_ref[...]
        given = jnp.where(first, between, given)
        low = jnp.where(first, keep_ref[...], got_ref[...])
        high = jnp.where(first, got_ref[...], keep_ref[...])
        following = jnp.concatenate([low, high], axis=0) + given[:1]
        copies = []
        for day in reversed(range(day_count)):
            following = dot_parts(split(following), parts(map_refs[day]), NN) + term_refs[day][...]
            held[day] = following.T
            copies.append(pltpu.make_async_copy(held.at[day], out_ref.at[day], sems.at[day]))
            copies[-1].start()
        for copy in copies:
            copy.wait()

    return call(
        last_body, shape(day_count, nodes, columns), "last_days", (where,),
        [
            kept_half, got_half, mean["high_back"], high_map, *mean["leaving"], *step_maps,
            *terms,
        ],
        work=4,
        scratch=[
            pltpu.VMEM((day_count, nodes, columns), F32), pltpu.SemaphoreType.DMA((day_count,)),
        ],
        out_specs=pl.BlockSpec(memory_space=pl.ANY),
    )


def solution(mesh):
    return jax.shard_map(
        local,
        mesh=mesh,
        in_specs=(
            P("tm", "row", None),
            P("tm", "row", None),
            P("tm", None, "row"),
            P(("tm", "row")),
            P(("tm", "row")),
            P(("tm", "row")),
        ),
        out_specs=P("tm", None, "row"),
        check_vma=False,
    )
```

```python
import functools

import jax
import jax.numpy as jnp
from jax import lax
from jax.experimental import pallas as pl
from jax.experimental.pallas import tpu as pltpu
from jax.sharding import PartitionSpec as P

F32 = jnp.float32
BF16 = jnp.bfloat16
CORES = 2
PAIR = 2
LINES = 8

NN = ((1,), (0,))
TN = ((0,), (0,))
NT = ((1,), (1,))


def split(value):
    high = value.astype(BF16)
    return high, (value - high.astype(F32)).astype(BF16)


def parts(ref):
    return ref[0], ref[1]


def dot_parts(left, right, dims):
    product = functools.partial(
        lax.dot_general, dimension_numbers=(dims, ((), ())), preferred_element_type=F32
    )
    return product(left[0], right[0]) + (product(left[0], right[1]) + product(left[1], right[0]))


def shape(*dims, dtype=F32):
    return jax.ShapeDtypeStruct(dims, dtype)


def in_vmem(value):
    return pltpu.with_memory_space_constraint(value, pltpu.VMEM)


def call(body, outs, name, scalars, arrays, work=1, scratch=(), out_specs=None):
    vmem = pl.BlockSpec(memory_space=pltpu.VMEM)
    out_shape = outs if out_specs else jax.tree.map(lambda o: pltpu.VMEM(o.shape, o.dtype), outs)
    return pl.pallas_call(
        body,
        out_shape=out_shape,
        in_specs=[vmem] * (len(scalars) + len(arrays)),
        out_specs=out_specs or jax.tree.map(lambda _: vmem, outs),
        scratch_shapes=list(scratch),
        compiler_params=pltpu.CompilerParams(vmem_limit_bytes=12 * 1024 * 1024),
        cost_estimate=pl.CostEstimate(
            flops=int(work * 2.0e8), transcendentals=0, bytes_accessed=1024
        ),
        name=name,
    )(*map(in_vmem, (*scalars, *arrays)))


def deal(where_ref, distance, total, keep_out, sent_out):
    count = total.shape[0] // 2
    upper = (where_ref[1, 0] & distance) != 0
    keep_out[...] = jnp.where(upper, total[count:], total[:count])
    sent_out[...] = jnp.where(upper, total[:count], total[count:])


def halved(where, distance, keep, got):
    def body(where_ref, keep_ref, got_ref, *outs):
        total = keep_ref[...] + got_ref[...]
        if distance:
            deal(where_ref, distance, total, *outs)
        else:
            outs[0][...] = total

    days, nodes = keep.shape
    outs = [shape(days // 2, nodes)] * 2 if distance else [keep]
    outs = [shape(*out.shape) for out in outs]
    return (*call(body, outs, "halved", (where,), [keep, got], work=0.05), None)[:2]


def bin_observations(where, obs_day, obs_node, obs_value, days, nodes, distance):
    chunk = min(512, obs_day.shape[0])
    chunks = obs_day.shape[0] // chunk

    def body(where_ref, day_ref, node_ref, value_ref, keep_out, sent_out):
        total = jnp.zeros((3 * days, nodes), F32)
        for index in range(chunks):
            row = pl.ds(index, 1)
            value = value_ref[row, :]
            high = value.astype(BF16).astype(F32)
            middle = (value - high).astype(BF16).astype(F32)
            low = value - high - middle
            is_day = lax.broadcasted_iota(jnp.int32, (days, chunk), 0) == day_ref[row, :]
            marked = jnp.concatenate(
                [jnp.where(is_day, part, 0.0).astype(BF16) for part in (high, middle, low)], axis=0
            )
            is_node = lax.broadcasted_iota(jnp.int32, (nodes, chunk), 0) == node_ref[row, :]
            total += lax.dot_general(
                marked, is_node.astype(F32).astype(BF16), (NT, ((), ())), preferred_element_type=F32
            )
        total = total[:days] + (total[days : 2 * days] + total[2 * days :])
        deal(where_ref, distance, total, keep_out, sent_out)

    return call(
        body,
        [shape(days // 2, nodes)] * 2,
        "bin_observations",
        (where,),
        [value.reshape(chunks, chunk) for value in (obs_day, obs_node, obs_value)],
        work=2,
    )


def gather_rows(where_ref, refs, take, out_ref):
    share = refs[0].shape[-2]
    for offset, ref in enumerate(refs):
        at = pl.ds(pl.multiple_of((where_ref[0, 0] ^ offset) * share, share), share)
        if len(ref.shape) == 3:
            ref = ref.at[take(offset) if callable(take) else take]
        out_ref[0, at, :], out_ref[1, at, :] = split(ref[...])


def local(inv_diag, coupling, noise, obs_day, obs_node, obs_value):
    part_count = lax.axis_size("tm")
    row_count = lax.axis_size("row")
    my_part = lax.axis_index("tm")
    my_row = lax.axis_index("row")
    day_count, share, nodes = inv_diag.shape
    columns = noise.shape[2]
    half = columns // PAIR
    half_nodes = nodes // CORES
    groups = part_count // PAIR
    chips = row_count // CORES
    early = day_count // 2
    late = day_count - early

    def to_row(value, distance):
        return lax.ppermute(value, "row", [(i, i ^ distance) for i in range(row_count)])

    def to_pair(value):
        return lax.ppermute(value, "tm", [(i, i ^ 1) for i in range(part_count)])

    def to_group(value, source, target):
        return lax.ppermute(
            value, "tm", [(PAIR * source + i, PAIR * target + i) for i in range(PAIR)]
        )

    def after(value, *others):
        return lax.optimization_barrier((value, *others))[0]

    where = jnp.broadcast_to(jnp.stack([my_row, my_part]).astype(jnp.int32)[:, None], (2, 128))

    line = shape(LINES, nodes)
    square = shape(nodes, nodes)
    map_parts = shape(2, nodes, nodes, dtype=BF16)
    samples_half = shape(half, nodes)
    samples_full = shape(columns, nodes)

    keep, sent = bin_observations(
        where, obs_day, obs_node, obs_value, part_count * day_count, nodes, part_count // 2
    )

    def over_chips(rows):
        return [to_row(rows, distance) for distance in range(CORES, row_count, CORES)]

    def shared(arrived, *ahead):
        return [piece for got in arrived for piece in (got, to_row(after(got, *ahead), 1))]

    arrived = []

    def send_rows(*rows):
        for piece in rows:
            if len(arrived) >= 2:
                piece = after(piece, *arrived[len(arrived) - 2][-1])
            pieces.append(over_chips(piece))
        arrived.append(pieces[-len(rows) :])

    pieces = []
    link_rows = [coupling[day : day + 1] for day in range(day_count)]
    for rows in (inv_diag, *link_rows[:-1]):
        send_rows(rows)
    own_inverse = [inv_diag, to_row(inv_diag, 1)]
    own_link = [coupling, to_row(coupling, 1)]
    where = after(where, keep, own_link[1], *link_rows)

    distance = part_count // 2
    while distance:
        got = lax.ppermute(sent, "tm", [(i, i ^ distance) for i in range(part_count)])
        distance //= 2
        keep, sent = halved(where, distance, keep, got)
    right_side = keep + to_row(keep, 1)

    first_rows = share // 2

    def pack_body(rows_ref, source_ref, first_out, rest_out):
        first_out[...] = rows_ref[0, :first_rows, :]
        rest_out[: share - first_rows, :] = rows_ref[0, first_rows:, :]
        rest_out[share - first_rows :, :] = jnp.zeros((LINES, nodes), F32)
        rest_out[share - first_rows : share - first_rows + day_count, :] = source_ref[...]

    packed = call(
        pack_body,
        (shape(first_rows, nodes), shape(share - first_rows + LINES, nodes)),
        "pack",
        (),
        [link_rows[-1], right_side],
        work=0.1,
    )
    send_rows(*packed)
    got_inverses, got_links = pieces[0], pieces[1:]

    def store(out_ref, pair):
        out_ref[0], out_ref[1] = pair

    def inverses_body(where_ref, *refs):
        row_refs, refs = refs[:row_count], refs[row_count:]
        noise_ref, gram_out, outs = refs[0], refs[1], refs[2:]
        for day in range(day_count):
            gather_rows(where_ref, row_refs, lambda offset: day, outs[day])
            outs[day_count + day][...] = dot_parts(
                split(noise_ref[day]), parts(outs[day]), TN
            )
        gram_out[...] = dot_parts(parts(outs[0]), parts(outs[0]), TN)

    gram, *results = call(
        inverses_body,
        [square, *[map_parts] * day_count, *[samples_full] * day_count],
        "inverses",
        (where,),
        [*own_inverse, *shared(got_inverses, where, *packed), noise],
        work=4,
    )
    inverses, local_terms = results[:day_count], results[day_count:]

    def early_body(where_ref, *refs):
        own_refs, refs = refs[:CORES], refs[CORES:]
        count = row_count - CORES
        got_refs, refs = refs[: count * early], refs[count * early :]
        noise_ref, term_ref, refs = refs[0], refs[1], refs[2:]
        inverse_refs, refs = refs[: early + 1], refs[early + 1 :]
        sum_out, *outs = refs
        link_outs, moved_outs, map_outs = outs[:early], outs[early : 2 * early], outs[2 * early :]
        for day in range(early):
            row_refs = (*own_refs, *got_refs[count * day : count * (day + 1)])
            gather_rows(
                where_ref, row_refs, lambda offset: day if offset < CORES else 0, link_outs[day]
            )
        total = term_ref[...]
        moved = parts(inverse_refs[0])
        for day in range(early):
            link = parts(link_outs[day])
            path = split(-dot_parts(link, moved, NN))
            if day == 0:
                store(map_outs[0], path)
            else:
                store(map_outs[day], split(-dot_parts(link, parts(inverse_refs[day]), NN)))
            moved = split(dot_parts(parts(inverse_refs[day + 1]), path, NN))
            store(moved_outs[day], moved)
            total = total + dot_parts(split(noise_ref[day + 1]), moved, TN)
        sum_out[...] = total

    summed, *results = call(
        early_body,
        [samples_full, *[map_parts] * (3 * early)],
        "early_days",
        (where,),
        [
            *own_link,
            *(piece for got in got_links[:early] for piece in shared(got, gram)),
            noise, local_terms[0], *inverses[: early + 1],
        ],
        work=6,
    )
    links, step_maps = list(results[:early]), list(results[2 * early :])
    moveds = [inverses[0], *results[early : 2 * early]]

    def next_body(day, where_ref, *refs):
        own_refs, got_refs, refs = refs[:CORES], refs[CORES:row_count], refs[row_count:]
        noise_ref, inverse_ref, sum_ref, moved_ref, link_out, moved_out, *sum_outs = refs
        gather_rows(
            where_ref, (*own_refs, *got_refs), lambda offset: day if offset < CORES else 0, link_out
        )
        path = split(-dot_parts(parts(link_out), parts(moved_ref), NN))
        moved = split(dot_parts(parts(inverse_ref), path, NN))
        store(moved_out, moved)
        total = sum_ref[...] + dot_parts(split(noise_ref[day + 1]), moved, TN)
        if len(sum_outs) == 1:
            sum_outs[0][...] = total
        else:
            first = (where_ref[1, 0] & (PAIR - 1)) == 0
            sum_outs[0][...] = jnp.where(first, total[:half], total[half:])
            sum_outs[1][...] = jnp.where(first, total[half:], total[:half])

    for day in range(early, day_count - 1):
        sums = [samples_half] * 2 if day == day_count - 2 else [samples_full]
        link, moved, *sums = call(
            functools.partial(next_body, day),
            [map_parts, map_parts, *sums],
            f"day_{day}",
            (where,),
            [
                *own_link, *shared(got_links[day], summed), noise, inverses[day + 1],
                summed, moveds[day],
            ],
            work=3,
        )
        summed = sums[0]
        moveds.append(moved)
        links.append(link)
    keep, send = sums
    other_sum = to_pair(send)

    def last_link_body(where_ref, *refs):
        own_refs, refs = refs[:CORES], refs[CORES:]
        count = row_count - CORES
        first_refs, rest_refs, refs = refs[:count], refs[count : 2 * count], refs[2 * count :]
        moved_ref, whole_out, half_out, link_out = refs
        rest_refs = [ref.at[pl.ds(0, share - first_rows)] for ref in rest_refs]
        pairs = [
            (ref.at[day_count - 1, pl.ds(0, first_rows)], ref.at[day_count - 1, pl.ds(first_rows, share - first_rows)])
            for ref in own_refs
        ] + list(zip(first_refs, rest_refs, strict=True))
        for offset, pair in enumerate(pairs):
            for ref, start, size in zip(
                pair, (0, first_rows), (first_rows, share - first_rows), strict=True
            ):
                start = (where_ref[0, 0] ^ offset) * share + start
                at = pl.ds(pl.multiple_of(start, first_rows), size)
                link_out[0, at, :], link_out[1, at, :] = split(ref[...])
        whole_out[...] = -dot_parts(parts(link_out), parts(moved_ref), NN)
        half_out[...] = whole_out[
            pl.ds(pl.multiple_of((where_ref[0, 0] & (CORES - 1)) * half_nodes, half_nodes), half_nodes), :
        ]

    path, path_half, link = call(
        last_link_body,
        (square, shape(half_nodes, nodes), map_parts),
        "last_link",
        (where,),
        [*own_link, *shared(got_links[-2], send), *shared(got_links[-1], send), moveds[-1]],
        work=1.5,
    )
    links.append(link)
    other_half = to_pair(after(path_half, other_sum))

    def lines_body(source_ref, *refs):
        got_refs, refs = refs[: chips - 1], refs[chips - 1 :]
        flux_out, back_out, current_out = refs[-3:]
        source = source_ref[...]
        for ref in got_refs:
            source = source + ref[share - first_rows : share - first_rows + day_count, :]
        applied = jnp.zeros((LINES, nodes), F32)
        back = applied
        for day in range(day_count):
            inverse_ref, link_ref, moved_ref = refs[3 * day : 3 * day + 3]
            wanted = source[day : day + 1] - applied
            current = dot_parts(split(wanted), parts(inverse_ref), NT)
            current_out[day] = current
            current = split(current)
            applied = dot_parts(current, parts(link_ref), NT)
            back = back + dot_parts(current, parts(moved_ref), NN)
        flux_out[...] = applied
        back_out[...] = back

    flux, back, currents = call(
        lines_body,
        (line, line, shape(day_count, LINES, nodes)),
        "lines",
        (),
        [
            right_side,
            *got_links[-1],
            *(
                ref for day in range(day_count)
                for ref in (inverses[day], links[day], moveds[day])
            ),
        ],
        work=5,
    )
    other_flux = to_pair(flux)

    def grams_body(gram_ref, *refs):
        total = gram_ref[...]
        for ref in refs[:-1]:
            total = total + dot_parts(parts(ref), parts(ref), TN)
        store(refs[-1], split(total))

    gram = call(grams_body, map_parts, "grams", (), [after(gram, flux), *moveds[1:]], work=3)

    def late_maps_body(*refs):
        for index in range(late):
            store(
                refs[2 * late + index],
                split(-dot_parts(parts(refs[late + index]), parts(refs[index]), NN)),
            )

    step_maps += call(
        late_maps_body,
        [map_parts] * late,
        "late_maps",
        (),
        [after(inverses[early], gram), *inverses[early + 1 :], *links[early:]],
        work=late,
    )

    other_rest = to_row(after(other_half, other_flux, *step_maps), 1)

    def pair_body(
        where_ref, path_ref, half_ref, rest_ref, sum_ref, other_ref, flux_ref, other_flux_ref,
        low_out, high_out, sum_out, high_sum_out, flux_out, low_flux_out,
    ):
        first = (where_ref[1, 0] & (PAIR - 1)) == 0
        lead = (where_ref[0, 0] & (CORES - 1)) == 0
        half_rows, rest_rows = half_ref[...], rest_ref[...]
        for at, rows in (
            (slice(0, half_nodes), jnp.where(lead, half_rows, rest_rows)),
            (slice(half_nodes, nodes), jnp.where(lead, rest_rows, half_rows)),
        ):
            own = path_ref[at, :]
            low_out[0, at, :], low_out[1, at, :] = split(jnp.where(first, own, rows))
            high_out[0, at, :], high_out[1, at, :] = split(jnp.where(first, rows, own))
        low_sum = jnp.where(first, sum_ref[...], other_ref[...])
        high_sum = jnp.where(first, other_ref[...], sum_ref[...])
        low_flux = jnp.where(first, flux_ref[...], other_flux_ref[...])
        high_flux = jnp.where(first, other_flux_ref[...], flux_ref[...])
        flux_out[...] = dot_parts(split(low_flux), parts(high_out), NT) + high_flux
        low_flux_out[...] = low_flux
        sum_out[...] = dot_parts(split(high_sum), parts(low_out), NN) + low_sum
        high_sum_out[...] = high_sum

    low_map, high_map, pair_sum, high_sum, pair_flux, low_flux = call(
        pair_body,
        (map_parts, map_parts, samples_half, samples_half, line, line),
        "pair_maps",
        (where,),
        [path, other_half, other_rest, keep, other_sum, flux, other_flux],
        work=1.5,
    )

    def group_map_body(low_ref, high_ref, out_ref):
        store(out_ref, split(dot_parts(parts(high_ref), parts(low_ref), NN)))

    group_map = call(
        group_map_body, map_parts, "group_map", (), [low_map, after(high_map, pair_sum)]
    )

    def link_body(dims, map_ref, local_ref, *refs):
        got = refs[0][...]
        for ref in refs[1:-1]:
            got = got + ref[...]
        refs[-1][...] = dot_parts(split(got), parts(map_ref), dims) + local_ref[...]

    def linked(dims, value_map, value, got, name):
        return call(
            functools.partial(link_body, dims), shape(*value.shape), name, (),
            [value_map, value, *got], work=0.6,
        )

    def added(refs):
        total = refs[0][...]
        for ref in refs[1:]:
            total = total + ref[...]
        return total

    def turn_body(where_ref, low_ref, flux_ref, gram_ref, back_ref, *refs):
        own_out, back_out, part_out = refs[-3:]
        given = added(refs[:-3])
        behind = dot_parts(split(given), parts(low_ref), NT) + flux_ref[...]
        first = (where_ref[1, 0] & (PAIR - 1)) == 0
        given = jnp.where(first, given, behind)
        own_out[...] = given
        own_back = back_ref[...] - dot_parts(split(given), parts(gram_ref), NN)
        back_out[...] = own_back
        part_out[...] = jnp.where(first, own_back, dot_parts(split(own_back), parts(low_ref), NN))

    def first_back_body(where_ref, map_ref, own_ref, other_ref, part_ref, mate_ref, *refs):
        value_out, pair_out, high_out = refs[-3:]
        first = (where_ref[1, 0] & (PAIR - 1)) == 0
        pair_back = part_ref[...] + mate_ref[...]
        pair_out[...] = pair_back
        high_out[...] = jnp.where(first, other_ref[...], own_ref[...])
        value_out[...] = dot_parts(split(added(refs[:-3])), parts(map_ref), NN) + pair_back

    mean = {}
    noise_step = []

    def mean_hops():
        value, got = pair_flux, []
        yield value
        for group in range(groups - 1):
            got.append(to_group(value, group, group + 1))
            if group < groups - 2:
                value = linked(NT, group_map, pair_flux, got, "forward_link")
                yield value
        mean["entering"], own_back, part = call(
            turn_body, (line, line, line), "mean_turn", (where,),
            [low_map, low_flux, gram, back, after(got[0], *noise_step), *got[1:]],
        )
        yield part
        last = PAIR * (groups - 1)
        got = [
            lax.ppermute(part, "tm", [(last + i, last - PAIR + (i ^ cross)) for i in range(PAIR)])
            for cross in range(PAIR)
        ]
        both = to_pair(jnp.concatenate([own_back, part], axis=0))
        value, pair_back, mean["high_back"] = call(
            first_back_body, (line, line, line), "first_back", (where,),
            [
                group_map, after(own_back, *noise_step), both[:LINES], part, both[LINES:], *got,
            ],
            work=0.6,
        )
        mean["leaving"] = got
        for group in range(groups - 2, 0, -1):
            yield value
            got.append(to_group(value, group, group - 1))
            if group > 1:
                gated = [after(got[0], *noise_step), *got[1:]]
                value = linked(NN, group_map, pair_back, gated, "backward_link")
        yield value

    hops = mean_hops()
    ahead = next(hops)

    leaving = []
    value = pair_sum
    for group in range(groups - 1, 0, -1):
        got = to_group(after(value, ahead), group, group - 1)
        ahead = next(hops)
        if group == groups - 1:
            ahead = next(hops, ahead)
        leaving.append(after(got, ahead))
        if group > 1:
            value = linked(NN, group_map, pair_sum, leaving, "noise_link")
            noise_step[:] = [value]
            if group < groups - 1:
                ahead = next(hops, ahead)
    for _ in hops:
        pass

    def divide_body(where_ref, map_ref, sum_ref, *refs):
        keep_out, send_out = refs[-2:]
        given = refs[0][...]
        for ref in refs[1:-2]:
            given = given + ref[...]
        between = dot_parts(split(given), parts(map_ref), NN) + sum_ref[...]
        first = (where_ref[1, 0] & (PAIR - 1)) == 0
        keep_out[...] = jnp.where(first, between, given)
        send_out[...] = jnp.where(first, given, between)

    kept_half, sent_half = call(
        divide_body, (samples_half, samples_half), "divide", (where,),
        [high_map, high_sum, *leaving],
    )
    got_half = to_pair(sent_half)

    def terms_body(entering_ref, current_ref, *refs):
        outs = refs[-day_count:]
        given = split(entering_ref[...])
        for day in range(day_count):
            local_ref, inverse_ref, moved_ref = refs[3 * day : 3 * day + 3]
            current = current_ref[day] - dot_parts(given, parts(moved_ref), NT)
            term = dot_parts(split(current), parts(inverse_ref), NN)
            outs[day][...] = local_ref[...] + term[:1]

    terms = call(
        terms_body, [samples_full] * day_count, "mean_terms", (),
        [
            after(mean["entering"], sent_half), currents,
            *(
                value for day in range(day_count)
                for value in (local_terms[day], inverses[day], moveds[day])
            ),
        ],
        work=4,
    )

    def last_body(where_ref, keep_ref, got_ref, back_ref, high_ref, *refs):
        count = len(mean["leaving"])
        got_means, refs = refs[:count], refs[count:]
        map_refs, term_refs = refs[:day_count], refs[day_count : 2 * day_count]
        out_ref, held, sems = refs[2 * day_count :]
        first = (where_ref[1, 0] & (PAIR - 1)) == 0
        given = got_means[0][...]
        for ref in got_means[1:]:
            given = given + ref[...]
        between = dot_parts(split(given), parts(high_ref), NN) + back_ref[...]
        given = jnp.where(first, between, given)
        low = jnp.where(first, keep_ref[...], got_ref[...])
        high = jnp.where(first, got_ref[...], keep_ref[...])
        following = jnp.concatenate([low, high], axis=0) + given[:1]
        copies = []
        for day in reversed(range(day_count)):
            following = dot_parts(split(following), parts(map_refs[day]), NN) + term_refs[day][...]
            held[day] = following.T
            copies.append(pltpu.make_async_copy(held.at[day], out_ref.at[day], sems.at[day]))
            copies[-1].start()
        for copy in copies:
            copy.wait()

    return call(
        last_body, shape(day_count, nodes, columns), "last_days", (where,),
        [
            kept_half, got_half, mean["high_back"], high_map, *mean["leaving"], *step_maps,
            *terms,
        ],
        work=4,
        scratch=[
            pltpu.VMEM((day_count, nodes, columns), F32), pltpu.SemaphoreType.DMA((day_count,)),
        ],
        out_specs=pl.BlockSpec(memory_space=pl.ANY),
    )


def solution(mesh):
    return jax.shard_map(
        local,
        mesh=mesh,
        in_specs=(
            P("tm", "row", None),
            P("tm", "row", None),
            P("tm", None, "row"),
            P(("tm", "row")),
            P(("tm", "row")),
            P(("tm", "row")),
        ),
        out_specs=P("tm", None, "row"),
        check_vma=False,
    )
```

```python
import functools

import jax
import jax.numpy as jnp
from jax import lax
from jax.experimental import pallas as pl
from jax.experimental.pallas import tpu as pltpu
from jax.sharding import PartitionSpec as P

F32 = jnp.float32
BF16 = jnp.bfloat16
CORES = 2
PAIR = 2
LINES = 8

NN = ((1,), (0,))
TN = ((0,), (0,))
NT = ((1,), (1,))


def split(value):
    high = value.astype(BF16)
    return high, (value - high.astype(F32)).astype(BF16)


def parts(ref):
    return ref[0], ref[1]


def dot_parts(left, right, dims):
    product = functools.partial(
        lax.dot_general, dimension_numbers=(dims, ((), ())), preferred_element_type=F32
    )
    return product(left[0], right[0]) + (product(left[0], right[1]) + product(left[1], right[0]))


def shape(*dims, dtype=F32):
    return jax.ShapeDtypeStruct(dims, dtype)


def in_vmem(value):
    return pltpu.with_memory_space_constraint(value, pltpu.VMEM)


def call(body, outs, name, scalars, arrays, work=1, scratch=(), out_specs=None):
    vmem = pl.BlockSpec(memory_space=pltpu.VMEM)
    out_shape = outs if out_specs else jax.tree.map(lambda o: pltpu.VMEM(o.shape, o.dtype), outs)
    return pl.pallas_call(
        body,
        out_shape=out_shape,
        in_specs=[vmem] * (len(scalars) + len(arrays)),
        out_specs=out_specs or jax.tree.map(lambda _: vmem, outs),
        scratch_shapes=list(scratch),
        compiler_params=pltpu.CompilerParams(vmem_limit_bytes=12 * 1024 * 1024),
        cost_estimate=pl.CostEstimate(
            flops=int(work * 2.0e8), transcendentals=0, bytes_accessed=1024
        ),
        name=name,
    )(*map(in_vmem, (*scalars, *arrays)))


def deal(where_ref, distance, total, keep_out, sent_out):
    count = total.shape[0] // 2
    upper = (where_ref[1, 0] & distance) != 0
    keep_out[...] = jnp.where(upper, total[count:], total[:count])
    sent_out[...] = jnp.where(upper, total[:count], total[count:])


def halved(where, distance, keep, got):
    def body(where_ref, keep_ref, got_ref, *outs):
        total = keep_ref[...] + got_ref[...]
        if distance:
            deal(where_ref, distance, total, *outs)
        else:
            outs[0][...] = total

    days, nodes = keep.shape
    outs = [shape(days // 2, nodes)] * 2 if distance else [keep]
    outs = [shape(*out.shape) for out in outs]
    return (*call(body, outs, "halved", (where,), [keep, got], work=0.05), None)[:2]


def bin_observations(where, obs_day, obs_node, obs_value, days, nodes, distance):
    chunk = min(512, obs_day.shape[0])
    chunks = obs_day.shape[0] // chunk

    def body(where_ref, day_ref, node_ref, value_ref, keep_out, sent_out):
        total = jnp.zeros((3 * days, nodes), F32)
        for index in range(chunks):
            row = pl.ds(index, 1)
            value = value_ref[row, :]
            high = value.astype(BF16).astype(F32)
            middle = (value - high).astype(BF16).astype(F32)
            low = value - high - middle
            is_day = lax.broadcasted_iota(jnp.int32, (days, chunk), 0) == day_ref[row, :]
            marked = jnp.concatenate(
                [jnp.where(is_day, part, 0.0).astype(BF16) for part in (high, middle, low)], axis=0
            )
            is_node = lax.broadcasted_iota(jnp.int32, (nodes, chunk), 0) == node_ref[row, :]
            total += lax.dot_general(
                marked, is_node.astype(F32).astype(BF16), (NT, ((), ())), preferred_element_type=F32
            )
        total = total[:days] + (total[days : 2 * days] + total[2 * days :])
        deal(where_ref, distance, total, keep_out, sent_out)

    return call(
        body,
        [shape(days // 2, nodes)] * 2,
        "bin_observations",
        (where,),
        [value.reshape(chunks, chunk) for value in (obs_day, obs_node, obs_value)],
        work=2,
    )


def gather_rows(where_ref, refs, take, out_ref):
    share = refs[0].shape[-2]
    for offset, ref in enumerate(refs):
        at = pl.ds(pl.multiple_of((where_ref[0, 0] ^ offset) * share, share), share)
        if len(ref.shape) == 3:
            ref = ref.at[take(offset) if callable(take) else take]
        out_ref[0, at, :], out_ref[1, at, :] = split(ref[...])


def local(inv_diag, coupling, noise, obs_day, obs_node, obs_value):
    part_count = lax.axis_size("tm")
    row_count = lax.axis_size("row")
    my_part = lax.axis_index("tm")
    my_row = lax.axis_index("row")
    day_count, share, nodes = inv_diag.shape
    columns = noise.shape[2]
    half = columns // PAIR
    half_nodes = nodes // CORES
    groups = part_count // PAIR
    chips = row_count // CORES
    early = day_count // 2
    rest = day_count - 1

    def to_row(value, distance):
        return lax.ppermute(value, "row", [(i, i ^ distance) for i in range(row_count)])

    def to_pair(value):
        return lax.ppermute(value, "tm", [(i, i ^ 1) for i in range(part_count)])

    def to_group(value, source, target):
        return lax.ppermute(
            value, "tm", [(PAIR * source + i, PAIR * target + i) for i in range(PAIR)]
        )

    def after(value, *others):
        return lax.optimization_barrier((value, *others))[0]

    where = jnp.broadcast_to(jnp.stack([my_row, my_part]).astype(jnp.int32)[:, None], (2, 128))

    line = shape(LINES, nodes)
    square = shape(nodes, nodes)
    map_parts = shape(2, nodes, nodes, dtype=BF16)
    samples_half = shape(half, nodes)
    samples_full = shape(columns, nodes)

    keep, sent = bin_observations(
        where, obs_day, obs_node, obs_value, part_count * day_count, nodes, part_count // 2
    )

    def over_chips(rows):
        return [to_row(rows, distance) for distance in range(CORES, row_count, CORES)]

    def shared(arrived, *ahead):
        return [piece for got in arrived for piece in (got, to_row(after(got, *ahead), 1))]

    arrived = []

    def send_rows(*rows):
        for piece in rows:
            if len(arrived) >= 2:
                piece = after(piece, *arrived[len(arrived) - 2][-1])
            pieces.append(over_chips(piece))
        arrived.append(pieces[-len(rows) :])

    pieces = []
    link_rows = [coupling[day : day + 1] for day in range(day_count)]
    for rows in (inv_diag, *link_rows[:-1]):
        send_rows(rows)
    own_inverse = [inv_diag, to_row(inv_diag, 1)]
    own_link = [coupling, to_row(coupling, 1)]
    where = after(where, keep, *link_rows)

    distance = part_count // 2
    while distance:
        got = lax.ppermute(sent, "tm", [(i, i ^ distance) for i in range(part_count)])
        distance //= 2
        keep, sent = halved(where, distance, keep, got)
    right_side = keep + to_row(keep, 1)

    first_rows = share // 2

    def pack_body(rows_ref, source_ref, first_out, rest_out):
        first_out[...] = rows_ref[0, :first_rows, :]
        rest_out[: share - first_rows, :] = rows_ref[0, first_rows:, :]
        rest_out[share - first_rows :, :] = jnp.zeros((LINES, nodes), F32)
        rest_out[share - first_rows : share - first_rows + day_count, :] = source_ref[...]

    packed = call(
        pack_body,
        (shape(first_rows, nodes), shape(share - first_rows + LINES, nodes)),
        "pack",
        (),
        [link_rows[-1], right_side],
        work=0.1,
    )
    send_rows(*packed)
    got_inverses, got_links = pieces[0], pieces[1:]

    def store(out_ref, pair):
        out_ref[0], out_ref[1] = pair

    def inverses_body(where_ref, *refs):
        row_refs, refs = refs[:row_count], refs[row_count:]
        noise_ref, gram_out, outs = refs[0], refs[1], refs[2:]
        for day in range(day_count):
            gather_rows(where_ref, row_refs, lambda offset: day, outs[day])
            outs[day_count + day][...] = dot_parts(
                split(noise_ref[day]), parts(outs[day]), TN
            )
        gram_out[...] = dot_parts(parts(outs[0]), parts(outs[0]), TN)

    gram, *results = call(
        inverses_body,
        [square, *[map_parts] * day_count, *[samples_full] * day_count],
        "inverses",
        (where,),
        [*own_inverse, *shared(got_inverses, where, *packed), noise],
        work=4,
    )
    inverses, local_terms = results[:day_count], results[day_count:]

    def early_body(where_ref, *refs):
        own_refs, refs = refs[:CORES], refs[CORES:]
        count = row_count - CORES
        got_refs, refs = refs[: count * early], refs[count * early :]
        noise_ref, term_ref, refs = refs[0], refs[1], refs[2:]
        inverse_refs, refs = refs[: early + 1], refs[early + 1 :]
        sum_out, *outs = refs
        link_outs, moved_outs, map_outs = outs[:early], outs[early : 2 * early], outs[2 * early :]
        for day in range(early):
            row_refs = (*own_refs, *got_refs[count * day : count * (day + 1)])
            gather_rows(
                where_ref, row_refs, lambda offset: day if offset < CORES else 0, link_outs[day]
            )
        total = term_ref[...]
        moved = parts(inverse_refs[0])
        for day in range(early):
            link = parts(link_outs[day])
            path = split(-dot_parts(link, moved, NN))
            if day == 0:
                store(map_outs[0], path)
            moved = split(dot_parts(parts(inverse_refs[day + 1]), path, NN))
            store(moved_outs[day], moved)
            total = total + dot_parts(split(noise_ref[day + 1]), moved, TN)
        sum_out[...] = total

    summed, *results = call(
        early_body,
        [samples_full, *[map_parts] * (2 * early + 1)],
        "early_days",
        (where,),
        [
            *own_link,
            *(piece for got in got_links[:early] for piece in shared(got, gram)),
            noise, local_terms[0], *inverses[: early + 1],
        ],
        work=6,
    )
    links, step_maps = list(results[:early]), list(results[2 * early :])
    moveds = [inverses[0], *results[early : 2 * early]]

    def next_body(day, where_ref, *refs):
        own_refs, got_refs, refs = refs[:CORES], refs[CORES:row_count], refs[row_count:]
        noise_ref, inverse_ref, sum_ref, moved_ref, link_out, moved_out, *sum_outs = refs
        gather_rows(
            where_ref, (*own_refs, *got_refs), lambda offset: day if offset < CORES else 0, link_out
        )
        path = split(-dot_parts(parts(link_out), parts(moved_ref), NN))
        moved = split(dot_parts(parts(inverse_ref), path, NN))
        store(moved_out, moved)
        total = sum_ref[...] + dot_parts(split(noise_ref[day + 1]), moved, TN)
        if len(sum_outs) == 1:
            sum_outs[0][...] = total
        else:
            first = (where_ref[1, 0] & (PAIR - 1)) == 0
            sum_outs[0][...] = jnp.where(first, total[:half], total[half:])
            sum_outs[1][...] = jnp.where(first, total[half:], total[:half])

    for day in range(early, day_count - 1):
        sums = [samples_half] * 2 if day == day_count - 2 else [samples_full]
        link, moved, *sums = call(
            functools.partial(next_body, day),
            [map_parts, map_parts, *sums],
            f"day_{day}",
            (where,),
            [
                *own_link, *shared(got_links[day], summed), noise, inverses[day + 1],
                summed, moveds[day],
            ],
            work=3,
        )
        summed = sums[0]
        moveds.append(moved)
        links.append(link)
    keep, send = sums
    other_sum = to_pair(send)

    def last_link_body(where_ref, *refs):
        own_refs, refs = refs[:CORES], refs[CORES:]
        count = row_count - CORES
        first_refs, rest_refs, refs = refs[:count], refs[count : 2 * count], refs[2 * count :]
        moved_ref, whole_out, half_out, link_out = refs
        rest_refs = [ref.at[pl.ds(0, share - first_rows)] for ref in rest_refs]
        pairs = [
            (ref.at[day_count - 1, pl.ds(0, first_rows)], ref.at[day_count - 1, pl.ds(first_rows, share - first_rows)])
            for ref in own_refs
        ] + list(zip(first_refs, rest_refs, strict=True))
        for offset, pair in enumerate(pairs):
            for ref, start, size in zip(
                pair, (0, first_rows), (first_rows, share - first_rows), strict=True
            ):
                start = (where_ref[0, 0] ^ offset) * share + start
                at = pl.ds(pl.multiple_of(start, first_rows), size)
                link_out[0, at, :], link_out[1, at, :] = split(ref[...])
        whole_out[...] = -dot_parts(parts(link_out), parts(moved_ref), NN)
        half_out[...] = whole_out[
            pl.ds(pl.multiple_of((where_ref[0, 0] & (CORES - 1)) * half_nodes, half_nodes), half_nodes), :
        ]

    path, path_half, link = call(
        last_link_body,
        (square, shape(half_nodes, nodes), map_parts),
        "last_link",
        (where,),
        [*own_link, *shared(got_links[-2], send), *shared(got_links[-1], send), moveds[-1]],
        work=1.5,
    )
    links.append(link)
    other_half = to_pair(after(path_half, other_sum))

    def lines_body(source_ref, *refs):
        got_refs, refs = refs[: chips - 1], refs[chips - 1 :]
        flux_out, back_out, current_out = refs[-3:]
        source = source_ref[...]
        for ref in got_refs:
            source = source + ref[share - first_rows : share - first_rows + day_count, :]
        applied = jnp.zeros((LINES, nodes), F32)
        back = applied
        for day in range(day_count):
            inverse_ref, link_ref, moved_ref = refs[3 * day : 3 * day + 3]
            wanted = source[day : day + 1] - applied
            current = dot_parts(split(wanted), parts(inverse_ref), NT)
            current_out[day] = current
            current = split(current)
            applied = dot_parts(current, parts(link_ref), NT)
            back = back + dot_parts(current, parts(moved_ref), NN)
        flux_out[...] = applied
        back_out[...] = back

    flux, back, currents = call(
        lines_body,
        (line, line, shape(day_count, LINES, nodes)),
        "lines",
        (),
        [
            right_side,
            *got_links[-1],
            *(
                ref for day in range(day_count)
                for ref in (inverses[day], links[day], moveds[day])
            ),
        ],
        work=5,
    )
    other_flux = to_pair(flux)

    def grams_body(gram_ref, *refs):
        total = gram_ref[...]
        for ref in refs[:-1]:
            total = total + dot_parts(parts(ref), parts(ref), TN)
        store(refs[-1], split(total))

    gram = call(grams_body, map_parts, "grams", (), [after(gram, flux), *moveds[1:]], work=3)

    def late_maps_body(*refs):
        for index in range(rest):
            store(
                refs[2 * rest + index],
                split(-dot_parts(parts(refs[rest + index]), parts(refs[index]), NN)),
            )

    step_maps += call(
        late_maps_body,
        [map_parts] * rest,
        "late_maps",
        (),
        [after(inverses[1], gram), *inverses[2:], *links[1:]],
        work=rest,
    )

    other_rest = to_row(after(other_half, other_flux, *step_maps), 1)

    def pair_body(
        where_ref, path_ref, half_ref, rest_ref, sum_ref, other_ref, flux_ref, other_flux_ref,
        low_out, high_out, sum_out, high_sum_out, flux_out, low_flux_out,
    ):
        first = (where_ref[1, 0] & (PAIR - 1)) == 0
        lead = (where_ref[0, 0] & (CORES - 1)) == 0
        half_rows, rest_rows = half_ref[...], rest_ref[...]
        for at, rows in (
            (slice(0, half_nodes), jnp.where(lead, half_rows, rest_rows)),
            (slice(half_nodes, nodes), jnp.where(lead, rest_rows, half_rows)),
        ):
            own = path_ref[at, :]
            low_out[0, at, :], low_out[1, at, :] = split(jnp.where(first, own, rows))
            high_out[0, at, :], high_out[1, at, :] = split(jnp.where(first, rows, own))
        low_sum = jnp.where(first, sum_ref[...], other_ref[...])
        high_sum = jnp.where(first, other_ref[...], sum_ref[...])
        low_flux = jnp.where(first, flux_ref[...], other_flux_ref[...])
        high_flux = jnp.where(first, other_flux_ref[...], flux_ref[...])
        flux_out[...] = dot_parts(split(low_flux), parts(high_out), NT) + high_flux
        low_flux_out[...] = low_flux
        sum_out[...] = dot_parts(split(high_sum), parts(low_out), NN) + low_sum
        high_sum_out[...] = high_sum

    low_map, high_map, pair_sum, high_sum, pair_flux, low_flux = call(
        pair_body,
        (map_parts, map_parts, samples_half, samples_half, line, line),
        "pair_maps",
        (where,),
        [path, other_half, other_rest, keep, other_sum, flux, other_flux],
        work=1.5,
    )

    def group_map_body(low_ref, high_ref, out_ref):
        store(out_ref, split(dot_parts(parts(high_ref), parts(low_ref), NN)))

    group_map = call(
        group_map_body, map_parts, "group_map", (), [low_map, after(high_map, pair_sum)]
    )

    def link_body(dims, map_ref, local_ref, *refs):
        got = refs[0][...]
        for ref in refs[1:-1]:
            got = got + ref[...]
        refs[-1][...] = dot_parts(split(got), parts(map_ref), dims) + local_ref[...]

    def linked(dims, value_map, value, got, name):
        return call(
            functools.partial(link_body, dims), shape(*value.shape), name, (),
            [value_map, value, *got], work=0.6,
        )

    def added(refs):
        total = refs[0][...]
        for ref in refs[1:]:
            total = total + ref[...]
        return total

    def turn_body(where_ref, low_ref, flux_ref, gram_ref, back_ref, *refs):
        own_out, back_out, part_out = refs[-3:]
        given = added(refs[:-3])
        behind = dot_parts(split(given), parts(low_ref), NT) + flux_ref[...]
        first = (where_ref[1, 0] & (PAIR - 1)) == 0
        given = jnp.where(first, given, behind)
        own_out[...] = given
        own_back = back_ref[...] - dot_parts(split(given), parts(gram_ref), NN)
        back_out[...] = own_back
        part_out[...] = jnp.where(first, own_back, dot_parts(split(own_back), parts(low_ref), NN))

    def first_back_body(where_ref, map_ref, own_ref, other_ref, part_ref, mate_ref, *refs):
        value_out, pair_out, high_out = refs[-3:]
        first = (where_ref[1, 0] & (PAIR - 1)) == 0
        pair_back = part_ref[...] + mate_ref[...]
        pair_out[...] = pair_back
        high_out[...] = jnp.where(first, other_ref[...], own_ref[...])
        value_out[...] = dot_parts(split(added(refs[:-3])), parts(map_ref), NN) + pair_back

    mean = {}
    noise_step = []

    def mean_hops():
        value, got = pair_flux, []
        yield value
        for group in range(groups - 1):
            got.append(to_group(value, group, group + 1))
            if group < groups - 2:
                value = linked(NT, group_map, pair_flux, got, "forward_link")
                yield value
        mean["entering"], own_back, part = call(
            turn_body, (line, line, line), "mean_turn", (where,),
            [low_map, low_flux, gram, back, after(got[0], *noise_step), *got[1:]],
        )
        yield part
        last = PAIR * (groups - 1)
        got = [
            lax.ppermute(part, "tm", [(last + i, last - PAIR + (i ^ cross)) for i in range(PAIR)])
            for cross in range(PAIR)
        ]
        both = to_pair(jnp.concatenate([own_back, part], axis=0))
        value, pair_back, mean["high_back"] = call(
            first_back_body, (line, line, line), "first_back", (where,),
            [
                group_map, after(own_back, *noise_step), both[:LINES], part, both[LINES:], *got,
            ],
            work=0.6,
        )
        mean["leaving"] = got
        for group in range(groups - 2, 0, -1):
            yield value
            got.append(to_group(value, group, group - 1))
            if group > 1:
                gated = [after(got[0], *noise_step), *got[1:]]
                value = linked(NN, group_map, pair_back, gated, "backward_link")
        yield value

    hops = mean_hops()
    ahead = next(hops)

    leaving = []
    value = pair_sum
    for group in range(groups - 1, 0, -1):
        got = to_group(after(value, ahead), group, group - 1)
        ahead = next(hops)
        if group == groups - 1:
            ahead = next(hops, ahead)
        leaving.append(after(got, ahead))
        if group > 1:
            value = linked(NN, group_map, pair_sum, leaving, "noise_link")
            noise_step[:] = [value]
            if group < groups - 1:
                ahead = next(hops, ahead)
    for _ in hops:
        pass

    def divide_body(where_ref, map_ref, sum_ref, *refs):
        keep_out, send_out = refs[-2:]
        given = refs[0][...]
        for ref in refs[1:-2]:
            given = given + ref[...]
        between = dot_parts(split(given), parts(map_ref), NN) + sum_ref[...]
        first = (where_ref[1, 0] & (PAIR - 1)) == 0
        keep_out[...] = jnp.where(first, between, given)
        send_out[...] = jnp.where(first, given, between)

    kept_half, sent_half = call(
        divide_body, (samples_half, samples_half), "divide", (where,),
        [high_map, high_sum, *leaving],
    )
    got_half = to_pair(sent_half)

    def terms_body(entering_ref, current_ref, *refs):
        outs = refs[-day_count:]
        given = split(entering_ref[...])
        for day in range(day_count):
            local_ref, inverse_ref, moved_ref = refs[3 * day : 3 * day + 3]
            current = current_ref[day] - dot_parts(given, parts(moved_ref), NT)
            term = dot_parts(split(current), parts(inverse_ref), NN)
            outs[day][...] = local_ref[...] + term[:1]

    terms = call(
        terms_body, [samples_full] * day_count, "mean_terms", (),
        [
            after(mean["entering"], sent_half), currents,
            *(
                value for day in range(day_count)
                for value in (local_terms[day], inverses[day], moveds[day])
            ),
        ],
        work=4,
    )

    def last_body(where_ref, keep_ref, got_ref, back_ref, high_ref, *refs):
        count = len(mean["leaving"])
        got_means, refs = refs[:count], refs[count:]
        map_refs, term_refs = refs[:day_count], refs[day_count : 2 * day_count]
        out_ref, held, sems = refs[2 * day_count :]
        first = (where_ref[1, 0] & (PAIR - 1)) == 0
        given = got_means[0][...]
        for ref in got_means[1:]:
            given = given + ref[...]
        between = dot_parts(split(given), parts(high_ref), NN) + back_ref[...]
        given = jnp.where(first, between, given)
        low = jnp.where(first, keep_ref[...], got_ref[...])
        high = jnp.where(first, got_ref[...], keep_ref[...])
        following = jnp.concatenate([low, high], axis=0) + given[:1]
        copies = []
        for day in reversed(range(day_count)):
            following = dot_parts(split(following), parts(map_refs[day]), NN) + term_refs[day][...]
            held[day] = following.T
            copies.append(pltpu.make_async_copy(held.at[day], out_ref.at[day], sems.at[day]))
            copies[-1].start()
        for copy in copies:
            copy.wait()

    return call(
        last_body, shape(day_count, nodes, columns), "last_days", (where,),
        [
            kept_half, got_half, mean["high_back"], high_map, *mean["leaving"], *step_maps,
            *terms,
        ],
        work=4,
        scratch=[
            pltpu.VMEM((day_count, nodes, columns), F32), pltpu.SemaphoreType.DMA((day_count,)),
        ],
        out_specs=pl.BlockSpec(memory_space=pl.ANY),
    )


def solution(mesh):
    return jax.shard_map(
        local,
        mesh=mesh,
        in_specs=(
            P("tm", "row", None),
            P("tm", "row", None),
            P("tm", None, "row"),
            P(("tm", "row")),
            P(("tm", "row")),
            P(("tm", "row")),
        ),
        out_specs=P("tm", None, "row"),
        check_vma=False,
    )
```

```python
import functools

import jax
import jax.numpy as jnp
from jax import lax
from jax.experimental import pallas as pl
from jax.experimental.pallas import tpu as pltpu
from jax.sharding import PartitionSpec as P

F32 = jnp.float32
BF16 = jnp.bfloat16
CORES = 2
PAIR = 2
LINES = 8

NN = ((1,), (0,))
TN = ((0,), (0,))
NT = ((1,), (1,))


def split(value):
    high = value.astype(BF16)
    return high, (value - high.astype(F32)).astype(BF16)


def parts(ref):
    return ref[0], ref[1]


def dot_parts(left, right, dims):
    product = functools.partial(
        lax.dot_general, dimension_numbers=(dims, ((), ())), preferred_element_type=F32
    )
    return product(left[0], right[0]) + (product(left[0], right[1]) + product(left[1], right[0]))


def shape(*dims, dtype=F32):
    return jax.ShapeDtypeStruct(dims, dtype)


def in_vmem(value):
    return pltpu.with_memory_space_constraint(value, pltpu.VMEM)


def call(body, outs, name, scalars, arrays, work=1, scratch=(), out_specs=None):
    vmem = pl.BlockSpec(memory_space=pltpu.VMEM)
    out_shape = outs if out_specs else jax.tree.map(lambda o: pltpu.VMEM(o.shape, o.dtype), outs)
    return pl.pallas_call(
        body,
        out_shape=out_shape,
        in_specs=[vmem] * (len(scalars) + len(arrays)),
        out_specs=out_specs or jax.tree.map(lambda _: vmem, outs),
        scratch_shapes=list(scratch),
        compiler_params=pltpu.CompilerParams(vmem_limit_bytes=12 * 1024 * 1024),
        cost_estimate=pl.CostEstimate(
            flops=int(work * 2.0e8), transcendentals=0, bytes_accessed=1024
        ),
        name=name,
    )(*map(in_vmem, (*scalars, *arrays)))


def deal(where_ref, distance, total, keep_out, sent_out):
    count = total.shape[0] // 2
    upper = (where_ref[1, 0] & distance) != 0
    keep_out[...] = jnp.where(upper, total[count:], total[:count])
    sent_out[...] = jnp.where(upper, total[:count], total[count:])


def halved(where, distance, keep, got):
    def body(where_ref, keep_ref, got_ref, *outs):
        total = keep_ref[...] + got_ref[...]
        if distance:
            deal(where_ref, distance, total, *outs)
        else:
            outs[0][...] = total

    days, nodes = keep.shape
    outs = [shape(days // 2, nodes)] * 2 if distance else [keep]
    outs = [shape(*out.shape) for out in outs]
    return (*call(body, outs, "halved", (where,), [keep, got], work=0.05), None)[:2]


def bin_observations(where, obs_day, obs_node, obs_value, days, nodes, distance):
    chunk = min(512, obs_day.shape[0])
    chunks = obs_day.shape[0] // chunk

    def body(where_ref, day_ref, node_ref, value_ref, keep_out, sent_out):
        total = jnp.zeros((3 * days, nodes), F32)
        for index in range(chunks):
            row = pl.ds(index, 1)
            value = value_ref[row, :]
            high = value.astype(BF16).astype(F32)
            middle = (value - high).astype(BF16).astype(F32)
            low = value - high - middle
            is_day = lax.broadcasted_iota(jnp.int32, (days, chunk), 0) == day_ref[row, :]
            marked = jnp.concatenate(
                [jnp.where(is_day, part, 0.0).astype(BF16) for part in (high, middle, low)], axis=0
            )
            is_node = lax.broadcasted_iota(jnp.int32, (nodes, chunk), 0) == node_ref[row, :]
            total += lax.dot_general(
                marked, is_node.astype(F32).astype(BF16), (NT, ((), ())), preferred_element_type=F32
            )
        total = total[:days] + (total[days : 2 * days] + total[2 * days :])
        deal(where_ref, distance, total, keep_out, sent_out)

    return call(
        body,
        [shape(days // 2, nodes)] * 2,
        "bin_observations",
        (where,),
        [value.reshape(chunks, chunk) for value in (obs_day, obs_node, obs_value)],
        work=2,
    )


def gather_rows(where_ref, refs, take, out_ref):
    share = refs[0].shape[-2]
    for offset, ref in enumerate(refs):
        at = pl.ds(pl.multiple_of((where_ref[0, 0] ^ offset) * share, share), share)
        if len(ref.shape) == 3:
            ref = ref.at[take(offset) if callable(take) else take]
        out_ref[0, at, :], out_ref[1, at, :] = split(ref[...])


def gather_halves(where_ref, own_refs, day, first_refs, rest_refs, out_ref):
    share = own_refs[0].shape[-2]
    count = share // 2
    halves = [(ref.at[day, pl.ds(0, count)], ref.at[day, pl.ds(count, count)]) for ref in own_refs]
    halves += zip(first_refs, rest_refs, strict=True)
    for offset, pair in enumerate(halves):
        for index, ref in enumerate(pair):
            start = (where_ref[0, 0] ^ offset) * share + index * count
            at = pl.ds(pl.multiple_of(start, count), count)
            out_ref[0, at, :], out_ref[1, at, :] = split(ref[...])


def local(inv_diag, coupling, noise, obs_day, obs_node, obs_value):
    part_count = lax.axis_size("tm")
    row_count = lax.axis_size("row")
    my_part = lax.axis_index("tm")
    my_row = lax.axis_index("row")
    day_count, share, nodes = inv_diag.shape
    columns = noise.shape[2]
    half = columns // PAIR
    half_nodes = nodes // CORES
    groups = part_count // PAIR
    chips = row_count // CORES
    early = day_count // 2
    rest = day_count - 1

    def to_row(value, distance):
        return lax.ppermute(value, "row", [(i, i ^ distance) for i in range(row_count)])

    def to_pair(value):
        return lax.ppermute(value, "tm", [(i, i ^ 1) for i in range(part_count)])

    def to_group(value, source, target):
        return lax.ppermute(
            value, "tm", [(PAIR * source + i, PAIR * target + i) for i in range(PAIR)]
        )

    def after(value, *others):
        return lax.optimization_barrier((value, *others))[0]

    where = jnp.broadcast_to(jnp.stack([my_row, my_part]).astype(jnp.int32)[:, None], (2, 128))

    line = shape(LINES, nodes)
    square = shape(nodes, nodes)
    map_parts = shape(2, nodes, nodes, dtype=BF16)
    samples_half = shape(half, nodes)
    samples_full = shape(columns, nodes)

    keep, sent = bin_observations(
        where, obs_day, obs_node, obs_value, part_count * day_count, nodes, part_count // 2
    )

    def over_chips(rows):
        return [to_row(rows, distance) for distance in range(CORES, row_count, CORES)]

    def shared(arrived, *ahead):
        return [piece for got in arrived for piece in (got, to_row(after(got, *ahead), 1))]

    arrived = []

    def send_rows(*rows):
        for piece in rows:
            if len(arrived) >= 2:
                piece = after(piece, *arrived[len(arrived) - 2][-1])
            pieces.append(over_chips(piece))
        arrived.append(pieces[-len(rows) :])

    pieces = []
    link_rows = [coupling[day : day + 1] for day in range(day_count)]
    first_rows = share // 2
    for rows in (inv_diag, *link_rows[:-1]):
        if rows is link_rows[early - 1]:
            send_rows(rows[0, :first_rows], rows[0, first_rows:])
        else:
            send_rows(rows)
    own_inverse = [inv_diag, to_row(inv_diag, 1)]
    own_link = [coupling, to_row(coupling, 1)]
    where = after(where, keep, *link_rows)

    distance = part_count // 2
    while distance:
        got = lax.ppermute(sent, "tm", [(i, i ^ distance) for i in range(part_count)])
        distance //= 2
        keep, sent = halved(where, distance, keep, got)
    right_side = keep + to_row(keep, 1)

    def pack_body(rows_ref, source_ref, first_out, rest_out):
        first_out[...] = rows_ref[0, :first_rows, :]
        rest_out[: share - first_rows, :] = rows_ref[0, first_rows:, :]
        rest_out[share - first_rows :, :] = jnp.zeros((LINES, nodes), F32)
        rest_out[share - first_rows : share - first_rows + day_count, :] = source_ref[...]

    packed = call(
        pack_body,
        (shape(first_rows, nodes), shape(share - first_rows + LINES, nodes)),
        "pack",
        (),
        [link_rows[-1], right_side],
        work=0.1,
    )
    send_rows(*packed)
    got_inverses, *got_links = pieces
    halved_day = got_links.pop(early)

    def store(out_ref, pair):
        out_ref[0], out_ref[1] = pair

    def inverses_body(where_ref, *refs):
        row_refs, refs = refs[:row_count], refs[row_count:]
        noise_ref, gram_out, outs = refs[0], refs[1], refs[2:]
        for day in range(day_count):
            gather_rows(where_ref, row_refs, lambda offset: day, outs[day])
            outs[day_count + day][...] = dot_parts(
                split(noise_ref[day]), parts(outs[day]), TN
            )
        gram_out[...] = dot_parts(parts(outs[0]), parts(outs[0]), TN)

    gram, *results = call(
        inverses_body,
        [square, *[map_parts] * day_count, *[samples_full] * day_count],
        "inverses",
        (where,),
        [*own_inverse, *shared(got_inverses, where, *packed), noise],
        work=4,
    )
    inverses, local_terms = results[:day_count], results[day_count:]

    def early_body(where_ref, *refs):
        own_refs, refs = refs[:CORES], refs[CORES:]
        count = row_count - CORES
        got_refs, refs = refs[: count * (early + 1)], refs[count * (early + 1) :]
        noise_ref, term_ref, refs = refs[0], refs[1], refs[2:]
        inverse_refs, refs = refs[: early + 1], refs[early + 1 :]
        sum_out, *outs = refs
        link_outs, moved_outs, map_outs = outs[:early], outs[early : 2 * early], outs[2 * early :]
        for day in range(early):
            got = got_refs[count * day : count * (day + 1)]
            if day < early - 1:
                gather_rows(
                    where_ref,
                    (*own_refs, *got),
                    lambda offset: day if offset < CORES else 0,
                    link_outs[day],
                )
            else:
                gather_halves(where_ref, own_refs, day, got, got_refs[count * early :], link_outs[day])
        total = term_ref[...]
        moved = parts(inverse_refs[0])
        for day in range(early):
            link = parts(link_outs[day])
            path = split(-dot_parts(link, moved, NN))
            if day == 0:
                store(map_outs[0], path)
            moved = split(dot_parts(parts(inverse_refs[day + 1]), path, NN))
            store(moved_outs[day], moved)
            total = total + dot_parts(split(noise_ref[day + 1]), moved, TN)
        sum_out[...] = total

    summed, *results = call(
        early_body,
        [samples_full, *[map_parts] * (2 * early + 1)],
        "early_days",
        (where,),
        [
            *own_link,
            *(piece for got in (*got_links[:early], halved_day) for piece in shared(got, gram)),
            noise, local_terms[0], *inverses[: early + 1],
        ],
        work=6,
    )
    links, step_maps = list(results[:early]), list(results[2 * early :])
    moveds = [inverses[0], *results[early : 2 * early]]

    def next_body(day, where_ref, *refs):
        own_refs, got_refs, refs = refs[:CORES], refs[CORES:row_count], refs[row_count:]
        noise_ref, inverse_ref, sum_ref, moved_ref, link_out, moved_out, *sum_outs = refs
        gather_rows(
            where_ref, (*own_refs, *got_refs), lambda offset: day if offset < CORES else 0, link_out
        )
        path = split(-dot_parts(parts(link_out), parts(moved_ref), NN))
        moved = split(dot_parts(parts(inverse_ref), path, NN))
        store(moved_out, moved)
        total = sum_ref[...] + dot_parts(split(noise_ref[day + 1]), moved, TN)
        if len(sum_outs) == 1:
            sum_outs[0][...] = total
        else:
            first = (where_ref[1, 0] & (PAIR - 1)) == 0
            sum_outs[0][...] = jnp.where(first, total[:half], total[half:])
            sum_outs[1][...] = jnp.where(first, total[half:], total[:half])

    for day in range(early, day_count - 1):
        sums = [samples_half] * 2 if day == day_count - 2 else [samples_full]
        link, moved, *sums = call(
            functools.partial(next_body, day),
            [map_parts, map_parts, *sums],
            f"day_{day}",
            (where,),
            [
                *own_link, *shared(got_links[day], summed), noise, inverses[day + 1],
                summed, moveds[day],
            ],
            work=3,
        )
        summed = sums[0]
        moveds.append(moved)
        links.append(link)
    keep, send = sums
    other_sum = to_pair(send)

    def last_link_body(where_ref, *refs):
        own_refs, refs = refs[:CORES], refs[CORES:]
        count = row_count - CORES
        first_refs, rest_refs, refs = refs[:count], refs[count : 2 * count], refs[2 * count :]
        moved_ref, whole_out, half_out, link_out = refs
        rest_refs = [ref.at[pl.ds(0, share - first_rows)] for ref in rest_refs]
        gather_halves(where_ref, own_refs, day_count - 1, first_refs, rest_refs, link_out)
        whole_out[...] = -dot_parts(parts(link_out), parts(moved_ref), NN)
        half_out[...] = whole_out[
            pl.ds(pl.multiple_of((where_ref[0, 0] & (CORES - 1)) * half_nodes, half_nodes), half_nodes), :
        ]

    path, path_half, link = call(
        last_link_body,
        (square, shape(half_nodes, nodes), map_parts),
        "last_link",
        (where,),
        [*own_link, *shared(got_links[-2], send), *shared(got_links[-1], send), moveds[-1]],
        work=1.5,
    )
    links.append(link)
    other_half = to_pair(after(path_half, other_sum))

    def lines_body(source_ref, *refs):
        got_refs, refs = refs[: chips - 1], refs[chips - 1 :]
        flux_out, back_out, current_out = refs[-3:]
        source = source_ref[...]
        for ref in got_refs:
            source = source + ref[share - first_rows : share - first_rows + day_count, :]
        applied = jnp.zeros((LINES, nodes), F32)
        back = applied
        for day in range(day_count):
            inverse_ref, link_ref, moved_ref = refs[3 * day : 3 * day + 3]
            wanted = source[day : day + 1] - applied
            current = dot_parts(split(wanted), parts(inverse_ref), NT)
            current_out[day] = current
            current = split(current)
            applied = dot_parts(current, parts(link_ref), NT)
            back = back + dot_parts(current, parts(moved_ref), NN)
        flux_out[...] = applied
        back_out[...] = back

    flux, back, currents = call(
        lines_body,
        (line, line, shape(day_count, LINES, nodes)),
        "lines",
        (),
        [
            right_side,
            *got_links[-1],
            *(
                ref for day in range(day_count)
                for ref in (inverses[day], links[day], moveds[day])
            ),
        ],
        work=5,
    )
    other_flux = to_pair(flux)

    def grams_body(gram_ref, *refs):
        total = gram_ref[...]
        for ref in refs[:-1]:
            total = total + dot_parts(parts(ref), parts(ref), TN)
        store(refs[-1], split(total))

    gram = call(grams_body, map_parts, "grams", (), [after(gram, flux), *moveds[1:]], work=3)

    def late_maps_body(*refs):
        for index in range(rest):
            store(
                refs[2 * rest + index],
                split(-dot_parts(parts(refs[rest + index]), parts(refs[index]), NN)),
            )

    step_maps += call(
        late_maps_body,
        [map_parts] * rest,
        "late_maps",
        (),
        [after(inverses[1], gram), *inverses[2:], *links[1:]],
        work=rest,
    )

    other_rest = to_row(after(other_half, other_flux, *step_maps), 1)

    def pair_body(
        where_ref, path_ref, half_ref, rest_ref, sum_ref, other_ref, flux_ref, other_flux_ref,
        low_out, high_out, sum_out, high_sum_out, flux_out, low_flux_out,
    ):
        first = (where_ref[1, 0] & (PAIR - 1)) == 0
        lead = (where_ref[0, 0] & (CORES - 1)) == 0
        half_rows, rest_rows = half_ref[...], rest_ref[...]
        for at, rows in (
            (slice(0, half_nodes), jnp.where(lead, half_rows, rest_rows)),
            (slice(half_nodes, nodes), jnp.where(lead, rest_rows, half_rows)),
        ):
            own = path_ref[at, :]
            low_out[0, at, :], low_out[1, at, :] = split(jnp.where(first, own, rows))
            high_out[0, at, :], high_out[1, at, :] = split(jnp.where(first, rows, own))
        low_sum = jnp.where(first, sum_ref[...], other_ref[...])
        high_sum = jnp.where(first, other_ref[...], sum_ref[...])
        low_flux = jnp.where(first, flux_ref[...], other_flux_ref[...])
        high_flux = jnp.where(first, other_flux_ref[...], flux_ref[...])
        flux_out[...] = dot_parts(split(low_flux), parts(high_out), NT) + high_flux
        low_flux_out[...] = low_flux
        sum_out[...] = dot_parts(split(high_sum), parts(low_out), NN) + low_sum
        high_sum_out[...] = high_sum

    low_map, high_map, pair_sum, high_sum, pair_flux, low_flux = call(
        pair_body,
        (map_parts, map_parts, samples_half, samples_half, line, line),
        "pair_maps",
        (where,),
        [path, other_half, other_rest, keep, other_sum, flux, other_flux],
        work=1.5,
    )

    def group_map_body(low_ref, high_ref, out_ref):
        store(out_ref, split(dot_parts(parts(high_ref), parts(low_ref), NN)))

    group_map = call(
        group_map_body, map_parts, "group_map", (), [low_map, after(high_map, pair_sum)]
    )

    def link_body(dims, map_ref, local_ref, *refs):
        got = refs[0][...]
        for ref in refs[1:-1]:
            got = got + ref[...]
        refs[-1][...] = dot_parts(split(got), parts(map_ref), dims) + local_ref[...]

    def linked(dims, value_map, value, got, name):
        return call(
            functools.partial(link_body, dims), shape(*value.shape), name, (),
            [value_map, value, *got], work=0.6,
        )

    def added(refs):
        total = refs[0][...]
        for ref in refs[1:]:
            total = total + ref[...]
        return total

    def turn_body(where_ref, low_ref, flux_ref, gram_ref, back_ref, *refs):
        own_out, back_out, part_out = refs[-3:]
        given = added(refs[:-3])
        behind = dot_parts(split(given), parts(low_ref), NT) + flux_ref[...]
        first = (where_ref[1, 0] & (PAIR - 1)) == 0
        given = jnp.where(first, given, behind)
        own_out[...] = given
        own_back = back_ref[...] - dot_parts(split(given), parts(gram_ref), NN)
        back_out[...] = own_back
        part_out[...] = jnp.where(first, own_back, dot_parts(split(own_back), parts(low_ref), NN))

    def first_back_body(where_ref, map_ref, own_ref, other_ref, part_ref, mate_ref, *refs):
        value_out, pair_out, high_out = refs[-3:]
        first = (where_ref[1, 0] & (PAIR - 1)) == 0
        pair_back = part_ref[...] + mate_ref[...]
        pair_out[...] = pair_back
        high_out[...] = jnp.where(first, other_ref[...], own_ref[...])
        value_out[...] = dot_parts(split(added(refs[:-3])), parts(map_ref), NN) + pair_back

    mean = {}
    noise_step = []

    def mean_hops():
        value, got = pair_flux, []
        yield value
        for group in range(groups - 1):
            got.append(to_group(value, group, group + 1))
            if group < groups - 2:
                value = linked(NT, group_map, pair_flux, got, "forward_link")
                yield value
        mean["entering"], own_back, part = call(
            turn_body, (line, line, line), "mean_turn", (where,),
            [low_map, low_flux, gram, back, after(got[0], *noise_step), *got[1:]],
        )
        yield part
        last = PAIR * (groups - 1)
        got = [
            lax.ppermute(part, "tm", [(last + i, last - PAIR + (i ^ cross)) for i in range(PAIR)])
            for cross in range(PAIR)
        ]
        both = to_pair(jnp.concatenate([own_back, part], axis=0))
        value, pair_back, mean["high_back"] = call(
            first_back_body, (line, line, line), "first_back", (where,),
            [
                group_map, after(own_back, *noise_step), both[:LINES], part, both[LINES:], *got,
            ],
            work=0.6,
        )
        mean["leaving"] = got
        for group in range(groups - 2, 0, -1):
            yield value
            got.append(to_group(value, group, group - 1))
            if group > 1:
                gated = [after(got[0], *noise_step), *got[1:]]
                value = linked(NN, group_map, pair_back, gated, "backward_link")
        yield value

    hops = mean_hops()
    ahead = next(hops)

    leaving = []
    value = pair_sum
    for group in range(groups - 1, 0, -1):
        got = to_group(after(value, ahead), group, group - 1)
        ahead = next(hops)
        if group == groups - 1:
            ahead = next(hops, ahead)
        leaving.append(after(got, ahead))
        if group > 1:
            value = linked(NN, group_map, pair_sum, leaving, "noise_link")
            noise_step[:] = [value]
            if group < groups - 1:
                ahead = next(hops, ahead)
    for _ in hops:
        pass

    def divide_body(where_ref, map_ref, sum_ref, *refs):
        keep_out, send_out = refs[-2:]
        given = refs[0][...]
        for ref in refs[1:-2]:
            given = given + ref[...]
        between = dot_parts(split(given), parts(map_ref), NN) + sum_ref[...]
        first = (where_ref[1, 0] & (PAIR - 1)) == 0
        keep_out[...] = jnp.where(first, between, given)
        send_out[...] = jnp.where(first, given, between)

    kept_half, sent_half = call(
        divide_body, (samples_half, samples_half), "divide", (where,),
        [high_map, high_sum, *leaving],
    )
    got_half = to_pair(sent_half)

    def terms_body(entering_ref, current_ref, *refs):
        outs = refs[-day_count:]
        given = split(entering_ref[...])
        for day in range(day_count):
            local_ref, inverse_ref, moved_ref = refs[3 * day : 3 * day + 3]
            current = current_ref[day] - dot_parts(given, parts(moved_ref), NT)
            term = dot_parts(split(current), parts(inverse_ref), NN)
            outs[day][...] = local_ref[...] + term[:1]

    terms = call(
        terms_body, [samples_full] * day_count, "mean_terms", (),
        [
            after(mean["entering"], sent_half), currents,
            *(
                value for day in range(day_count)
                for value in (local_terms[day], inverses[day], moveds[day])
            ),
        ],
        work=4,
    )

    def last_body(where_ref, keep_ref, got_ref, back_ref, high_ref, *refs):
        count = len(mean["leaving"])
        got_means, refs = refs[:count], refs[count:]
        map_refs, term_refs = refs[:day_count], refs[day_count : 2 * day_count]
        out_ref, held, sems = refs[2 * day_count :]
        first = (where_ref[1, 0] & (PAIR - 1)) == 0
        given = got_means[0][...]
        for ref in got_means[1:]:
            given = given + ref[...]
        between = dot_parts(split(given), parts(high_ref), NN) + back_ref[...]
        given = jnp.where(first, between, given)
        low = jnp.where(first, keep_ref[...], got_ref[...])
        high = jnp.where(first, got_ref[...], keep_ref[...])
        following = jnp.concatenate([low, high], axis=0) + given[:1]
        copies = []
        for day in reversed(range(day_count)):
            following = dot_parts(split(following), parts(map_refs[day]), NN) + term_refs[day][...]
            held[day] = following.T
            copies.append(pltpu.make_async_copy(held.at[day], out_ref.at[day], sems.at[day]))
            copies[-1].start()
        for copy in copies:
            copy.wait()

    return call(
        last_body, shape(day_count, nodes, columns), "last_days", (where,),
        [
            kept_half, got_half, mean["high_back"], high_map, *mean["leaving"], *step_maps,
            *terms,
        ],
        work=4,
        scratch=[
            pltpu.VMEM((day_count, nodes, columns), F32), pltpu.SemaphoreType.DMA((day_count,)),
        ],
        out_specs=pl.BlockSpec(memory_space=pl.ANY),
    )


def solution(mesh):
    return jax.shard_map(
        local,
        mesh=mesh,
        in_specs=(
            P("tm", "row", None),
            P("tm", "row", None),
            P("tm", None, "row"),
            P(("tm", "row")),
            P(("tm", "row")),
            P(("tm", "row")),
        ),
        out_specs=P("tm", None, "row"),
        check_vma=False,
    )
```

```python
import functools

import jax
import jax.numpy as jnp
from jax import lax
from jax.experimental import pallas as pl
from jax.experimental.pallas import tpu as pltpu
from jax.sharding import PartitionSpec as P

F32 = jnp.float32
BF16 = jnp.bfloat16
CORES = 2
PAIR = 2
LINES = 8

NN = ((1,), (0,))
TN = ((0,), (0,))
NT = ((1,), (1,))


def split(value):
    high = value.astype(BF16)
    return high, (value - high.astype(F32)).astype(BF16)


def parts(ref):
    return ref[0], ref[1]


def dot_parts(left, right, dims):
    product = functools.partial(
        lax.dot_general, dimension_numbers=(dims, ((), ())), preferred_element_type=F32
    )
    return product(left[0], right[0]) + (product(left[0], right[1]) + product(left[1], right[0]))


def shape(*dims, dtype=F32):
    return jax.ShapeDtypeStruct(dims, dtype)


def in_vmem(value):
    return pltpu.with_memory_space_constraint(value, pltpu.VMEM)


def call(body, outs, name, scalars, arrays, work=1, scratch=(), out_specs=None):
    vmem = pl.BlockSpec(memory_space=pltpu.VMEM)
    out_shape = outs if out_specs else jax.tree.map(lambda o: pltpu.VMEM(o.shape, o.dtype), outs)
    return pl.pallas_call(
        body,
        out_shape=out_shape,
        in_specs=[vmem] * (len(scalars) + len(arrays)),
        out_specs=out_specs or jax.tree.map(lambda _: vmem, outs),
        scratch_shapes=list(scratch),
        compiler_params=pltpu.CompilerParams(vmem_limit_bytes=12 * 1024 * 1024),
        cost_estimate=pl.CostEstimate(
            flops=int(work * 2.0e8), transcendentals=0, bytes_accessed=1024
        ),
        name=name,
    )(*map(in_vmem, (*scalars, *arrays)))


def deal(where_ref, distance, total, keep_out, sent_out):
    count = total.shape[0] // 2
    upper = (where_ref[1, 0] & distance) != 0
    keep_out[...] = jnp.where(upper, total[count:], total[:count])
    sent_out[...] = jnp.where(upper, total[:count], total[count:])


def halved(where, distance, keep, got):
    def body(where_ref, keep_ref, got_ref, *outs):
        total = keep_ref[...] + got_ref[...]
        if distance:
            deal(where_ref, distance, total, *outs)
        else:
            outs[0][...] = total

    days, nodes = keep.shape
    outs = [shape(days // 2, nodes)] * 2 if distance else [keep]
    outs = [shape(*out.shape) for out in outs]
    return (*call(body, outs, "halved", (where,), [keep, got], work=0.05), None)[:2]


def bin_observations(where, obs_day, obs_node, obs_value, days, nodes, distance):
    chunk = min(512, obs_day.shape[0])
    chunks = obs_day.shape[0] // chunk

    def body(where_ref, day_ref, node_ref, value_ref, keep_out, sent_out):
        total = jnp.zeros((3 * days, nodes), F32)
        for index in range(chunks):
            row = pl.ds(index, 1)
            value = value_ref[row, :]
            high = value.astype(BF16).astype(F32)
            middle = (value - high).astype(BF16).astype(F32)
            low = value - high - middle
            is_day = lax.broadcasted_iota(jnp.int32, (days, chunk), 0) == day_ref[row, :]
            marked = jnp.concatenate(
                [jnp.where(is_day, part, 0.0).astype(BF16) for part in (high, middle, low)], axis=0
            )
            is_node = lax.broadcasted_iota(jnp.int32, (nodes, chunk), 0) == node_ref[row, :]
            total += lax.dot_general(
                marked, is_node.astype(F32).astype(BF16), (NT, ((), ())), preferred_element_type=F32
            )
        total = total[:days] + (total[days : 2 * days] + total[2 * days :])
        deal(where_ref, distance, total, keep_out, sent_out)

    return call(
        body,
        [shape(days // 2, nodes)] * 2,
        "bin_observations",
        (where,),
        [value.reshape(chunks, chunk) for value in (obs_day, obs_node, obs_value)],
        work=2,
    )


def gather_rows(where_ref, refs, take, out_ref):
    share = refs[0].shape[-2]
    for offset, ref in enumerate(refs):
        at = pl.ds(pl.multiple_of((where_ref[0, 0] ^ offset) * share, share), share)
        if len(ref.shape) == 3:
            ref = ref.at[take(offset) if callable(take) else take]
        out_ref[0, at, :], out_ref[1, at, :] = split(ref[...])


def gather_halves(where_ref, own_refs, day, first_refs, rest_refs, out_ref):
    share = own_refs[0].shape[-2]
    count = share // 2
    halves = [(ref.at[day, pl.ds(0, count)], ref.at[day, pl.ds(count, count)]) for ref in own_refs]
    halves += zip(first_refs, rest_refs, strict=True)
    for offset, pair in enumerate(halves):
        for index, ref in enumerate(pair):
            start = (where_ref[0, 0] ^ offset) * share + index * count
            at = pl.ds(pl.multiple_of(start, count), count)
            out_ref[0, at, :], out_ref[1, at, :] = split(ref[...])


def local(inv_diag, coupling, noise, obs_day, obs_node, obs_value):
    part_count = lax.axis_size("tm")
    row_count = lax.axis_size("row")
    my_part = lax.axis_index("tm")
    my_row = lax.axis_index("row")
    day_count, share, nodes = inv_diag.shape
    columns = noise.shape[2]
    half = columns // PAIR
    half_nodes = nodes // CORES
    groups = part_count // PAIR
    chips = row_count // CORES
    early = day_count // 2
    rest = day_count - 1

    def to_row(value, distance):
        return lax.ppermute(value, "row", [(i, i ^ distance) for i in range(row_count)])

    def to_pair(value):
        return lax.ppermute(value, "tm", [(i, i ^ 1) for i in range(part_count)])

    def to_group(value, source, target):
        return lax.ppermute(
            value, "tm", [(PAIR * source + i, PAIR * target + i) for i in range(PAIR)]
        )

    def after(value, *others):
        return lax.optimization_barrier((value, *others))[0]

    where = jnp.broadcast_to(jnp.stack([my_row, my_part]).astype(jnp.int32)[:, None], (2, 128))

    line = shape(LINES, nodes)
    square = shape(nodes, nodes)
    map_parts = shape(2, nodes, nodes, dtype=BF16)
    samples_half = shape(half, nodes)
    samples_full = shape(columns, nodes)

    keep, sent = bin_observations(
        where, obs_day, obs_node, obs_value, part_count * day_count, nodes, part_count // 2
    )

    def over_chips(rows):
        return [to_row(rows, distance) for distance in range(CORES, row_count, CORES)]

    def shared(arrived, *ahead):
        return [piece for got in arrived for piece in (got, to_row(after(got, *ahead), 1))]

    arrived = []

    def send_rows(*rows):
        for piece in rows:
            if len(arrived) >= 2:
                piece = after(piece, *arrived[len(arrived) - 2][-1])
            pieces.append(over_chips(piece))
        arrived.append(pieces[-len(rows) :])

    pieces = []
    link_rows = [coupling[day : day + 1] for day in range(day_count)]
    first_rows = share // 2
    for rows in (inv_diag, *link_rows[:-1]):
        if rows is link_rows[early - 1]:
            send_rows(rows[0, :first_rows], rows[0, first_rows:])
        else:
            send_rows(rows)
    own_inverse = [inv_diag, to_row(inv_diag, 1)]
    own_link = [coupling, to_row(coupling, 1)]
    where = after(where, keep, *link_rows)

    distance = part_count // 2
    while distance:
        got = lax.ppermute(sent, "tm", [(i, i ^ distance) for i in range(part_count)])
        distance //= 2
        keep, sent = halved(where, distance, keep, got)
    right_side = keep + to_row(keep, 1)

    def pack_body(rows_ref, source_ref, first_out, rest_out):
        first_out[...] = rows_ref[0, :first_rows, :]
        rest_out[: share - first_rows, :] = rows_ref[0, first_rows:, :]
        rest_out[share - first_rows :, :] = jnp.zeros((LINES, nodes), F32)
        rest_out[share - first_rows : share - first_rows + day_count, :] = source_ref[...]

    packed = call(
        pack_body,
        (shape(first_rows, nodes), shape(share - first_rows + LINES, nodes)),
        "pack",
        (),
        [link_rows[-1], right_side],
        work=0.1,
    )
    send_rows(*packed)
    got_inverses, *got_links = pieces
    halved_day = got_links.pop(early)

    def store(out_ref, pair):
        out_ref[0], out_ref[1] = pair

    def inverses_body(where_ref, *refs):
        row_refs, refs = refs[:row_count], refs[row_count:]
        noise_ref, gram_out, outs = refs[0], refs[1], refs[2:]
        for day in range(day_count):
            gather_rows(where_ref, row_refs, lambda offset: day, outs[day])
            outs[day_count + day][...] = dot_parts(
                split(noise_ref[day]), parts(outs[day]), TN
            )
        gram_out[...] = dot_parts(parts(outs[0]), parts(outs[0]), TN)

    gram, *results = call(
        inverses_body,
        [square, *[map_parts] * day_count, *[samples_full] * day_count],
        "inverses",
        (where,),
        [*own_inverse, *shared(got_inverses, where, *packed), noise],
        work=4,
    )
    inverses, local_terms = results[:day_count], results[day_count:]

    def early_body(where_ref, *refs):
        own_refs, refs = refs[:CORES], refs[CORES:]
        count = row_count - CORES
        got_refs, refs = refs[: count * (early + 1)], refs[count * (early + 1) :]
        noise_ref, term_ref, refs = refs[0], refs[1], refs[2:]
        inverse_refs, refs = refs[: early + 1], refs[early + 1 :]
        sum_out, *outs = refs
        link_outs, moved_outs, map_outs = outs[:early], outs[early : 2 * early], outs[2 * early :]
        for day in range(early):
            got = got_refs[count * day : count * (day + 1)]
            if day < early - 1:
                gather_rows(
                    where_ref,
                    (*own_refs, *got),
                    lambda offset: day if offset < CORES else 0,
                    link_outs[day],
                )
            else:
                gather_halves(where_ref, own_refs, day, got, got_refs[count * early :], link_outs[day])
        total = term_ref[...]
        moved = parts(inverse_refs[0])
        for day in range(early):
            link = parts(link_outs[day])
            path = split(-dot_parts(link, moved, NN))
            if day == 0:
                store(map_outs[0], path)
            moved = split(dot_parts(parts(inverse_refs[day + 1]), path, NN))
            store(moved_outs[day], moved)
            total = total + dot_parts(split(noise_ref[day + 1]), moved, TN)
        sum_out[...] = total

    summed, *results = call(
        early_body,
        [samples_full, *[map_parts] * (2 * early + 1)],
        "early_days",
        (where,),
        [
            *own_link,
            *(piece for got in (*got_links[:early], halved_day) for piece in shared(got, gram)),
            noise, local_terms[0], *inverses[: early + 1],
        ],
        work=6,
    )
    links, step_maps = list(results[:early]), list(results[2 * early :])
    moveds = [inverses[0], *results[early : 2 * early]]

    def next_body(day, where_ref, *refs):
        own_refs, got_refs, refs = refs[:CORES], refs[CORES:row_count], refs[row_count:]
        noise_ref, inverse_ref, sum_ref, moved_ref, link_out, moved_out, *sum_outs = refs
        gather_rows(
            where_ref, (*own_refs, *got_refs), lambda offset: day if offset < CORES else 0, link_out
        )
        path = split(-dot_parts(parts(link_out), parts(moved_ref), NN))
        moved = split(dot_parts(parts(inverse_ref), path, NN))
        store(moved_out, moved)
        total = sum_ref[...] + dot_parts(split(noise_ref[day + 1]), moved, TN)
        if len(sum_outs) == 1:
            sum_outs[0][...] = total
        else:
            first = (where_ref[1, 0] & (PAIR - 1)) == 0
            sum_outs[0][...] = jnp.where(first, total[:half], total[half:])
            sum_outs[1][...] = jnp.where(first, total[half:], total[:half])

    for day in range(early, day_count - 1):
        sums = [samples_half] * 2 if day == day_count - 2 else [samples_full]
        link, moved, *sums = call(
            functools.partial(next_body, day),
            [map_parts, map_parts, *sums],
            f"day_{day}",
            (where,),
            [
                *own_link, *shared(got_links[day], summed), noise, inverses[day + 1],
                summed, moveds[day],
            ],
            work=3,
        )
        summed = sums[0]
        moveds.append(moved)
        links.append(link)
    keep, send = sums
    other_sum = to_pair(send)

    def last_link_body(where_ref, *refs):
        own_refs, refs = refs[:CORES], refs[CORES:]
        count = row_count - CORES
        first_refs, rest_refs, refs = refs[:count], refs[count : 2 * count], refs[2 * count :]
        moved_ref, whole_out, half_out, link_out = refs
        rest_refs = [ref.at[pl.ds(0, share - first_rows)] for ref in rest_refs]
        gather_halves(where_ref, own_refs, day_count - 1, first_refs, rest_refs, link_out)
        whole_out[...] = -dot_parts(parts(link_out), parts(moved_ref), NN)
        half_out[...] = whole_out[
            pl.ds(pl.multiple_of((where_ref[0, 0] & (CORES - 1)) * half_nodes, half_nodes), half_nodes), :
        ]

    path, path_half, link = call(
        last_link_body,
        (square, shape(half_nodes, nodes), map_parts),
        "last_link",
        (where,),
        [*own_link, *shared(got_links[-2], send), *shared(got_links[-1], send), moveds[-1]],
        work=1.5,
    )
    links.append(link)
    other_half = to_pair(after(path_half, other_sum))

    def lines_body(source_ref, *refs):
        got_refs, refs = refs[: chips - 1], refs[chips - 1 :]
        flux_out, back_out, current_out = refs[-3:]
        source = source_ref[...]
        for ref in got_refs:
            source = source + ref[share - first_rows : share - first_rows + day_count, :]
        applied = jnp.zeros((LINES, nodes), F32)
        back = applied
        for day in range(day_count):
            inverse_ref, link_ref, moved_ref = refs[3 * day : 3 * day + 3]
            wanted = source[day : day + 1] - applied
            current = dot_parts(split(wanted), parts(inverse_ref), NT)
            current_out[day] = current
            current = split(current)
            applied = dot_parts(current, parts(link_ref), NT)
            back = back + dot_parts(current, parts(moved_ref), NN)
        flux_out[...] = applied
        back_out[...] = back

    flux, back, currents = call(
        lines_body,
        (line, line, shape(day_count, LINES, nodes)),
        "lines",
        (),
        [
            right_side,
            *got_links[-1],
            *(
                ref for day in range(day_count)
                for ref in (inverses[day], links[day], moveds[day])
            ),
        ],
        work=5,
    )
    other_flux = to_pair(flux)

    def grams_body(gram_ref, *refs):
        total = gram_ref[...]
        for ref in refs[:-1]:
            total = total + dot_parts(parts(ref), parts(ref), TN)
        store(refs[-1], split(total))

    gram = call(grams_body, map_parts, "grams", (), [after(gram, flux), *moveds[1:]], work=3)

    def late_maps_body(*refs):
        for index in range(rest):
            store(
                refs[2 * rest + index],
                split(-dot_parts(parts(refs[rest + index]), parts(refs[index]), NN)),
            )

    step_maps += call(
        late_maps_body,
        [map_parts] * rest,
        "late_maps",
        (),
        [after(inverses[1], gram), *inverses[2:], *links[1:]],
        work=rest,
    )

    other_rest = to_row(after(other_half, other_flux, *step_maps), 1)

    def pair_body(
        where_ref, path_ref, half_ref, rest_ref, sum_ref, other_ref, flux_ref, other_flux_ref,
        low_out, high_out, sum_out, high_sum_out, flux_out, low_flux_out,
    ):
        first = (where_ref[1, 0] & (PAIR - 1)) == 0
        lead = (where_ref[0, 0] & (CORES - 1)) == 0
        half_rows, rest_rows = half_ref[...], rest_ref[...]
        for at, rows in (
            (slice(0, half_nodes), jnp.where(lead, half_rows, rest_rows)),
            (slice(half_nodes, nodes), jnp.where(lead, rest_rows, half_rows)),
        ):
            own = path_ref[at, :]
            low_out[0, at, :], low_out[1, at, :] = split(jnp.where(first, own, rows))
            high_out[0, at, :], high_out[1, at, :] = split(jnp.where(first, rows, own))
        low_sum = jnp.where(first, sum_ref[...], other_ref[...])
        high_sum = jnp.where(first, other_ref[...], sum_ref[...])
        low_flux = jnp.where(first, flux_ref[...], other_flux_ref[...])
        high_flux = jnp.where(first, other_flux_ref[...], flux_ref[...])
        flux_out[...] = dot_parts(split(low_flux), parts(high_out), NT) + high_flux
        low_flux_out[...] = low_flux
        sum_out[...] = dot_parts(split(high_sum), parts(low_out), NN) + low_sum
        high_sum_out[...] = high_sum

    low_map, high_map, pair_sum, high_sum, pair_flux, low_flux = call(
        pair_body,
        (map_parts, map_parts, samples_half, samples_half, line, line),
        "pair_maps",
        (where,),
        [path, other_half, other_rest, keep, other_sum, flux, other_flux],
        work=1.5,
    )

    def group_map_body(low_ref, high_ref, out_ref):
        store(out_ref, split(dot_parts(parts(high_ref), parts(low_ref), NN)))

    group_map = call(
        group_map_body, map_parts, "group_map", (), [low_map, after(high_map, pair_sum)]
    )

    def link_body(dims, map_ref, local_ref, *refs):
        got = refs[0][...]
        for ref in refs[1:-1]:
            got = got + ref[...]
        refs[-1][...] = dot_parts(split(got), parts(map_ref), dims) + local_ref[...]

    def linked(dims, value_map, value, got, name):
        return call(
            functools.partial(link_body, dims), shape(*value.shape), name, (),
            [value_map, value, *got], work=0.6,
        )

    def added(refs):
        total = refs[0][...]
        for ref in refs[1:]:
            total = total + ref[...]
        return total

    def turn_body(where_ref, low_ref, flux_ref, gram_ref, back_ref, *refs):
        own_out, back_out, part_out = refs[-3:]
        given = added(refs[:-3])
        behind = dot_parts(split(given), parts(low_ref), NT) + flux_ref[...]
        first = (where_ref[1, 0] & (PAIR - 1)) == 0
        given = jnp.where(first, given, behind)
        own_out[...] = given
        own_back = back_ref[...] - dot_parts(split(given), parts(gram_ref), NN)
        back_out[...] = own_back
        part_out[...] = jnp.where(first, own_back, dot_parts(split(own_back), parts(low_ref), NN))

    def first_back_body(where_ref, map_ref, own_ref, other_ref, part_ref, mate_ref, *refs):
        value_out, pair_out, high_out = refs[-3:]
        first = (where_ref[1, 0] & (PAIR - 1)) == 0
        pair_back = part_ref[...] + mate_ref[...]
        pair_out[...] = pair_back
        high_out[...] = jnp.where(first, other_ref[...], own_ref[...])
        value_out[...] = dot_parts(split(added(refs[:-3])), parts(map_ref), NN) + pair_back

    mean = {}
    noise_step = []

    def mean_hops():
        value, got = pair_flux, []
        yield value
        for group in range(groups - 1):
            got.append(to_group(value, group, group + 1))
            if group < groups - 2:
                value = linked(NT, group_map, pair_flux, got, "forward_link")
                yield value
        mean["entering"], own_back, part = call(
            turn_body, (line, line, line), "mean_turn", (where,),
            [low_map, low_flux, gram, back, after(got[0], *noise_step), *got[1:]],
        )
        yield part
        last = PAIR * (groups - 1)
        got = [
            lax.ppermute(part, "tm", [(last + i, last - PAIR + (i ^ cross)) for i in range(PAIR)])
            for cross in range(PAIR)
        ]
        both = to_pair(jnp.concatenate([own_back, part], axis=0))
        value, pair_back, mean["high_back"] = call(
            first_back_body, (line, line, line), "first_back", (where,),
            [
                group_map, after(own_back, *noise_step), both[:LINES], part, both[LINES:], *got,
            ],
            work=0.6,
        )
        mean["leaving"] = got
        for group in range(groups - 2, 0, -1):
            yield value
            got.append(to_group(value, group, group - 1))
            if group > 1:
                gated = [after(got[0], *noise_step), *got[1:]]
                value = linked(NN, group_map, pair_back, gated, "backward_link")
        yield value

    hops = mean_hops()
    ahead = next(hops)

    leaving = []
    value = pair_sum
    for group in range(groups - 1, 0, -1):
        got = to_group(after(value, ahead), group, group - 1)
        if group > 1:
            ahead = next(hops)
        if group == groups - 1:
            ahead = next(hops, ahead)
        leaving.append(after(got, ahead))
        if group > 1:
            value = linked(NN, group_map, pair_sum, leaving, "noise_link")
            noise_step[:] = [value]
            if group < groups - 1:
                ahead = next(hops, ahead)
    def divide_body(where_ref, map_ref, sum_ref, *refs):
        keep_out, send_out = refs[-2:]
        given = refs[0][...]
        for ref in refs[1:-2]:
            given = given + ref[...]
        between = dot_parts(split(given), parts(map_ref), NN) + sum_ref[...]
        first = (where_ref[1, 0] & (PAIR - 1)) == 0
        keep_out[...] = jnp.where(first, between, given)
        send_out[...] = jnp.where(first, given, between)

    kept_half, sent_half = call(
        divide_body, (samples_half, samples_half), "divide", (where,),
        [high_map, high_sum, *leaving],
    )
    got_half = to_pair(sent_half)
    noise_step[:] = [sent_half]
    for _ in hops:
        pass

    def terms_body(entering_ref, current_ref, *refs):
        outs = refs[-day_count:]
        given = split(entering_ref[...])
        for day in range(day_count):
            local_ref, inverse_ref, moved_ref = refs[3 * day : 3 * day + 3]
            current = current_ref[day] - dot_parts(given, parts(moved_ref), NT)
            term = dot_parts(split(current), parts(inverse_ref), NN)
            outs[day][...] = local_ref[...] + term[:1]

    terms = call(
        terms_body, [samples_full] * day_count, "mean_terms", (),
        [
            after(mean["entering"], sent_half), currents,
            *(
                value for day in range(day_count)
                for value in (local_terms[day], inverses[day], moveds[day])
            ),
        ],
        work=4,
    )

    def last_body(where_ref, keep_ref, got_ref, back_ref, high_ref, *refs):
        count = len(mean["leaving"])
        got_means, refs = refs[:count], refs[count:]
        map_refs, term_refs = refs[:day_count], refs[day_count : 2 * day_count]
        out_ref, held, sems = refs[2 * day_count :]
        first = (where_ref[1, 0] & (PAIR - 1)) == 0
        given = got_means[0][...]
        for ref in got_means[1:]:
            given = given + ref[...]
        between = dot_parts(split(given), parts(high_ref), NN) + back_ref[...]
        given = jnp.where(first, between, given)
        low = jnp.where(first, keep_ref[...], got_ref[...])
        high = jnp.where(first, got_ref[...], keep_ref[...])
        following = jnp.concatenate([low, high], axis=0) + given[:1]
        copies = []
        for day in reversed(range(day_count)):
            following = dot_parts(split(following), parts(map_refs[day]), NN) + term_refs[day][...]
            held[day] = following.T
            copies.append(pltpu.make_async_copy(held.at[day], out_ref.at[day], sems.at[day]))
            copies[-1].start()
        for copy in copies:
            copy.wait()

    return call(
        last_body, shape(day_count, nodes, columns), "last_days", (where,),
        [
            kept_half, got_half, mean["high_back"], high_map, *mean["leaving"], *step_maps,
            *terms,
        ],
        work=4,
        scratch=[
            pltpu.VMEM((day_count, nodes, columns), F32), pltpu.SemaphoreType.DMA((day_count,)),
        ],
        out_specs=pl.BlockSpec(memory_space=pl.ANY),
    )


def solution(mesh):
    return jax.shard_map(
        local,
        mesh=mesh,
        in_specs=(
            P("tm", "row", None),
            P("tm", "row", None),
            P("tm", None, "row"),
            P(("tm", "row")),
            P(("tm", "row")),
            P(("tm", "row")),
        ),
        out_specs=P("tm", None, "row"),
        check_vma=False,
    )
```
